128 devices in a mesh: rad: 4 (over y), lon: 32 (over x, z, core).
Axes of the slice: x: 4, y: 4, z: 4, core: 2. Of those that a mesh axis runs over, the one named last changes fastest.
Arguments:
- state: float32 [8, 256, 512, 256], P(None, 'rad', 'lon'), may hold values from -6 to 6
- flux_matrices: float32 [2, 8, 8], replicated, may hold values from -2 to 2
- wave_speed: float32 [2], replicated, may hold values from 0.5 to 2
- flux_volume: float32 [256, 512, 256], P('rad', 'lon'), may hold values from 0.02 to 0.2
- block_tile: int32 [32, 256, 1], P('lon', 'rad'), may hold values from 0 to 127; in each aligned block of 64 rows (0 to 63, 64 to 127, ..., all dimensions but the last counted through in order) at most 2 rows name the same one
- tile_of_device: int32 [128], replicated, may hold values from 0 to 127, each once
- phase_density: float32 [128, 200, 128], P(('rad', 'lon')), may hold values from -6 to 6
- injection: float32 [2, 200], replicated, may hold values from -3 to 3
- drift_courant: float32 [200], replicated, may hold values from 0.05 to 0.9
- energy_weight: float32 [200], replicated, may hold values from 0.01 to 0.1
Outputs:
- coupled_state: float32 [8, 256, 512, 256], P(None, 'rad', 'lon')
- drifted_density: float32 [128, 200, 128], P(('rad', 'lon'))
The draws below stay inside these ranges and needn't reach their ends.
Inputs may be any that keep to these rules, and one draw needn't show every extreme that they name: `block_tile`: in each longitude sector and each aligned run of 64 radial rows, no tile is reached by more than 2 blocks. `tile_of_device`: every tile has exactly one owner.
All inputs are finite; a program needn't handle non-finite values.
Results may differ from the reference program's by a relative error of at most 0.000067.
Values sent between devices are 32-bit elements; how exact they have to be, the bound alone decides.
A program may use at most 192 MiB of HBM per device.

```python
import math
import jax
import jax.numpy as jnp
import numpy as np
from jax import lax

NF = 8
CR = 64
CL = 16
CZ = 256
ZSEG = 8
CH = 200
MOST = 2
DRIFT = 3
TP = 128
NR = 256
NL = 512
N_LON = 32
DEVICES = 128


def block_levels(key, shape, shards, smallest, high):
    loudness, own = 1.0, jax.random.fold_in(key, 6)
    for axis_at, shards_of in shards:
        steps = jnp.exp(jax.random.uniform(jax.random.fold_in(own, axis_at), (shards_of,), jnp.float32, smallest / len(shards), high / len(shards)))
        loudness = loudness * jnp.repeat(steps, shape[axis_at] // shards_of).reshape([-1 if axis == axis_at else 1 for axis in range(len(shape))])
    return loudness


def assign_block(stream_key, own, number, rows, number_of, top, limit, slope):
    order = jax.random.permutation(stream_key, number_of)
    packed, common = shares(number_of, rows * top, limit, slope, True), shares(number_of, rows * top, limit, slope, False)
    places = jnp.arange(number_of)

    def named(sizes, rotation):
        used = int((sizes > 0).sum())
        fixed = max(1, used // 4)
        moved = fixed + (places - fixed + rotation * (used - fixed)) % max(1, number_of - fixed)
        return jnp.zeros((number_of,), jnp.int32).at[order[jnp.where(places < fixed, places, moved)]].set(jnp.asarray(sizes, jnp.int32))

    sizes = jnp.where(number % 4 == 0, named(packed, number // 4), named(common, number - number // 4 - 1))
    mixed = jax.random.permutation(jax.random.fold_in(own, 3), number_of)
    donor, sink = mixed[0:number_of // 2 * 2:2], mixed[1:number_of // 2 * 2:2]
    slack = jnp.minimum(sizes[donor] - 1, limit - sizes[sink]) // 2
    slack = jnp.where((donor == order[0]) | (sink == order[0]) | (sizes[sink] == 0), 0, jnp.maximum(slack, 0))
    moved = jax.random.randint(jax.random.fold_in(own, 4), (number_of // 2,), 0, 1 << 20) % (slack + 1)
    sizes = sizes.at[donor].add(-moved).at[sink].add(moved)
    members = jnp.searchsorted(jnp.cumsum(sizes), jnp.arange(rows * top), side="right").astype(jnp.int32)
    grid = members.reshape(top, rows).T
    grid = grid[jax.random.permutation(jax.random.fold_in(own, 1), rows)]
    rotation = jax.random.randint(jax.random.fold_in(own, 2), (rows, 1), 0, top)
    return jnp.take_along_axis(grid, (jnp.arange(top)[None, :] + rotation) % top, axis=1)


def shares(number_of, total, reach, slope, full):
    weights = [(1 << 20) // math.isqrt(grade ** slope) + 1 for grade in range(1, number_of + 1)]
    largest = reach if full else min(reach, max(-(-total // number_of), total * weights[0] // sum(weights)))
    least = 1 if total - largest >= number_of - 1 else 0
    holding, surplus = [largest] + [least] * (number_of - 1), total - largest - least * (number_of - 1)
    while surplus > 0:
        free = [i for i in range(1, number_of) if holding[i] < largest] or [i for i in range(1, number_of) if holding[i] < reach]
        whole, budget = sum([weights[i] for i in free]), surplus
        for i in free:
            addition = min(reach - holding[i], max(1, budget * weights[i] // whole), surplus)
            holding[i] = holding[i] + addition
            surplus = surplus - addition
    return np.array(holding)


def gaussian(key, shape, scale, reach, shards=(), held_as=jnp.bfloat16):
    level = block_levels(key, shape, shards, -0.22, 0.18) if shards else 1.0
    values = jax.random.normal(key, shape, jnp.float32) * scale * level
    return jnp.minimum(jnp.maximum(values, -reach), reach).astype(held_as)


def setup_inputs(seed: int = 0) -> dict:
    keys = jax.random.split(jax.random.key(seed), 11)
    state = gaussian(keys[0], (NF, NR, NL, CZ), 1.0, 6.0, ((1, 4), (2, 32)), jnp.float32)
    flux_matrices = gaussian(keys[1], (2, NF, NF), NF ** -0.5, 2.0, (), jnp.float32)
    wave_speed = jnp.clip(jnp.exp(jax.random.uniform(keys[2], (2,), jnp.float32, math.log(0.5), math.log(2.0))), 0.5, 2.0)
    flux_volume = jnp.clip(jnp.exp(math.log(0.2) - 2.3025851 * jax.random.uniform(keys[3], (NR, NL, CZ), jnp.float32) ** block_levels(keys[3], (NR, NL, CZ), ((0, 4), (1, 32)), -0.2, 0.2)), 0.02, 0.2)
    block_tile_keys = jax.random.split(jax.random.fold_in(keys[4], 1), N_LON * NR // CR)
    block_tile_turns = jax.random.permutation(jax.random.fold_in(keys[4], 3), N_LON * NR // CR)
    block_tile = jax.vmap(lambda own, number: assign_block(jax.random.fold_in(keys[4], 2), own, number, CR, DEVICES, 1, MOST, 2))(block_tile_keys, block_tile_turns).reshape((N_LON, NR, 1))
    tile_of_device = jax.random.permutation(keys[5], DEVICES).astype(jnp.int32)
    phase_density = gaussian(keys[6], (DEVICES, CH, TP), 1.0, 6.0, ((0, 128),), jnp.float32)
    injection = gaussian(keys[7], (2, CH), 0.5, 3.0, (), jnp.float32)
    drift_courant = jnp.clip(jnp.exp(jax.random.uniform(keys[8], (CH,), jnp.float32, math.log(0.05), math.log(0.9))), 0.05, 0.9)
    energy_weight = jnp.clip(jnp.exp(jax.random.uniform(keys[9], (CH,), jnp.float32, math.log(0.01), math.log(0.1))), 0.01, 0.1)
    return {"state": state, "flux_matrices": flux_matrices, "wave_speed": wave_speed, "flux_volume": flux_volume, "block_tile": block_tile, "tile_of_device": tile_of_device, "phase_density": phase_density, "injection": injection, "drift_courant": drift_courant, "energy_weight": energy_weight}


courant_step = 0.4
nudge_rate = 0.5
inner_step = 0.5


def divergence(padded, along_axis, extent, matrix, wave_rate):
    shifted = [lax.slice_in_dim(padded, offset, offset + extent + 1, axis=along_axis) for offset in range(6)]
    left_state = (2.0 * shifted[0] - 13.0 * shifted[1] + 47.0 * shifted[2] + 27.0 * shifted[3] - 3.0 * shifted[4]) / 60.0
    right_state = (-3.0 * shifted[1] + 27.0 * shifted[2] + 47.0 * shifted[3] - 13.0 * shifted[4] + 2.0 * shifted[5]) / 60.0
    face_flux = 0.5 * jnp.einsum("ab,bxyz->axyz", matrix, left_state + right_state, precision=lax.Precision.HIGHEST) - 0.5 * wave_rate * (right_state - left_state)
    return lax.slice_in_dim(face_flux, 1, extent + 1, axis=along_axis) - lax.slice_in_dim(face_flux, 0, extent, axis=along_axis)


def reference(state, flux_matrices, wave_speed, flux_volume, block_tile, tile_of_device, phase_density, injection, drift_courant, energy_weight):
    seg_cells = CZ // ZSEG
    state_parts = jnp.moveaxis(state.reshape(NF, NR, NL, ZSEG, seg_cells), 3, 0)
    volume_parts = jnp.moveaxis(flux_volume.reshape(NR, NL, ZSEG, seg_cells), 2, 0)

    def advance(pair):
        segment, volume = pair
        radial = jnp.pad(segment, ((0, 0), (3, 3), (0, 0), (0, 0)))
        beside_all = jnp.pad(segment, ((0, 0), (0, 0), (3, 3), (0, 0)), mode="wrap")
        change = divergence(radial, 1, NR, flux_matrices[0], wave_speed[0]) + divergence(beside_all, 2, NL, flux_matrices[1], wave_speed[1])
        updated = segment - courant_step * change
        picked = jnp.stack([updated[0], updated[7]])
        return updated, jnp.sum(picked * volume[None], axis=-1)

    updated_parts, line_parts = lax.map(advance, (state_parts, volume_parts))
    line_sums = jnp.moveaxis(line_parts, 0, -1)
    payload = line_sums.reshape(2, NR, N_LON, CL, ZSEG).transpose(2, 1, 0, 3, 4).reshape(N_LON, NR, 2, TP)
    targets = block_tile[..., 0]
    one_hot = (targets[..., None] == jnp.arange(DEVICES, dtype=jnp.int32)).astype(jnp.float32)
    tile_source = jnp.einsum("jrt,jrcp->tcp", one_hot, payload, precision=lax.Precision.HIGHEST)
    owned_source = tile_source[tile_of_device]

    def inner(density_tile, source_tile):
        density = density_tile + inner_step * (injection[0][:, None] * source_tile[0][None, :] + injection[1][:, None] * source_tile[1][None, :])
        for substep in range(DRIFT):
            density = density - drift_courant[:, None] * (density - jnp.roll(density, 1, axis=1))
        return density, jnp.dot(energy_weight, density, precision=lax.Precision.HIGHEST)

    drifted_density, owner_pressure = jax.vmap(inner)(phase_density, owned_source)
    tile_pressure = jnp.zeros((DEVICES, TP), jnp.float32).at[tile_of_device].set(owner_pressure)
    returned = tile_pressure[targets]
    returned = returned.reshape(N_LON, NR, CL, ZSEG).transpose(1, 0, 2, 3).reshape(NR, NL, ZSEG)
    returned = jnp.moveaxis(returned, 2, 0)[..., None]
    pressure_old = updated_parts[:, 7]
    pressure_new = pressure_old + nudge_rate * (returned - pressure_old)
    coupled_parts = updated_parts.at[:, 7].set(pressure_new)
    coupled_state = jnp.moveaxis(coupled_parts, 0, 3).reshape(NF, NR, NL, CZ)
    return coupled_state, drifted_density
```

```python
import numpy as np

import jax
import jax.numpy as jnp
import ml_dtypes
from jax import lax
from jax.experimental import pallas as pl
from jax.experimental.pallas import tpu as pltpu
from jax.sharding import PartitionSpec as P

F32 = jnp.float32
BF16 = jnp.bfloat16
HIGHEST = lax.Precision.HIGHEST
MESH = pl.DeviceIdType.MESH

NF, CR, CL, CZ = 8, 64, 16, 256
ZSEG = 8
DRIFT = 3
CH, TP = 200, 128
NRAD, NLON = 4, 32
NYX, NZC = 16, 8
DEVICES = NRAD * NLON

SCALE = 0.4 * 0.5 / 30.0
ORDER = (0, 7, 1, 2, 3, 4, 5, 6)
ODD = {-3: -1.0, -2: 9.0, -1: -45.0, 1: 45.0, 2: -9.0, 3: 1.0}
EVEN = {-3: 1.0, -2: -6.0, -1: 15.0, 0: -20.0, 1: 15.0, 2: -6.0, 3: 1.0}

RB = 8
NB = CR // RB

C_FIX07, C_FIX, C_SEG, C_MASK, C_ODD, C_EVEN, C_EODD, C_EEVEN, C_END = (
    0, 128, 224, 480, 496, 512, 528, 576, 624
)


def constants():
    t = np.zeros((C_END, 128), np.float32)
    half = 64
    for c in range(2):
        for r in range(4):
            for l in range(CL):
                row = C_FIX07 + (c * 4 + r) * CL + l
                for h in range(2):
                    if l < 3:
                        t[row, h * half + r * 8 + 3 * c + l] = 1
                    if l >= CL - 3:
                        t[row, h * half + 32 + r * 8 + 3 * c + l - (CL - 3)] = 1
    for pos in range(2, NF):
        for l in range(CL):
            row = C_FIX + (pos - 2) * CL + l
            for h in range(2):
                if l < 3:
                    t[row, h * half + 3 * pos + l] = 1
                if l >= CL - 3:
                    t[row, h * half + 24 + 3 * pos + l - (CL - 3)] = 1
    for z in range(CZ):
        for p in range(TP):
            t[C_SEG + z, p] = z // (CZ // ZSEG) == p % ZSEG
    for l in range(CL):
        for p in range(TP):
            t[C_MASK + l, p] = p // ZSEG == l
    for l in range(CL):
        for f in range(NF):
            for j in range(CL):
                t[C_ODD + l, f * CL + j] = ODD.get(j - l, 0.0)
                t[C_EVEN + l, f * CL + j] = EVEN.get(j - l, 0.0)
    for side in range(2):
        for pos in range(NF):
            for k in range(3):
                row = side * 24 + 3 * pos + k
                for f in range(NF):
                    for j in range(CL):
                        off = j - CL - k if side == 0 else 3 + j - k
                        t[C_EODD + row, f * CL + j] = ODD.get(off, 0.0)
                        if f == ORDER[pos]:
                            t[C_EEVEN + row, f * CL + j] = EVEN.get(off, 0.0)
    return t.astype(ml_dtypes.bfloat16)


def split(x):
    hi = x.astype(BF16)
    return hi, (x - hi.astype(F32)).astype(BF16)


def kernel(
    state, volume, phase, matrices, speeds, targets, tiles, injection, courant, weight, table,
    out, drifted,
    cells, vol, dens, lhs, edge_lhs, send0, send1, recv0, recv1, rad_send, rad_recv,
    cols, pay, buf, ra, rb, rbs, g0, g1, g2,
    load_sem, vol_sem, dens_sem, lon_s0, lon_r0, lon_s1, lon_r1, rad_s, rad_r,
    ra_s, ra_r, rb_s, rb_r, g1_s, g1_r, g2_s, g2_r,
):
    rad, lon = lax.axis_index("rad"), lax.axis_index("lon")
    right, left = lax.rem(lon + 1, NLON), lax.rem(lon + NLON - 1, NLON)
    me_yx = rad * (NYX // NRAD) + lax.div(lon, NZC)
    me_zc = lax.rem(lon, NZC)

    def yx_peer(k):
        a = lax.rem(me_yx + k, NYX)
        return a, (lax.div(a, NYX // NRAD), lax.rem(a, NYX // NRAD) * NZC + me_zc)

    def zc_peer(k):
        i = lax.rem(me_zc + k, NZC)
        return i, (rad, lon - me_zc + i)

    def load(b):
        return pltpu.make_async_copy(
            state.at[:, pl.ds(b * RB, RB)], cells.at[:, pl.ds(3 + b * RB, RB)], load_sem.at[b]
        )

    for b in [0, NB - 1] + list(range(1, NB - 1)):
        load(b).start()
    vol_copy = pltpu.make_async_copy(volume, vol, vol_sem)
    vol_copy.start()
    dens_copy = pltpu.make_async_copy(phase, dens, dens_sem)
    dens_copy.start()

    barrier = pltpu.get_barrier_semaphore()

    def greet(device):
        pl.semaphore_signal(barrier, inc=1, device_id=device, device_id_type=MESH)

    greet((rad, right))
    greet((rad, left))
    for k in range(1, NYX):
        greet(yx_peer(k)[1])
    for k in range(1, NZC):
        greet(zc_peer(k)[1])

    cells[:, 0:3] = jnp.zeros((NF, 3, CL, CZ), F32)
    cells[:, 3 + CR :] = jnp.zeros((NF, 3, CL, CZ), F32)

    lane = lax.broadcasted_iota(jnp.int32, (CL, 128), 1)
    sub = lax.broadcasted_iota(jnp.int32, (CL, 128), 0)
    block = lax.shift_right_logical(lane, 4)
    same_l = jnp.bitwise_and(lane, CL - 1) == sub
    odd, even = table[C_ODD : C_ODD + CL].astype(F32), table[C_EVEN : C_EVEN + CL].astype(F32)
    rows_l = []
    for f in range(NF):
        row_r = jnp.zeros((CL, 128), F32)
        row_l = jnp.zeros((CL, 128), F32)
        for g in range(NF):
            row_r = jnp.where(block == g, matrices[0, f, g], row_r)
            row_l = jnp.where(block == g, matrices[1, f, g], row_l)
        rows_l.append(row_l)
        w = (SCALE * speeds[1]) * jnp.where(block == f, even, 0.0) - SCALE * row_l * odd
        whi, wlo = split(w)
        rhi, rlo = split(jnp.where(same_l, -SCALE * row_r, 0.0))
        at = f * CL
        lhs[at : at + CL, 0:128] = whi
        lhs[at : at + CL, 128:256] = rhi
        lhs[128 + at : 128 + at + CL, 0:128] = wlo
        lhs[128 + at : 128 + at + CL, 128:256] = rlo
    q = lax.broadcasted_iota(jnp.int32, (24, 128), 0)
    row_e = jnp.zeros((24, 128), F32)
    for pos, f in enumerate(ORDER):
        wide = jnp.concatenate([rows_l[f][0:8]] * 3, axis=0)
        row_e = jnp.where((q >= 3 * pos) & (q < 3 * pos + 3), wide, row_e)
    row_e = jnp.concatenate([row_e, row_e], axis=0)
    we = (SCALE * speeds[1]) * table[C_EEVEN : C_EEVEN + 48].astype(F32) - (
        SCALE * row_e * table[C_EODD : C_EODD + 48].astype(F32)
    )
    ehi, elo = split(we)
    edge_lhs[0:48, 0:128] = ehi
    edge_lhs[0:48, 128:256] = ehi
    edge_lhs[48:96, 0:128] = elo
    edge_lhs[48:96, 128:256] = jnp.zeros((48, 128), BF16)

    def row(i):
        return cells[:, i].reshape(NF * CL, CZ)

    load(0).wait()
    load(NB - 1).wait()

    def rad_edge(side):
        for k in range(3):
            d = jnp.zeros((128, CZ), F32)
            e = jnp.zeros((128, CZ), F32)
            for j in range(3):
                off = j - k - 3 if side == 0 else 3 + j - k
                if off in ODD:
                    u = row(CR + j if side == 0 else 3 + j)
                    d = d + ODD[off] * u
                    e = e + EVEN[off] * u
            dh, dl = split(d)
            y = (
                jnp.dot(lhs[0:128, 128:256], dh, preferred_element_type=F32)
                + jnp.dot(lhs[128:256, 128:256], dh, preferred_element_type=F32)
                + jnp.dot(lhs[0:128, 128:256], dl, preferred_element_type=F32)
                + (SCALE * speeds[0]) * e
            )
            for pos, f in enumerate(ORDER):
                rad_send[side, pos, k] = y[f * CL : (f + 1) * CL]

    def rad_copy(side, part):
        fields = pl.ds(0, 2) if part == 0 else pl.ds(2, NF - 2)
        return pltpu.make_async_remote_copy(
            src_ref=rad_send.at[side, fields],
            dst_ref=rad_recv.at[side, fields],
            send_sem=rad_s.at[side, part],
            recv_sem=rad_r.at[side, part],
            device_id=(rad + 1 if side == 0 else rad - 1, lon),
            device_id_type=MESH,
        )

    has = (rad < NRAD - 1, rad > 0)
    rad_edge(0)
    rad_edge(1)

    pl.semaphore_wait(barrier, 2 + NYX - 1 + NZC - 1)
    for side in range(2):
        @pl.when(has[side])
        def _():
            rad_copy(side, 0).start()

    def lon_copy(side, part, b):
        src, dst = (send0, recv0) if part == 0 else (send1, recv1)
        ss, rs = (lon_s0, lon_r0) if part == 0 else (lon_s1, lon_r1)
        rows = pl.ds(b * RB, RB)
        return pltpu.make_async_remote_copy(
            src_ref=src.at[side, rows],
            dst_ref=dst.at[side, rows],
            send_sem=ss.at[side, b],
            recv_sem=rs.at[side, b],
            device_id=(rad, right if side == 0 else left),
            device_id_type=MESH,
        )

    def edge_chunk(b, _):
        @pl.when((b > 0) & (b < NB - 1))
        def _():
            load(b).wait()

        def edge_row(i, _):
            r = b * RB + i
            hi, lo = split(row(3 + r))
            y = jnp.dot(
                edge_lhs[...], jnp.concatenate([hi, lo], axis=0), preferred_element_type=F32
            )
            y = y[0:48] + y[48:96]
            for side in range(2):
                send0[side, r] = y[side * 24 : side * 24 + 8]
                send1[side, r] = y[side * 24 + 8 : side * 24 + 24]
            return 0

        lax.fori_loop(0, RB, edge_row, 0, unroll=4)
        lon_copy(0, 0, b).start()
        lon_copy(1, 0, b).start()
        return 0

    lax.fori_loop(0, NB, edge_chunk, 0)

    def send_rest(b, _):
        lon_copy(0, 1, b).start()
        lon_copy(1, 1, b).start()
        return 0

    lax.fori_loop(0, NB, send_rest, 0)
    for side in range(2):
        @pl.when(has[side])
        def _():
            rad_copy(side, 1).start()

    def bulk(r, _):
        m3, m2, m1, u, p1, p2, p3 = (row(r + i) for i in range(7))
        d = 45.0 * (p1 - m1) - 9.0 * (p2 - m2) + (p3 - m3)
        e = 15.0 * (p1 + m1) - 6.0 * (p2 + m2) + (p3 + m3) - 20.0 * u
        xh, xl = split(u)
        dh, dl = split(d)
        t1 = jnp.concatenate([xh, dh], axis=0)
        t2 = jnp.concatenate([xl, dl], axis=0)
        y1 = jnp.dot(lhs[...], t1, preferred_element_type=F32)
        y2 = jnp.dot(lhs[0:128], t2, preferred_element_type=F32)
        new = u + (SCALE * speeds[0]) * e + (y1[0:128] + y1[128:256] + y2)
        out[:, r] = new.reshape(NF, CL, CZ)
        return 0

    lax.fori_loop(0, CR, bulk, 0, unroll=2)

    def add_rad(part):
        for side in range(2):
            @pl.when(has[1 - side])
            def _():
                rad_copy(side, part).wait_recv()
                for pos in range(2) if part == 0 else range(2, NF):
                    for k in range(3):
                        r = k if side == 0 else CR - 3 + k
                        out[ORDER[pos], r] = out[ORDER[pos], r] + rad_recv[side, pos, k]

    add_rad(0)
    vol_copy.wait()
    seg = table[C_SEG : C_SEG + CZ]
    mask = table[C_MASK : C_MASK + CL].astype(F32)

    def early(b, _):
        lon_copy(0, 0, b).wait_recv()
        lon_copy(1, 0, b).wait_recv()
        for h in range(RB // 4):
            r = b * RB + h * 4
            got = jnp.concatenate(
                [recv0[0, pl.ds(r, 4)].reshape(32, CZ), recv0[1, pl.ds(r, 4)].reshape(32, CZ)],
                axis=0,
            )
            hi, lo = split(got)
            add = jnp.dot(
                table[C_FIX07 : C_FIX07 + 128],
                jnp.concatenate([hi, lo], axis=0),
                preferred_element_type=F32,
            )
            v = vol[pl.ds(r, 4)].reshape(64, CZ)
            for c, f in enumerate((0, 7)):
                new = out[f, pl.ds(r, 4)].reshape(64, CZ) + add[c * 64 : (c + 1) * 64]
                out[f, pl.ds(r, 4)] = new.reshape(4, CL, CZ)
                yh, yl = split(v * new)
                t = jnp.dot(yh, seg, preferred_element_type=F32) + jnp.dot(
                    yl, seg, preferred_element_type=F32
                )
                t = t.reshape(4, CL, TP) * mask[None]
                pay[pl.ds(r * 8, 32), c * TP : (c + 1) * TP] = (t[:, 0:8] + t[:, 8:16]).reshape(
                    32, TP
                )
        return 0

    lax.fori_loop(0, NB, early, 0)

    hit = (targets[...] == tiles[...]).astype(F32)
    hit8 = jnp.broadcast_to(hit[:, None, :], (CR, 8, DEVICES)).reshape(CR * 8, DEVICES)
    buf[...] = lax.dot_general(
        hit8, pay[...], (((0,), (0,)), ((), ())), precision=HIGHEST, preferred_element_type=F32
    ).reshape(NYX, NZC, 2 * TP)

    def ra_copy(k):
        a, device = yx_peer(k)
        return pltpu.make_async_remote_copy(
            src_ref=buf.at[a], dst_ref=ra.at[k], send_sem=ra_s.at[k], recv_sem=ra_r.at[k],
            device_id=device, device_id_type=MESH,
        )

    def rb_copy(k):
        i, device = zc_peer(k)
        return pltpu.make_async_remote_copy(
            src_ref=rbs.at[i], dst_ref=rb.at[k], send_sem=rb_s.at[k], recv_sem=rb_r.at[k],
            device_id=device, device_id_type=MESH,
        )

    def g1_copy(k):
        i, device = zc_peer(k)
        return pltpu.make_async_remote_copy(
            src_ref=g0, dst_ref=g1.at[me_zc], send_sem=g1_s.at[k], recv_sem=g1_r.at[k],
            device_id=device, device_id_type=MESH,
        )

    def g2_copy(k):
        a, device = yx_peer(k)
        return pltpu.make_async_remote_copy(
            src_ref=g1, dst_ref=g2.at[me_yx], send_sem=g2_s.at[k], recv_sem=g2_r.at[k],
            device_id=device, device_id_type=MESH,
        )

    for k in range(1, NYX):
        ra_copy(k).start()
    total = buf[me_yx]
    cols[...] = jnp.zeros((8, 256), F32)
    cols[0:2, 0:CH] = injection[...]
    cols[2:3, 0:CH] = courant[...]
    cols[3:4, 0:CH] = weight[...]
    columns = cols[...].T
    dens_copy.wait()
    for k in range(1, NYX):
        ra_copy(k).wait_recv()
        total = total + ra[k]
    for i in range(NZC):
        rbs[i] = total[i : i + 1]
    for k in range(1, NZC):
        rb_copy(k).start()
    source = rbs[me_zc]
    for k in range(1, NZC):
        rb_copy(k).wait_recv()
        source = source + rb[k]

    density = dens[...] + 0.5 * (
        columns[0:CH, 0:1] * source[:, 0:TP] + columns[0:CH, 1:2] * source[:, TP:]
    )
    rate = jnp.broadcast_to(columns[0:CH, 2:3], (CH, TP))
    for _ in range(DRIFT):
        density = density - rate * (density - pltpu.roll(density, 1, axis=1))
    drifted[...] = density
    pressure = jnp.sum(columns[0:CH, 3:4] * density, axis=0, keepdims=True)
    g0[...] = pressure
    for k in range(1, NZC):
        g1_copy(k).start()
    g1[me_zc] = pressure
    for k in range(1, NZC):
        g1_copy(k).wait_recv()
    for k in range(1, NYX):
        g2_copy(k).start()
    g2[me_yx] = g1[...]

    add_rad(1)

    def late(b, _):
        lon_copy(0, 1, b).wait_recv()
        lon_copy(1, 1, b).wait_recv()

        def late_row(i, _):
            r = b * RB + i
            got = jnp.concatenate(
                [recv0[0, r], recv1[0, r], recv0[1, r], recv1[1, r], jnp.zeros((16, CZ), F32)],
                axis=0,
            )
            hi, lo = split(got)
            add = jnp.dot(
                table[C_FIX : C_FIX + 96],
                jnp.concatenate([hi, lo], axis=0),
                preferred_element_type=F32,
            )
            out[1:7, r] = out[1:7, r] + add.reshape(6, CL, CZ)
            return 0

        lax.fori_loop(0, RB, late_row, 0, unroll=4)
        return 0

    lax.fori_loop(0, NB, late, 0)

    for k in range(1, NYX):
        g2_copy(k).wait_recv()
    returned = jnp.dot(
        hit, g2[...].reshape(DEVICES, TP), precision=HIGHEST, preferred_element_type=F32
    )
    pay[0:CR, 0:TP] = returned

    def nudge(b, _):
        got = pay[pl.ds(b * RB, RB), 0:TP]
        wide = jnp.broadcast_to(got[:, None, :], (RB, CL, TP)) * mask[None]
        hi, lo = split(wide.reshape(RB * CL, TP))
        dims = (((1,), (1,)), ((), ()))
        back = lax.dot_general(hi, seg, dims, preferred_element_type=F32) + lax.dot_general(
            lo, seg, dims, preferred_element_type=F32
        )
        old = out[7, pl.ds(b * RB, RB)].reshape(RB * CL, CZ)
        out[7, pl.ds(b * RB, RB)] = (old + 0.5 * (back - old)).reshape(RB, CL, CZ)
        return 0

    lax.fori_loop(0, NB, nudge, 0)

    def sent(b, _):
        for side in range(2):
            for part in range(2):
                lon_copy(side, part, b).wait_send()
        return 0

    lax.fori_loop(0, NB, sent, 0)
    for side in range(2):
        @pl.when(has[side])
        def _():
            rad_copy(side, 0).wait_send()
            rad_copy(side, 1).wait_send()
    for k in range(1, NYX):
        ra_copy(k).wait_send()
        g2_copy(k).wait_send()
    for k in range(1, NZC):
        rb_copy(k).wait_send()
        g1_copy(k).wait_send()


def per_device(
    state, flux_matrices, wave_speed, flux_volume, block_tile, tile_of_device,
    phase_density, injection, drift_courant, energy_weight,
):
    any_spec = pl.BlockSpec(memory_space=pl.ANY)
    smem = pl.BlockSpec(memory_space=pltpu.SMEM)
    vmem = pl.BlockSpec(memory_space=pltpu.VMEM)
    dma = pltpu.SemaphoreType.DMA
    coupled, drifted = pl.pallas_call(
        kernel,
        out_shape=(
            pltpu.VMEM((NF, CR, CL, CZ), F32),
            jax.ShapeDtypeStruct((CH, TP), F32),
        ),
        in_specs=[any_spec] * 3 + [smem] * 2 + [vmem] * 6,
        out_specs=(vmem, vmem),
        scratch_shapes=[
            pltpu.VMEM((NF, CR + 6, CL, CZ), F32),
            pltpu.VMEM((CR, CL, CZ), F32),
            pltpu.VMEM((CH, TP), F32),
            pltpu.VMEM((256, 256), BF16),
            pltpu.VMEM((96, 256), BF16),
            pltpu.VMEM((2, CR, 8, CZ), F32),
            pltpu.VMEM((2, CR, 16, CZ), F32),
            pltpu.VMEM((2, CR, 8, CZ), F32),
            pltpu.VMEM((2, CR, 16, CZ), F32),
            pltpu.VMEM((2, NF, 3, CL, CZ), F32),
            pltpu.VMEM((2, NF, 3, CL, CZ), F32),
            pltpu.VMEM((8, 256), F32),
            pltpu.VMEM((CR * 8, 2 * TP), F32),
            pltpu.VMEM((NYX, NZC, 2 * TP), F32),
            pltpu.VMEM((NYX, NZC, 2 * TP), F32),
            pltpu.VMEM((NZC, 1, 2 * TP), F32),
            pltpu.VMEM((NZC, 1, 2 * TP), F32),
            pltpu.VMEM((1, TP), F32),
            pltpu.VMEM((NZC, 1, TP), F32),
            pltpu.VMEM((NYX, NZC, 1, TP), F32),
            dma((NB,)), dma, dma,
            dma((2, NB)), dma((2, NB)), dma((2, NB)), dma((2, NB)),
            dma((2, 2)), dma((2, 2)),
            dma((NYX,)), dma((NYX,)), dma((NZC,)), dma((NZC,)),
            dma((NZC,)), dma((NZC,)), dma((NYX,)), dma((NYX,)),
        ],
        compiler_params=pltpu.CompilerParams(
            collective_id=0, has_side_effects=True, vmem_limit_bytes=40 << 20
        ),
    )(
        state,
        flux_volume,
        phase_density.reshape(CH, TP),
        flux_matrices,
        wave_speed,
        block_tile.reshape(CR, 1),
        tile_of_device.reshape(1, DEVICES),
        injection,
        drift_courant.reshape(1, CH),
        energy_weight.reshape(1, CH),
        jnp.asarray(constants()),
    )
    return coupled, drifted[None]


def solution(mesh):
    in_specs = (
        P(None, "rad", "lon", None),
        P(),
        P(),
        P("rad", "lon", None),
        P("lon", "rad", None),
        P(),
        P(("rad", "lon"), None, None),
        P(),
        P(),
        P(),
    )
    out_specs = (P(None, "rad", "lon", None), P(("rad", "lon"), None, None))
    return jax.shard_map(
        per_device, mesh=mesh, in_specs=in_specs, out_specs=out_specs, check_vma=False
    )
```

```python
import numpy as np

import jax
import jax.numpy as jnp
import ml_dtypes
from jax import lax
from jax.experimental import pallas as pl
from jax.experimental.pallas import tpu as pltpu
from jax.sharding import PartitionSpec as P

F32 = jnp.float32
BF16 = jnp.bfloat16
HIGHEST = lax.Precision.HIGHEST
MESH = pl.DeviceIdType.MESH

NF, CR, CL, CZ = 8, 64, 16, 256
ZSEG = 8
DRIFT = 3
CH, TP = 200, 128
NRAD, NLON = 4, 32
NYX, NZC = 16, 8
DEVICES = NRAD * NLON

SCALE = 0.4 * 0.5 / 30.0
ORDER = (0, 7, 1, 2, 3, 4, 5, 6)
ODD = {-3: -1.0, -2: 9.0, -1: -45.0, 1: 45.0, 2: -9.0, 3: 1.0}
EVEN = {-3: 1.0, -2: -6.0, -1: 15.0, 0: -20.0, 1: 15.0, 2: -6.0, 3: 1.0}

RB = 8
NB = CR // RB
AHEAD = 4

C_FIX07, C_FIX, C_SEG, C_MASK, C_ODD, C_EVEN, C_EODD, C_EEVEN, C_END = (
    0, 128, 224, 480, 496, 512, 528, 576, 624
)


def constants():
    t = np.zeros((C_END, 128), np.float32)
    half = 64
    for c in range(2):
        for r in range(4):
            for l in range(CL):
                row = C_FIX07 + (c * 4 + r) * CL + l
                for h in range(2):
                    if l < 3:
                        t[row, h * half + r * 8 + 3 * c + l] = 1
                    if l >= CL - 3:
                        t[row, h * half + 32 + r * 8 + 3 * c + l - (CL - 3)] = 1
    for pos in range(2, NF):
        for l in range(CL):
            row = C_FIX + (pos - 2) * CL + l
            for h in range(2):
                if l < 3:
                    t[row, h * half + 3 * pos + l] = 1
                if l >= CL - 3:
                    t[row, h * half + 24 + 3 * pos + l - (CL - 3)] = 1
    for z in range(CZ):
        for p in range(TP):
            t[C_SEG + z, p] = z // (CZ // ZSEG) == p % ZSEG
    for l in range(CL):
        for p in range(TP):
            t[C_MASK + l, p] = p // ZSEG == l
    for l in range(CL):
        for f in range(NF):
            for j in range(CL):
                t[C_ODD + l, f * CL + j] = ODD.get(j - l, 0.0)
                t[C_EVEN + l, f * CL + j] = EVEN.get(j - l, 0.0)
    for side in range(2):
        for pos in range(NF):
            for k in range(3):
                row = side * 24 + 3 * pos + k
                for f in range(NF):
                    for j in range(CL):
                        off = j - CL - k if side == 0 else 3 + j - k
                        t[C_EODD + row, f * CL + j] = ODD.get(off, 0.0)
                        if f == ORDER[pos]:
                            t[C_EEVEN + row, f * CL + j] = EVEN.get(off, 0.0)
    return t.astype(ml_dtypes.bfloat16)


def split(x):
    hi = x.astype(BF16)
    return hi, (x - hi.astype(F32)).astype(BF16)


def kernel(
    state, volume, phase, matrices_in, speeds_in, targets_in, tiles_in, injection, courant, weight,
    table_in,
    out, drifted,
    matrices, speeds, targets, tiles, table, inj, cou, wei, cells, vol, dens, lhs, send0, send1,
    recv0, recv1, rad_send, rad_recv, cols, pay, hit_db, hit_bd, buf, ra, part, rb, p0, g0, g2,
    small_sem, load_sem, vol_sem, dens_sem, lon_s0, lon_r0, lon_s1, lon_r1, rad_s, rad_r,
    p0_s, p0_r, ra_s, ra_r, rb_s, rb_r, g2_s, g2_r,
):
    rad, lon = lax.axis_index("rad"), lax.axis_index("lon")
    right, left = lax.rem(lon + 1, NLON), lax.rem(lon + NLON - 1, NLON)
    me_yx = rad * (NYX // NRAD) + lax.div(lon, NZC)
    me_zc = lax.rem(lon, NZC)

    def yx_peer(k):
        a = lax.rem(me_yx + k, NYX)
        return a, (lax.div(a, NYX // NRAD), lax.rem(a, NYX // NRAD) * NZC + me_zc)

    def zc_peer(k):
        i = lax.rem(me_zc + k, NZC)
        return i, (rad, lon - me_zc + i)

    small = [
        pltpu.make_async_copy(src, dst, small_sem.at[i])
        for i, (src, dst) in enumerate((
            (matrices_in, matrices), (speeds_in, speeds), (table_in, table),
            (targets_in, targets), (tiles_in, tiles),
            (injection, inj), (courant, cou), (weight, wei),
        ))
    ]
    for copy in small:
        copy.start()

    def load(b):
        return pltpu.make_async_copy(
            state.at[:, pl.ds(b * RB, RB)], cells.at[:, pl.ds(3 + b * RB, RB)], load_sem.at[b]
        )

    for b in [0, 1, NB - 1] + list(range(2, NB - 1)):
        load(b).start()
    vol_copy = pltpu.make_async_copy(volume, vol, vol_sem)
    vol_copy.start()
    dens_copy = pltpu.make_async_copy(phase, dens, dens_sem)
    dens_copy.start()

    barrier = pltpu.get_barrier_semaphore()

    def greet(device):
        pl.semaphore_signal(barrier, inc=1, device_id=device, device_id_type=MESH)

    greet((rad, right))
    greet((rad, left))
    for k in range(1, NYX):
        greet(yx_peer(k)[1])
    for k in range(1, NZC):
        greet(zc_peer(k)[1])

    cells[:, 0:3] = jnp.zeros((NF, 3, CL, CZ), F32)
    cells[:, 3 + CR :] = jnp.zeros((NF, 3, CL, CZ), F32)

    for copy in small:
        copy.wait()
    lane = lax.broadcasted_iota(jnp.int32, (CL, 128), 1)
    sub = lax.broadcasted_iota(jnp.int32, (CL, 128), 0)
    block = lax.shift_right_logical(lane, 4)
    same_l = jnp.bitwise_and(lane, CL - 1) == sub
    odd, even = table[C_ODD : C_ODD + CL].astype(F32), table[C_EVEN : C_EVEN + CL].astype(F32)
    rows_l = []
    for f in range(NF):
        row_r = jnp.zeros((CL, 128), F32)
        row_l = jnp.zeros((CL, 128), F32)
        for g in range(NF):
            row_r = jnp.where(block == g, matrices[0, f, g], row_r)
            row_l = jnp.where(block == g, matrices[1, f, g], row_l)
        rows_l.append(row_l)
        eye = lane == sub + f * CL
        w = (
            (SCALE * speeds[1]) * jnp.where(block == f, even, 0.0)
            - SCALE * row_l * odd
            + jnp.where(eye, 1.0 - 20.0 * SCALE * speeds[0], 0.0)
        )
        whi, wlo = split(w)
        rhi, rlo = split(jnp.where(same_l, (-45.0 * SCALE) * row_r, 0.0))
        at = f * CL
        lhs[at : at + CL, 0:128] = wlo
        lhs[at : at + CL, 128:256] = rlo
        lhs[128 + at : 128 + at + CL, 0:128] = whi
        lhs[128 + at : 128 + at + CL, 128:256] = rhi
    q = lax.broadcasted_iota(jnp.int32, (24, 128), 0)
    row_e = jnp.zeros((24, 128), F32)
    for pos, f in enumerate(ORDER):
        wide = jnp.concatenate([rows_l[f][0:8]] * 3, axis=0)
        row_e = jnp.where((q >= 3 * pos) & (q < 3 * pos + 3), wide, row_e)
    row_e = jnp.concatenate([row_e, row_e], axis=0)
    we = (SCALE * speeds[1]) * table[C_EEVEN : C_EEVEN + 48].astype(F32) - (
        SCALE * row_e * table[C_EODD : C_EODD + 48].astype(F32)
    )
    ehi, elo = split(we)
    lhs[256:304, 0:128] = ehi
    lhs[304:352, 0:128] = elo
    lhs[256:352, 128:256] = jnp.zeros((96, 128), BF16)

    def row(i):
        return cells[:, i].reshape(NF * CL, CZ)

    def rad_edge(side):
        for k in range(3):
            d = jnp.zeros((128, CZ), F32)
            e = jnp.zeros((128, CZ), F32)
            for j in range(3):
                off = j - k - 3 if side == 0 else 3 + j - k
                if off in ODD:
                    u = row(CR + j if side == 0 else 3 + j)
                    d = d + (ODD[off] / 45.0) * u
                    e = e + EVEN[off] * u
            dh, dl = split(d)
            y = (
                jnp.dot(lhs[0:128, 128:256], dh, preferred_element_type=F32)
                + jnp.dot(lhs[128:256, 128:256], dh, preferred_element_type=F32)
                + jnp.dot(lhs[128:256, 128:256], dl, preferred_element_type=F32)
                + (SCALE * speeds[0]) * e
            )
            for pos, f in enumerate(ORDER):
                rad_send[side, pos, k] = y[f * CL : (f + 1) * CL]

    def rad_copy(side, part):
        fields = pl.ds(0, 2) if part == 0 else pl.ds(2, NF - 2)
        return pltpu.make_async_remote_copy(
            src_ref=rad_send.at[side, fields],
            dst_ref=rad_recv.at[side, fields],
            send_sem=rad_s.at[side, part],
            recv_sem=rad_r.at[side, part],
            device_id=(rad + 1 if side == 0 else rad - 1, lon),
            device_id_type=MESH,
        )

    has = (rad < NRAD - 1, rad > 0)

    def lon_copy(side, part, b):
        src, dst = (send0, recv0) if part == 0 else (send1, recv1)
        ss, rs = (lon_s0, lon_r0) if part == 0 else (lon_s1, lon_r1)
        rows = pl.ds(b * RB, RB)
        return pltpu.make_async_remote_copy(
            src_ref=src.at[side, rows],
            dst_ref=dst.at[side, rows],
            send_sem=ss.at[side, b],
            recv_sem=rs.at[side, b],
            device_id=(rad, right if side == 0 else left),
            device_id_type=MESH,
        )

    def bulk(r, _):
        m3, m2, m1, u, p1, p2, p3 = (row(r + i) for i in range(7))
        d = (p1 - m1) - 0.2 * ((p2 - m2) - (1.0 / 9.0) * (p3 - m3))
        e = (p1 + m1) - 0.4 * ((p2 + m2) - (1.0 / 6.0) * (p3 + m3))
        xh, xl = split(u)
        dh, dl = split(d)
        t1 = jnp.concatenate([xh, dh], axis=0)
        t2 = jnp.concatenate([xl, dl], axis=0)
        y1 = jnp.dot(lhs[...], t1, preferred_element_type=F32)
        y2 = jnp.dot(lhs[128:304], t2, preferred_element_type=F32)
        new = (y1[0:128] + y1[128:256] + y2[0:128]) + (15.0 * SCALE * speeds[0]) * e
        out[:, r] = new.reshape(NF, CL, CZ)
        edge = y1[256:304] + y1[304:352] + y2[128:176]
        for side in range(2):
            send0[side, r] = edge[side * 24 : side * 24 + 8]
            send1[side, r] = edge[side * 24 + 8 : side * 24 + 24]
        return 0

    def bulk_chunk(b):
        lax.fori_loop(0, RB, lambda i, _: bulk(b * RB + i, _), 0, unroll=4)

    def send_early(b):
        lon_copy(0, 0, b).start()
        lon_copy(1, 0, b).start()

    def send_late(b, _):
        lon_copy(0, 1, b).start()
        lon_copy(1, 1, b).start()
        return 0

    load(0).wait()
    load(1).wait()
    bulk_chunk(0)
    pl.semaphore_wait(barrier, 2 + NYX - 1 + NZC - 1)
    send_early(0)
    load(NB - 1).wait()
    rad_edge(0)
    rad_edge(1)
    for part_of in range(2):
        for side in range(2):
            @pl.when(has[side])
            def _():
                rad_copy(side, part_of).start()

    cols[...] = jnp.zeros((8, 256), F32)
    cols[0:2, 0:CH] = inj[...]
    cols[2:3, 0:CH] = cou[...]
    cols[3:4, 0:CH] = wei[...]
    columns = cols[...].T
    channel_rate = jnp.broadcast_to(columns[0:CH, 2:3], (CH, TP))
    channel_weight = jnp.broadcast_to(columns[0:CH, 3:4], (CH, TP))

    def drift(density):
        for _ in range(DRIFT):
            density = density - channel_rate * (density - pltpu.roll(density, 1, axis=1))
        return density

    def moment(density):
        return jnp.sum(channel_weight * density, axis=0, keepdims=True)

    def p0_copy(k):
        i, device = zc_peer(k)
        return pltpu.make_async_remote_copy(
            src_ref=p0.at[me_zc], dst_ref=p0.at[me_zc], send_sem=p0_s.at[k],
            recv_sem=p0_r.at[k], device_id=device, device_id_type=MESH,
        )

    dens_copy.wait()
    p0[me_zc] = moment(drift(dens[...]))
    for k in range(1, NZC):
        p0_copy(k).start()

    rate_row, weight_row = cols[2:3], cols[3:4]
    keep = 1.0 - rate_row
    powers = (
        keep * keep * keep,
        3.0 * keep * keep * rate_row,
        3.0 * keep * rate_row * rate_row,
        rate_row * rate_row * rate_row,
    )
    taps = [
        [
            jnp.sum(0.5 * weight_row * cols[i : i + 1] * power, axis=1, keepdims=True)
            for power in powers
        ]
        for i in range(2)
    ]

    tile_col = jnp.broadcast_to(tiles[...].astype(F32), (DEVICES, DEVICES)).T
    target_row = jnp.broadcast_to(targets[...].astype(F32), (DEVICES, CR))
    hit = (tile_col[:, 0:CR] == target_row).astype(BF16)
    spread = lax.shift_right_logical(
        lax.broadcasted_iota(jnp.int32, (CR, CR * 8), 1), 3
    ) == lax.broadcasted_iota(jnp.int32, (CR, CR * 8), 0)
    hit_db[...] = jnp.dot(
        hit, spread.astype(F32).astype(BF16), preferred_element_type=F32
    ).astype(BF16)
    target_col = jnp.concatenate(
        [target_row, jnp.zeros((DEVICES, DEVICES - CR), F32)], axis=1
    ).T
    hit_bd[...] = (target_col[0:CR] == tiles[...].astype(F32)).astype(F32).astype(BF16)

    def rest(b, _):
        @pl.when(b < NB - 2)
        def _():
            load(b + 1).wait()

        bulk_chunk(b)
        send_early(b)
        return 0

    lax.fori_loop(1, NB, rest, 0)
    lax.fori_loop(0, AHEAD, send_late, 0)

    def add_rad(part):
        for side in range(2):
            @pl.when(has[1 - side])
            def _():
                rad_copy(side, part).wait_recv()
                for pos in range(2) if part == 0 else range(2, NF):
                    for k in range(3):
                        r = k if side == 0 else CR - 3 + k
                        out[ORDER[pos], r] = out[ORDER[pos], r] + rad_recv[side, pos, k]

    add_rad(0)
    vol_copy.wait()
    seg = table[C_SEG : C_SEG + CZ]
    mask = table[C_MASK : C_MASK + CL].astype(F32)

    def early(b, _):
        for i in range(2):
            lon_copy(0, 0, 2 * b + i).wait_recv()
            lon_copy(1, 0, 2 * b + i).wait_recv()
        for h in range(2 * RB // 4):
            r = b * 2 * RB + h * 4
            got = jnp.concatenate(
                [recv0[0, pl.ds(r, 4)].reshape(32, CZ), recv0[1, pl.ds(r, 4)].reshape(32, CZ)],
                axis=0,
            )
            hi, lo = split(got)
            add = jnp.dot(
                table[C_FIX07 : C_FIX07 + 128],
                jnp.concatenate([hi, lo], axis=0),
                preferred_element_type=F32,
            )
            v = vol[pl.ds(r, 4)].reshape(64, CZ)
            for c, f in enumerate((0, 7)):
                new = out[f, pl.ds(r, 4)].reshape(64, CZ) + add[c * 64 : (c + 1) * 64]
                out[f, pl.ds(r, 4)] = new.reshape(4, CL, CZ)
                yh, yl = split(v * new)
                t = jnp.dot(yh, seg, preferred_element_type=F32) + jnp.dot(
                    yl, seg, preferred_element_type=F32
                )
                t = t.reshape(4, CL, TP) * mask[None]
                pay[pl.ds(r * 8, 32), c * TP : (c + 1) * TP] = (t[:, 0:8] + t[:, 8:16]).reshape(
                    32, TP
                )
        return 0

    lax.fori_loop(0, NB // 2, early, 0)

    pay_hi, pay_lo = split(pay[...])
    buf[...] = (
        jnp.dot(hit_db[...], pay_hi, preferred_element_type=F32)
        + jnp.dot(hit_db[...], pay_lo, preferred_element_type=F32)
    ).reshape(NYX, NZC, 2 * TP)

    def ra_copy(k):
        a, device = yx_peer(k)
        return pltpu.make_async_remote_copy(
            src_ref=buf.at[a], dst_ref=ra.at[k], send_sem=ra_s.at[k], recv_sem=ra_r.at[k],
            device_id=device, device_id_type=MESH,
        )

    def rb_copy(k):
        i, device = zc_peer(k)
        return pltpu.make_async_remote_copy(
            src_ref=part, dst_ref=rb.at[k], send_sem=rb_s.at[k], recv_sem=rb_r.at[k],
            device_id=device, device_id_type=MESH,
        )

    def g2_copy(k):
        a, device = yx_peer(k)
        return pltpu.make_async_remote_copy(
            src_ref=g0, dst_ref=g2.at[me_yx], send_sem=g2_s.at[k], recv_sem=g2_r.at[k],
            device_id=device, device_id_type=MESH,
        )

    def late(b, _):
        lon_copy(0, 1, b).wait_recv()
        lon_copy(1, 1, b).wait_recv()

        def late_row(i, _):
            r = b * RB + i
            got = jnp.concatenate(
                [recv0[0, r], recv1[0, r], recv0[1, r], recv1[1, r], jnp.zeros((16, CZ), F32)],
                axis=0,
            )
            hi, lo = split(got)
            add = jnp.dot(
                table[C_FIX : C_FIX + 96],
                jnp.concatenate([hi, lo], axis=0),
                preferred_element_type=F32,
            )
            out[1:7, r] = out[1:7, r] + add.reshape(6, CL, CZ)
            return 0

        lax.fori_loop(0, RB, late_row, 0, unroll=8)
        return 0

    for k in range(1, NYX):
        ra_copy(k).start()
    add_rad(1)
    lax.fori_loop(0, 2, late, 0)
    total = buf[me_yx]
    for k in range(1, NYX):
        ra_copy(k).wait_recv()
        total = total + ra[k]
    part[...] = total
    for k in range(1, NZC):
        rb_copy(k).start()
    lax.fori_loop(AHEAD, NB, send_late, 0)
    lax.fori_loop(2, AHEAD, late, 0)
    source = part[...]
    for k in range(1, NZC):
        rb_copy(k).wait_recv()
        source = source + rb[k]
    for k in range(1, NZC):
        p0_copy(k).wait_recv()
    pressure = p0[...].reshape(NZC, TP)
    for i in range(2):
        s = source[:, i * TP : (i + 1) * TP]
        for n in range(4):
            pressure = pressure + taps[i][n] * (pltpu.roll(s, n, axis=1) if n else s)
    g0[...] = pressure
    for k in range(1, NYX):
        g2_copy(k).start()
    g2[me_yx] = pressure

    own = lax.broadcasted_iota(jnp.int32, (NZC, 2 * TP), 0) == me_zc
    mine = jnp.sum(jnp.where(own, source, 0.0), axis=0, keepdims=True)
    drifted[...] = drift(
        dens[...]
        + 0.5 * (columns[0:CH, 0:1] * mine[:, 0:TP] + columns[0:CH, 1:2] * mine[:, TP:])
    )
    lax.fori_loop(AHEAD, NB - 1, late, 0)

    for k in range(1, NYX):
        g2_copy(k).wait_recv()
    back_hi, back_lo = split(g2[...].reshape(DEVICES, TP))
    pay[0:CR, 0:TP] = jnp.dot(hit_bd[...], back_hi, preferred_element_type=F32) + jnp.dot(
        hit_bd[...], back_lo, preferred_element_type=F32
    )

    def nudge(b, _):
        got = pay[pl.ds(b * RB, RB), 0:TP]
        wide = jnp.broadcast_to(got[:, None, :], (RB, CL, TP)) * mask[None]
        hi, lo = split(wide.reshape(RB * CL, TP))
        dims = (((1,), (1,)), ((), ()))
        back = lax.dot_general(hi, seg, dims, preferred_element_type=F32) + lax.dot_general(
            lo, seg, dims, preferred_element_type=F32
        )
        old = out[7, pl.ds(b * RB, RB)].reshape(RB * CL, CZ)
        out[7, pl.ds(b * RB, RB)] = (old + 0.5 * (back - old)).reshape(RB, CL, CZ)
        return 0

    lax.fori_loop(0, NB, nudge, 0)
    lax.fori_loop(NB - 1, NB, late, 0)

    def sent(b, _):
        for side in range(2):
            for part in range(2):
                lon_copy(side, part, b).wait_send()
        return 0

    lax.fori_loop(0, NB, sent, 0)
    for side in range(2):
        @pl.when(has[side])
        def _():
            rad_copy(side, 0).wait_send()
            rad_copy(side, 1).wait_send()
    for k in range(1, NYX):
        ra_copy(k).wait_send()
        g2_copy(k).wait_send()
    for k in range(1, NZC):
        rb_copy(k).wait_send()
        p0_copy(k).wait_send()


def finish(fields, density, fields_out, density_out, sem):
    copies = [
        pltpu.make_async_copy(fields.at[f], fields_out.at[f], sem.at[f]) for f in range(NF)
    ] + [pltpu.make_async_copy(density, density_out, sem.at[NF])]
    for copy in copies:
        copy.start()
    for copy in copies:
        copy.wait()


def per_device(
    state, flux_matrices, wave_speed, flux_volume, block_tile, tile_of_device,
    phase_density, injection, drift_courant, energy_weight,
):
    hbm = pl.BlockSpec(memory_space=pltpu.HBM)
    vmem = pl.BlockSpec(memory_space=pltpu.VMEM)
    dma = pltpu.SemaphoreType.DMA
    coupled, drifted = pl.pallas_call(
        kernel,
        out_shape=(
            pltpu.VMEM((NF, CR, CL, CZ), F32),
            pltpu.VMEM((CH, TP), F32),
        ),
        in_specs=[hbm] * 11,
        out_specs=(vmem, vmem),
        scratch_shapes=[
            pltpu.SMEM((2, NF, NF), F32),
            pltpu.SMEM((2,), F32),
            pltpu.VMEM((1, CR), jnp.int32),
            pltpu.VMEM((1, DEVICES), jnp.int32),
            pltpu.VMEM((C_END, 128), BF16),
            pltpu.VMEM((2, CH), F32),
            pltpu.VMEM((1, CH), F32),
            pltpu.VMEM((1, CH), F32),
            pltpu.VMEM((NF, CR + 6, CL, CZ), F32),
            pltpu.VMEM((CR, CL, CZ), F32),
            pltpu.VMEM((CH, TP), F32),
            pltpu.VMEM((352, 256), BF16),
            pltpu.VMEM((2, CR, 8, CZ), F32),
            pltpu.VMEM((2, CR, 16, CZ), F32),
            pltpu.VMEM((2, CR, 8, CZ), F32),
            pltpu.VMEM((2, CR, 16, CZ), F32),
            pltpu.VMEM((2, NF, 3, CL, CZ), F32),
            pltpu.VMEM((2, NF, 3, CL, CZ), F32),
            pltpu.VMEM((8, 256), F32),
            pltpu.VMEM((CR * 8, 2 * TP), F32),
            pltpu.VMEM((DEVICES, CR * 8), BF16),
            pltpu.VMEM((CR, DEVICES), BF16),
            pltpu.VMEM((NYX, NZC, 2 * TP), F32),
            pltpu.VMEM((NYX, NZC, 2 * TP), F32),
            pltpu.VMEM((NZC, 2 * TP), F32),
            pltpu.VMEM((NZC, NZC, 2 * TP), F32),
            pltpu.VMEM((NZC, 1, TP), F32),
            pltpu.VMEM((NZC, TP), F32),
            pltpu.VMEM((NYX, NZC, TP), F32),
            dma((8,)), dma((NB,)), dma, dma,
            dma((2, NB)), dma((2, NB)), dma((2, NB)), dma((2, NB)),
            dma((2, 2)), dma((2, 2)),
            dma((NZC,)), dma((NZC,)), dma((NYX,)), dma((NYX,)),
            dma((NZC,)), dma((NZC,)), dma((NYX,)), dma((NYX,)),
        ],
        compiler_params=pltpu.CompilerParams(
            collective_id=0, has_side_effects=True, vmem_limit_bytes=54 << 20
        ),
    )(
        state,
        flux_volume,
        phase_density.reshape(CH, TP),
        flux_matrices,
        wave_speed,
        block_tile.reshape(1, CR),
        tile_of_device.reshape(1, DEVICES),
        injection,
        drift_courant.reshape(1, CH),
        energy_weight.reshape(1, CH),
        jnp.asarray(constants()),
    )
    coupled, drifted = pl.pallas_call(
        finish,
        out_shape=(
            jax.ShapeDtypeStruct((NF, CR, CL, CZ), F32),
            jax.ShapeDtypeStruct((CH, TP), F32),
        ),
        in_specs=[vmem, vmem],
        out_specs=(hbm, hbm),
        scratch_shapes=[dma((NF + 1,))],
        compiler_params=pltpu.CompilerParams(vmem_limit_bytes=1 << 20),
    )(coupled, drifted)
    return coupled, drifted[None]


def solution(mesh):
    in_specs = (
        P(None, "rad", "lon", None),
        P(),
        P(),
        P("rad", "lon", None),
        P("lon", "rad", None),
        P(),
        P(("rad", "lon"), None, None),
        P(),
        P(),
        P(),
    )
    out_specs = (P(None, "rad", "lon", None), P(("rad", "lon"), None, None))
    return jax.shard_map(
        per_device, mesh=mesh, in_specs=in_specs, out_specs=out_specs, check_vma=False
    )
```

```python
import numpy as np

import jax
import jax.numpy as jnp
import ml_dtypes
from jax import lax
from jax.experimental import pallas as pl
from jax.experimental.pallas import tpu as pltpu
from jax.sharding import PartitionSpec as P

F32 = jnp.float32
BF16 = jnp.bfloat16
HIGHEST = lax.Precision.HIGHEST
MESH = pl.DeviceIdType.MESH

NF, CR, CL, CZ = 8, 64, 16, 256
ZSEG = 8
DRIFT = 3
CH, TP = 200, 128
NRAD, NLON = 4, 32
NYX, NZC = 16, 8
DEVICES = NRAD * NLON

SCALE = 0.4 * 0.5 / 30.0
ORDER = (0, 7, 1, 2, 3, 4, 5, 6)
ODD = {-3: -1.0, -2: 9.0, -1: -45.0, 1: 45.0, 2: -9.0, 3: 1.0}
EVEN = {-3: 1.0, -2: -6.0, -1: 15.0, 0: -20.0, 1: 15.0, 2: -6.0, 3: 1.0}

RB = 8
NB = CR // RB
SENDS = (0, 2, 4, 6, NB)
PASS = (10,)
LATE = (4, 7)

C_FIX07, C_FIX, C_SEG, C_MASK, C_ODD, C_EVEN, C_EODD, C_EEVEN, C_END = (
    0, 128, 512, 768, 784, 800, 816, 864, 912
)
L_07, H_07, H_EDGE, L_EDGE, L_16, H_16, M_END = 0, 32, 64, 112, 160, 256, 352


def constants():
    t = np.zeros((C_END, 128), np.float32)
    half = 64
    for c in range(2):
        for r in range(4):
            for l in range(CL):
                row = C_FIX07 + (c * 4 + r) * CL + l
                for h in range(2):
                    if l < 3:
                        t[row, h * half + r * 6 + 3 * c + l] = 1
                    if l >= CL - 3:
                        t[row, h * half + 24 + r * 6 + 3 * c + l - (CL - 3)] = 1
    for r in range(4):
        for pos in range(2, NF):
            for l in range(CL):
                row = C_FIX + r * 96 + (pos - 2) * CL + l
                side = 0 if l < 3 else 1
                k = l if l < 3 else l - (CL - 3)
                if 0 <= k < 3:
                    q = 3 * pos + k
                    at = side * 16 + q - 8 if q >= 8 else 32 + side * 8 + r * 2 + q - 6
                    for h in range(2):
                        t[row, h * half + at] = 1
    for z in range(CZ):
        for p in range(TP):
            t[C_SEG + z, p] = z // (CZ // ZSEG) == p % ZSEG
    for l in range(CL):
        for p in range(TP):
            t[C_MASK + l, p] = p // ZSEG == l
    for l in range(CL):
        for f in range(NF):
            for j in range(CL):
                t[C_ODD + l, f * CL + j] = ODD.get(j - l, 0.0)
                t[C_EVEN + l, f * CL + j] = EVEN.get(j - l, 0.0)
    for side in range(2):
        for pos in range(NF):
            for k in range(3):
                row = side * 24 + 3 * pos + k
                for f in range(NF):
                    for j in range(CL):
                        off = j - CL - k if side == 0 else 3 + j - k
                        t[C_EODD + row, f * CL + j] = ODD.get(off, 0.0)
                        if f == ORDER[pos]:
                            t[C_EEVEN + row, f * CL + j] = EVEN.get(off, 0.0)
    return t.astype(ml_dtypes.bfloat16)


def split(x):
    hi = x.astype(BF16)
    return hi, (x - hi.astype(F32)).astype(BF16)


def kernel(
    state, volume, phase, matrices_in, speeds_in, targets_in, tiles_in, injection, courant, weight,
    table_in,
    out, drifted,
    matrices, speeds, targets, tiles, table, inj, cou, wei, cells, vol, dens, lhs, tt1, tt2,
    send0, send1, recv0, recv1, rad_send, rad_recv, cols, pay, hit_db, hit_bd, seg_t, buf, ra,
    part, rb, g0, g2,
    small_sem, load_sem, vol_sem, dens_sem, lon_s0, lon_r0, lon_s1, lon_r1, rad_s, rad_r,
    ra_s, ra_r, rb_s, rb_r, g2_s, g2_r,
):
    rad, lon = lax.axis_index("rad"), lax.axis_index("lon")
    right, left = lax.rem(lon + 1, NLON), lax.rem(lon + NLON - 1, NLON)
    me_yx = rad * (NYX // NRAD) + lax.div(lon, NZC)
    me_zc = lax.rem(lon, NZC)

    def yx_peer(k):
        a = lax.rem(me_yx + k, NYX)
        return a, (lax.div(a, NYX // NRAD), lax.rem(a, NYX // NRAD) * NZC + me_zc)

    def zc_peer(k):
        i = lax.rem(me_zc + k, NZC)
        return i, (rad, lon - me_zc + i)

    small = [
        pltpu.make_async_copy(src, dst, small_sem.at[i])
        for i, (src, dst) in enumerate((
            (matrices_in, matrices), (speeds_in, speeds), (table_in, table),
            (targets_in, targets), (tiles_in, tiles),
            (injection, inj), (courant, cou), (weight, wei),
        ))
    ]
    for copy in small:
        copy.start()

    def load(b):
        return pltpu.make_async_copy(
            state.at[:, pl.ds(b * RB, RB)], cells.at[:, pl.ds(3 + b * RB, RB)], load_sem.at[b]
        )

    for b in [0, 1, NB - 1] + list(range(2, NB - 1)):
        load(b).start()
    vol_copy = pltpu.make_async_copy(volume, vol, vol_sem)
    vol_copy.start()
    dens_copy = pltpu.make_async_copy(phase, dens, dens_sem)
    dens_copy.start()

    barrier = pltpu.get_barrier_semaphore()

    def greet(device):
        pl.semaphore_signal(barrier, inc=1, device_id=device, device_id_type=MESH)

    greet((rad, right))
    greet((rad, left))
    for k in range(1, NYX):
        greet(yx_peer(k)[1])
    for k in range(1, NZC):
        greet(zc_peer(k)[1])

    cells[:, 0:3] = jnp.zeros((NF, 3, CL, CZ), F32)
    cells[:, 3 + CR :] = jnp.zeros((NF, 3, CL, CZ), F32)

    for copy in small:
        copy.wait()
    lane = lax.broadcasted_iota(jnp.int32, (CL, 128), 1)
    sub = lax.broadcasted_iota(jnp.int32, (CL, 128), 0)
    block = lax.shift_right_logical(lane, 4)
    same_l = jnp.bitwise_and(lane, CL - 1) == sub
    odd, even = table[C_ODD : C_ODD + CL].astype(F32), table[C_EVEN : C_EVEN + CL].astype(F32)
    rows_l = []
    for f in range(NF):
        row_r = jnp.zeros((CL, 128), F32)
        row_l = jnp.zeros((CL, 128), F32)
        for g in range(NF):
            row_r = jnp.where(block == g, matrices[0, f, g], row_r)
            row_l = jnp.where(block == g, matrices[1, f, g], row_l)
        rows_l.append(row_l)
        eye = lane == sub + f * CL
        w = (
            (SCALE * speeds[1]) * jnp.where(block == f, even, 0.0)
            - SCALE * row_l * odd
            + jnp.where(eye, 1.0 - 20.0 * SCALE * speeds[0], 0.0)
        )
        whi, wlo = split(w)
        rhi, rlo = split(jnp.where(same_l, (-45.0 * SCALE) * row_r, 0.0))
        if f in (0, 7):
            lo_at, hi_at = L_07 + (0 if f == 0 else CL), H_07 + (0 if f == 0 else CL)
        else:
            lo_at, hi_at = L_16 + (f - 1) * CL, H_16 + (f - 1) * CL
        lhs[lo_at : lo_at + CL, 0:128] = wlo
        lhs[lo_at : lo_at + CL, 128:256] = rlo
        lhs[hi_at : hi_at + CL, 0:128] = whi
        lhs[hi_at : hi_at + CL, 128:256] = rhi
    q = lax.broadcasted_iota(jnp.int32, (24, 128), 0)
    row_e = jnp.zeros((24, 128), F32)
    for pos, f in enumerate(ORDER):
        wide = jnp.concatenate([rows_l[f][0:8]] * 3, axis=0)
        row_e = jnp.where((q >= 3 * pos) & (q < 3 * pos + 3), wide, row_e)
    row_e = jnp.concatenate([row_e, row_e], axis=0)
    we = (SCALE * speeds[1]) * table[C_EEVEN : C_EEVEN + 48].astype(F32) - (
        SCALE * row_e * table[C_EODD : C_EODD + 48].astype(F32)
    )
    ehi, elo = split(we)
    lhs[H_EDGE : H_EDGE + 48, 0:128] = ehi
    lhs[L_EDGE : L_EDGE + 48, 0:128] = elo
    lhs[H_EDGE : H_EDGE + 96, 128:256] = jnp.zeros((96, 128), BF16)

    def row(i):
        return cells[:, i].reshape(NF * CL, CZ)

    def rad_edge(side):
        high = jnp.concatenate([lhs[H_07 : H_07 + 32, 128:], lhs[H_16 : H_16 + 96, 128:]], axis=0)
        low = jnp.concatenate([lhs[L_07 : L_07 + 32, 128:], lhs[L_16 : L_16 + 96, 128:]], axis=0)
        for k in range(3):
            d = jnp.zeros((128, CZ), F32)
            e = jnp.zeros((128, CZ), F32)
            for j in range(3):
                off = j - k - 3 if side == 0 else 3 + j - k
                if off in ODD:
                    u = row(CR + j if side == 0 else 3 + j)
                    d = d + (ODD[off] / 45.0) * u
                    e = e + EVEN[off] * u
            dh, dl = split(d)
            y = (
                jnp.dot(high, dh, preferred_element_type=F32)
                + jnp.dot(low, dh, preferred_element_type=F32)
                + jnp.dot(high, dl, preferred_element_type=F32)
            )
            for pos, f in enumerate(ORDER):
                rad_send[side, pos, k] = y[pos * CL : (pos + 1) * CL] + (
                    SCALE * speeds[0]
                ) * e[f * CL : (f + 1) * CL]

    rad_parts = ((0, 2), (2, 3), (5, 3))

    def rad_copy(side, part_of):
        fields = pl.ds(*rad_parts[part_of])
        return pltpu.make_async_remote_copy(
            src_ref=rad_send.at[side, fields],
            dst_ref=rad_recv.at[side, fields],
            send_sem=rad_s.at[side, part_of],
            recv_sem=rad_r.at[side, part_of],
            device_id=(rad + 1 if side == 0 else rad - 1, lon),
            device_id_type=MESH,
        )

    def send_rad(part_of):
        for side in range(2):
            @pl.when(has[side])
            def _():
                rad_copy(side, part_of).start()

    has = (rad < NRAD - 1, rad > 0)

    def lon_copy(side, part, b):
        src, dst = (send0, recv0) if part == 0 else (send1, recv1)
        ss, rs = (lon_s0, lon_r0) if part == 0 else (lon_s1, lon_r1)
        rows = pl.ds(b * (RB // 4), RB // 4)
        return pltpu.make_async_remote_copy(
            src_ref=src.at[side, rows],
            dst_ref=dst.at[side, rows],
            send_sem=ss.at[side, b],
            recv_sem=rs.at[side, b],
            device_id=(rad, right if side == 0 else left),
            device_id_type=MESH,
        )

    first_eight = lax.broadcasted_iota(jnp.int32, (8, CZ), 0)

    def pick(n, a, b):
        return jnp.where(first_eight < n, a, b)

    def first_pass(g, _):
        tops = ([], [])
        for i in range(4):
            r = 4 * g + i
            m3, m2, m1, u, p1, p2, p3 = (row(r + n) for n in range(7))
            d = (p1 - m1) - 0.2 * ((p2 - m2) - (1.0 / 9.0) * (p3 - m3))
            m3, m2, m1, p1, p2, p3 = (
                jnp.concatenate([x[0:CL], x[112:128]], axis=0) for x in (m3, m2, m1, p1, p2, p3)
            )
            e = (p1 + m1) - 0.4 * ((p2 + m2) - (1.0 / 6.0) * (p3 + m3))
            xh, xl = split(u)
            dh, dl = split(d)
            t1 = jnp.concatenate([xh, dh], axis=0)
            t2 = jnp.concatenate([xl, dl], axis=0)
            tt1[r] = t1
            tt2[r] = t2
            y1 = jnp.dot(lhs[L_07:L_16], t1, preferred_element_type=F32)
            y2 = jnp.dot(lhs[H_07:L_EDGE], t2, preferred_element_type=F32)
            new = (y1[0:32] + y1[32:64] + y2[0:32]) + (15.0 * SCALE * speeds[0]) * e
            out[0, r] = new[0:CL]
            out[7, r] = new[CL:]
            edge = y1[64:112] + y1[112:160] + y2[32:80]
            for side in range(2):
                tops[side].append(edge[side * 24 : side * 24 + 8])
                send1[side, g, i * 16 : (i + 1) * 16] = edge[side * 24 + 8 : side * 24 + 24]
        for side in range(2):
            z0, z1, z2, z3 = tops[side]
            a, b, c = pltpu.roll(z1, 6, axis=0), pltpu.roll(z2, 4, axis=0), pltpu.roll(z3, 2, axis=0)
            send0[side, g, 0:8] = pick(6, z0, a)
            send0[side, g, 8:16] = pick(4, a, b)
            send0[side, g, 16:24] = pick(2, b, c)
            a, b, c = pltpu.roll(z0, 2, axis=0), pltpu.roll(z1, 4, axis=0), pltpu.roll(z2, 6, axis=0)
            send1[side, g, 64:72] = pick(2, a, pick(4, b, pick(6, c, z3)))
        return 0

    def bulk_chunk(b):
        lax.fori_loop(0, RB // 4, lambda i, _: first_pass(b * (RB // 4) + i, _), 0)

    def second_pass(g, _):
        for i in range(4):
            r = 4 * g + i
            m3, m2, m1, _, p1, p2, p3 = (cells[1:7, r + n].reshape(96, CZ) for n in range(7))
            e = (p1 + m1) - 0.4 * ((p2 + m2) - (1.0 / 6.0) * (p3 + m3))
            y1 = jnp.dot(lhs[L_16:M_END], tt1[r], preferred_element_type=F32)
            y2 = jnp.dot(lhs[H_16:M_END], tt2[r], preferred_element_type=F32)
            new = (y1[0:96] + y1[96:192] + y2) + (15.0 * SCALE * speeds[0]) * e
            out[1:7, r] = new.reshape(6, CL, CZ)
        return 0

    def send_early(b):
        lon_copy(0, 0, b).start()
        lon_copy(1, 0, b).start()

    def send_late(b, _):
        lon_copy(0, 1, b).start()
        lon_copy(1, 1, b).start()
        return 0

    load(0).wait()
    load(1).wait()
    bulk_chunk(0)
    pl.semaphore_wait(barrier, 2 + NYX - 1 + NZC - 1)
    send_early(0)
    load(NB - 1).wait()
    rad_edge(0)
    rad_edge(1)
    send_rad(0)
    send_rad(1)

    tile_col = jnp.broadcast_to(tiles[...].astype(F32), (DEVICES, DEVICES)).T
    target_row = jnp.broadcast_to(targets[...].astype(F32), (DEVICES, CR))
    hit = (tile_col[:, 0:CR] == target_row).astype(BF16)
    spread = lax.shift_right_logical(
        lax.broadcasted_iota(jnp.int32, (CR, CR * 8), 1), 3
    ) == lax.broadcasted_iota(jnp.int32, (CR, CR * 8), 0)
    hit_db[...] = jnp.dot(
        hit, spread.astype(F32).astype(BF16), preferred_element_type=F32
    ).astype(BF16)
    target_col = jnp.concatenate(
        [target_row, jnp.zeros((DEVICES, DEVICES - CR), F32)], axis=1
    ).T
    hit_bd[...] = (target_col[0:CR] == tiles[...].astype(F32)).astype(F32).astype(BF16)

    seg_t[...] = (
        jnp.bitwise_and(lax.broadcasted_iota(jnp.int32, (2 * TP, CZ), 0), ZSEG - 1)
        == lax.shift_right_logical(lax.broadcasted_iota(jnp.int32, (2 * TP, CZ), 1), 5)
    ).astype(F32).astype(BF16)

    def rest(b, _):
        @pl.when(b < NB - 2)
        def _():
            load(b + 1).wait()

        bulk_chunk(b)
        send_early(b)
        return 0

    lax.fori_loop(1, NB, rest, 0)
    lax.fori_loop(SENDS[0], SENDS[1], send_late, 0)

    def add_rad(part_of):
        for side in range(2):
            @pl.when(has[1 - side])
            def _():
                rad_copy(side, part_of).wait_recv()
                for pos in range(rad_parts[part_of][0], sum(rad_parts[part_of])):
                    for k in range(3):
                        r = k if side == 0 else CR - 3 + k
                        out[ORDER[pos], r] = out[ORDER[pos], r] + rad_recv[side, pos, k]

    add_rad(0)
    vol_copy.wait()
    seg = table[C_SEG : C_SEG + CZ]
    mask = table[C_MASK : C_MASK + CL].astype(F32)

    def early(b, _):
        for i in range(2):
            lon_copy(0, 0, 2 * b + i).wait_recv()
            lon_copy(1, 0, 2 * b + i).wait_recv()
        highs, lows = [], []
        for h in range(4):
            g = b * 4 + h
            got = jnp.concatenate(
                [recv0[0, g], recv0[1, g], jnp.zeros((16, CZ), F32)], axis=0
            )
            add = jnp.dot(
                table[C_FIX07 : C_FIX07 + 128],
                jnp.concatenate(split(got), axis=0),
                preferred_element_type=F32,
            )
            v = vol[pl.ds(4 * g, 4)].reshape(64, CZ)
            for c, f in enumerate((0, 7)):
                new = out[f, pl.ds(4 * g, 4)].reshape(64, CZ) + add[c * 64 : (c + 1) * 64]
                out[f, pl.ds(4 * g, 4)] = new.reshape(4, CL, CZ)
                yh, yl = split(v * new)
                highs.append(yh)
                lows.append(yl)
        t = jnp.dot(jnp.concatenate(highs + lows, axis=0), seg, preferred_element_type=F32)
        t = t[0:512] + t[512:1024]
        for h in range(4):
            for c in range(2):
                at = (h * 2 + c) * 64
                x = t[at : at + 64].reshape(4, CL, TP) * mask[None]
                pay[pl.ds(b * 128 + h * 32, 32), c * TP : (c + 1) * TP] = (
                    x[:, 0:8] + x[:, 8:16]
                ).reshape(32, TP)
        return 0

    lax.fori_loop(0, NB // 2, early, 0)

    pay_hi, pay_lo = split(pay[...])
    buf[...] = (
        jnp.dot(hit_db[...], pay_hi, preferred_element_type=F32)
        + jnp.dot(hit_db[...], pay_lo, preferred_element_type=F32)
    ).reshape(NYX, NZC, 2 * TP)

    def ra_copy(k):
        a, device = yx_peer(k)
        return pltpu.make_async_remote_copy(
            src_ref=buf.at[a], dst_ref=ra.at[k], send_sem=ra_s.at[k], recv_sem=ra_r.at[k],
            device_id=device, device_id_type=MESH,
        )

    def rb_copy(k):
        i, device = zc_peer(k)
        return pltpu.make_async_remote_copy(
            src_ref=part, dst_ref=rb.at[me_zc], send_sem=rb_s.at[k], recv_sem=rb_r.at[k],
            device_id=device, device_id_type=MESH,
        )

    def g2_copy(k):
        a, device = yx_peer(k)
        return pltpu.make_async_remote_copy(
            src_ref=g0, dst_ref=g2.at[me_yx], send_sem=g2_s.at[k], recv_sem=g2_r.at[k],
            device_id=device, device_id_type=MESH,
        )

    def late(b, _):
        lon_copy(0, 1, b).wait_recv()
        lon_copy(1, 1, b).wait_recv()

        def late_row(i, _):
            r = b * RB + i
            got = jnp.concatenate(
                [recv0[0, r], recv1[0, r], recv0[1, r], recv1[1, r], jnp.zeros((16, CZ), F32)],
                axis=0,
            )
            hi, lo = split(got)
            add = jnp.dot(
                table[C_FIX : C_FIX + 96],
                jnp.concatenate([hi, lo], axis=0),
                preferred_element_type=F32,
            )
            out[1:7, r] = out[1:7, r] + add.reshape(6, CL, CZ)
            return 0

        lax.fori_loop(0, RB, late_row, 0, unroll=8)
        return 0

    def late(b, _):
        lon_copy(0, 1, b).wait_recv()
        lon_copy(1, 1, b).wait_recv()
        for h in range(RB // 4):
            g = b * (RB // 4) + h
            tail = [recv1[0, g, 64:72], recv1[1, g, 64:72], jnp.zeros((16, CZ), F32)]
            for i in range(4):
                got = jnp.concatenate(
                    [recv1[side, g, i * 16 : (i + 1) * 16] for side in range(2)] + tail, axis=0
                )
                add = jnp.dot(
                    table[C_FIX + i * 96 : C_FIX + (i + 1) * 96],
                    jnp.concatenate(split(got), axis=0),
                    preferred_element_type=F32,
                )
                r = 4 * g + i
                out[1:7, r] = out[1:7, r] + add.reshape(6, CL, CZ)
        return 0

    for k in range(1, NYX):
        ra_copy(k).start()
    lax.fori_loop(SENDS[1], SENDS[2], send_late, 0)
    send_rad(2)

    lax.fori_loop(0, PASS[0], second_pass, 0)
    cols[...] = jnp.zeros((8, 256), F32)
    cols[0:2, 0:CH] = inj[...]
    cols[2:3, 0:CH] = cou[...]
    cols[3:4, 0:CH] = wei[...]
    columns = cols[...].T
    channel_rate = jnp.broadcast_to(columns[0:CH, 2:3], (CH, TP))
    channel_weight = jnp.broadcast_to(columns[0:CH, 3:4], (CH, TP))

    def drift(density):
        for _ in range(DRIFT):
            density = density - channel_rate * (density - pltpu.roll(density, 1, axis=1))
        return density

    dens_copy.wait()
    bare = jnp.sum(channel_weight * drift(dens[...]), axis=0, keepdims=True)

    rate_row, weight_row = cols[2:3], cols[3:4]
    keep = 1.0 - rate_row
    powers = (
        keep * keep * keep,
        3.0 * keep * keep * rate_row,
        3.0 * keep * rate_row * rate_row,
        rate_row * rate_row * rate_row,
    )
    taps = [
        [
            jnp.sum(0.5 * weight_row * cols[i : i + 1] * power, axis=1, keepdims=True)
            for power in powers
        ]
        for i in range(2)
    ]

    total = buf[me_yx]
    for k in range(1, NYX):
        ra_copy(k).wait_recv()
        total = total + ra[k]
    part[:, 0 : 2 * TP] = total
    part[:, 2 * TP :] = jnp.broadcast_to(bare, (NZC, TP))
    for k in range(1, NZC):
        rb_copy(k).start()
    lax.fori_loop(SENDS[2], SENDS[3], send_late, 0)
    lax.fori_loop(PASS[0], CR // 4, second_pass, 0)
    add_rad(1)
    lax.fori_loop(0, LATE[0], late, 0)
    rb[me_zc] = part[...]
    for k in range(1, NZC):
        rb_copy(k).wait_recv()
    source = rb[0, :, 0 : 2 * TP]
    for j in range(1, NZC):
        source = source + rb[j, :, 0 : 2 * TP]
    tile_row = lax.broadcasted_iota(jnp.int32, (NZC, TP), 0)
    pressure = jnp.zeros((NZC, TP), F32)
    for j in range(NZC):
        pressure = jnp.where(tile_row == j, rb[j, :, 2 * TP :], pressure)
    for i in range(2):
        s = source[:, i * TP : (i + 1) * TP]
        for n in range(4):
            pressure = pressure + taps[i][n] * (pltpu.roll(s, n, axis=1) if n else s)
    g0[...] = pressure
    for k in range(1, NYX):
        g2_copy(k).start()
    lax.fori_loop(SENDS[3], SENDS[4], send_late, 0)
    g2[me_yx] = pressure

    own = lax.broadcasted_iota(jnp.int32, (NZC, 2 * TP), 0) == me_zc
    mine = jnp.sum(jnp.where(own, source, 0.0), axis=0, keepdims=True)
    drifted[...] = drift(
        dens[...]
        + 0.5 * (columns[0:CH, 0:1] * mine[:, 0:TP] + columns[0:CH, 1:2] * mine[:, TP:])
    )
    add_rad(2)
    lax.fori_loop(LATE[0], LATE[1], late, 0)

    for k in range(1, NYX):
        g2_copy(k).wait_recv()
    back_hi, back_lo = split(g2[...].reshape(DEVICES, TP))
    pay[0:CR, 0:TP] = jnp.dot(hit_bd[...], back_hi, preferred_element_type=F32) + jnp.dot(
        hit_bd[...], back_lo, preferred_element_type=F32
    )

    def nudge(b, _):
        got = pay[pl.ds(b * 16, 16), 0:TP]
        wide = jnp.broadcast_to(got[:, None, :], (16, CL, TP)) * mask[None]
        back = jnp.dot(
            jnp.concatenate(split(wide.reshape(16 * CL, TP)), axis=1),
            seg_t[...],
            preferred_element_type=F32,
        )
        old = out[7, pl.ds(b * 16, 16)].reshape(16 * CL, CZ)
        out[7, pl.ds(b * 16, 16)] = (old + 0.5 * (back - old)).reshape(16, CL, CZ)
        return 0

    lax.fori_loop(0, CR // 16, nudge, 0, unroll=2)
    lax.fori_loop(LATE[1], NB, late, 0)

    def sent(b, _):
        for side in range(2):
            for part in range(2):
                lon_copy(side, part, b).wait_send()
        return 0

    lax.fori_loop(0, NB, sent, 0)
    for side in range(2):
        @pl.when(has[side])
        def _():
            for part_of in range(3):
                rad_copy(side, part_of).wait_send()
    for k in range(1, NYX):
        ra_copy(k).wait_send()
        g2_copy(k).wait_send()
    for k in range(1, NZC):
        rb_copy(k).wait_send()


def finish(fields, density, fields_out, density_out, sem):
    copies = [
        pltpu.make_async_copy(fields.at[f], fields_out.at[f], sem.at[f]) for f in range(NF)
    ] + [pltpu.make_async_copy(density, density_out, sem.at[NF])]
    for copy in copies:
        copy.start()
    for copy in copies:
        copy.wait()


def per_device(
    state, flux_matrices, wave_speed, flux_volume, block_tile, tile_of_device,
    phase_density, injection, drift_courant, energy_weight,
):
    hbm = pl.BlockSpec(memory_space=pltpu.HBM)
    vmem = pl.BlockSpec(memory_space=pltpu.VMEM)
    dma = pltpu.SemaphoreType.DMA
    coupled, drifted = pl.pallas_call(
        kernel,
        out_shape=(
            pltpu.VMEM((NF, CR, CL, CZ), F32),
            pltpu.VMEM((CH, TP), F32),
        ),
        in_specs=[hbm] * 11,
        out_specs=(vmem, vmem),
        scratch_shapes=[
            pltpu.SMEM((2, NF, NF), F32),
            pltpu.SMEM((2,), F32),
            pltpu.VMEM((1, CR), jnp.int32),
            pltpu.VMEM((1, DEVICES), jnp.int32),
            pltpu.VMEM((C_END, 128), BF16),
            pltpu.VMEM((2, CH), F32),
            pltpu.VMEM((1, CH), F32),
            pltpu.VMEM((1, CH), F32),
            pltpu.VMEM((NF, CR + 6, CL, CZ), F32),
            pltpu.VMEM((CR, CL, CZ), F32),
            pltpu.VMEM((CH, TP), F32),
            pltpu.VMEM((M_END, 256), BF16),
            pltpu.VMEM((CR, 256, CZ), BF16),
            pltpu.VMEM((CR, 256, CZ), BF16),
            pltpu.VMEM((2, CR // 4, 24, CZ), F32),
            pltpu.VMEM((2, CR // 4, 72, CZ), F32),
            pltpu.VMEM((2, CR // 4, 24, CZ), F32),
            pltpu.VMEM((2, CR // 4, 72, CZ), F32),
            pltpu.VMEM((2, NF, 3, CL, CZ), F32),
            pltpu.VMEM((2, NF, 3, CL, CZ), F32),
            pltpu.VMEM((8, 256), F32),
            pltpu.VMEM((CR * 8, 2 * TP), F32),
            pltpu.VMEM((DEVICES, CR * 8), BF16),
            pltpu.VMEM((CR, DEVICES), BF16),
            pltpu.VMEM((2 * TP, CZ), BF16),
            pltpu.VMEM((NYX, NZC, 2 * TP), F32),
            pltpu.VMEM((NYX, NZC, 2 * TP), F32),
            pltpu.VMEM((NZC, 3 * TP), F32),
            pltpu.VMEM((NZC, NZC, 3 * TP), F32),
            pltpu.VMEM((NZC, TP), F32),
            pltpu.VMEM((NYX, NZC, TP), F32),
            dma((8,)), dma((NB,)), dma, dma,
            dma((2, NB)), dma((2, NB)), dma((2, NB)), dma((2, NB)),
            dma((2, 3)), dma((2, 3)), dma((NYX,)), dma((NYX,)),
            dma((NZC,)), dma((NZC,)), dma((NYX,)), dma((NYX,)),
        ],
        compiler_params=pltpu.CompilerParams(
            collective_id=0, has_side_effects=True, vmem_limit_bytes=54 << 20
        ),
    )(
        state,
        flux_volume,
        phase_density.reshape(CH, TP),
        flux_matrices,
        wave_speed,
        block_tile.reshape(1, CR),
        tile_of_device.reshape(1, DEVICES),
        injection,
        drift_courant.reshape(1, CH),
        energy_weight.reshape(1, CH),
        jnp.asarray(constants()),
    )
    coupled, drifted = pl.pallas_call(
        finish,
        out_shape=(
            jax.ShapeDtypeStruct((NF, CR, CL, CZ), F32),
            jax.ShapeDtypeStruct((CH, TP), F32),
        ),
        in_specs=[vmem, vmem],
        out_specs=(hbm, hbm),
        scratch_shapes=[dma((NF + 1,))],
        compiler_params=pltpu.CompilerParams(vmem_limit_bytes=1 << 20),
    )(coupled, drifted)
    return coupled, drifted[None]


def solution(mesh):
    in_specs = (
        P(None, "rad", "lon", None),
        P(),
        P(),
        P("rad", "lon", None),
        P("lon", "rad", None),
        P(),
        P(("rad", "lon"), None, None),
        P(),
        P(),
        P(),
    )
    out_specs = (P(None, "rad", "lon", None), P(("rad", "lon"), None, None))
    return jax.shard_map(
        per_device, mesh=mesh, in_specs=in_specs, out_specs=out_specs, check_vma=False
    )
```

```python
import numpy as np

import jax
import jax.numpy as jnp
import ml_dtypes
from jax import lax
from jax.experimental import pallas as pl
from jax.experimental.pallas import tpu as pltpu
from jax.sharding import PartitionSpec as P

F32 = jnp.float32
BF16 = jnp.bfloat16
HIGHEST = lax.Precision.HIGHEST
MESH = pl.DeviceIdType.MESH

NF, CR, CL, CZ = 8, 64, 16, 256
ZSEG = 8
DRIFT = 3
CH, TP = 200, 128
NRAD, NLON = 4, 32
NYX, NZC = 16, 8
DEVICES = NRAD * NLON

SCALE = 0.4 * 0.5 / 30.0
ORDER = (0, 7, 1, 2, 3, 4, 5, 6)
ODD = {-3: -1.0, -2: 9.0, -1: -45.0, 1: 45.0, 2: -9.0, 3: 1.0}
EVEN = {-3: 1.0, -2: -6.0, -1: 15.0, 0: -20.0, 1: 15.0, 2: -6.0, 3: 1.0}

RB = 8
NB = CR // RB
SENDS = (0, 3, 5, 7, NB)
PASS = (10,)
LATE = (4, 7)

C_FIX07, C_FIX, C_SEG, C_MASK, C_ODD, C_EVEN, C_EODD, C_EEVEN, C_END = (
    0, 128, 512, 768, 784, 800, 816, 864, 912
)
H_07, L_07, H_EDGE, L_EDGE, HR_07, LR_07, H_16, L_16, HR_16, LR_16, M_END = (
    0, 32, 64, 112, 160, 192, 224, 320, 416, 512, 608
)


def constants():
    t = np.zeros((C_END, 128), np.float32)
    half = 64
    for c in range(2):
        for r in range(4):
            for l in range(CL):
                row = C_FIX07 + (c * 4 + r) * CL + l
                for h in range(2):
                    if l < 3:
                        t[row, h * half + r * 6 + 3 * c + l] = 1
                    if l >= CL - 3:
                        t[row, h * half + 24 + r * 6 + 3 * c + l - (CL - 3)] = 1
    for r in range(4):
        for pos in range(2, NF):
            for l in range(CL):
                row = C_FIX + r * 96 + (pos - 2) * CL + l
                side = 0 if l < 3 else 1
                k = l if l < 3 else l - (CL - 3)
                if 0 <= k < 3:
                    q = 3 * pos + k
                    at = side * 16 + q - 8 if q >= 8 else 32 + side * 8 + r * 2 + q - 6
                    for h in range(2):
                        t[row, h * half + at] = 1
    for z in range(CZ):
        for p in range(TP):
            t[C_SEG + z, p] = z // (CZ // ZSEG) == p % ZSEG
    for l in range(CL):
        for p in range(TP):
            t[C_MASK + l, p] = p // ZSEG == l
    for l in range(CL):
        for f in range(NF):
            for j in range(CL):
                t[C_ODD + l, f * CL + j] = ODD.get(j - l, 0.0)
                t[C_EVEN + l, f * CL + j] = EVEN.get(j - l, 0.0)
    for side in range(2):
        for pos in range(NF):
            for k in range(3):
                row = side * 24 + 3 * pos + k
                for f in range(NF):
                    for j in range(CL):
                        off = j - CL - k if side == 0 else 3 + j - k
                        t[C_EODD + row, f * CL + j] = ODD.get(off, 0.0)
                        if f == ORDER[pos]:
                            t[C_EEVEN + row, f * CL + j] = EVEN.get(off, 0.0)
    return t.astype(ml_dtypes.bfloat16)


def split(x):
    hi = x.astype(BF16)
    return hi, (x - hi.astype(F32)).astype(BF16)


def kernel(
    state, volume, phase, matrices_in, speeds_in, targets_in, tiles_in, injection, courant, weight,
    table_in,
    out, drifted,
    matrices, speeds, targets, tiles, table, inj, cou, wei, cells, vol, dens, lhs, tt1, tt2,
    send0, send1, recv0, recv1, rad_send, rad_recv, cols, pay, hit_db, hit_bd, seg_t, buf, ra,
    part, rb, g0, g2,
    small_sem, load_sem, vol_sem, dens_sem, lon_s0, lon_r0, lon_s1, lon_r1, rad_s, rad_r,
    ra_s, ra_r, rb_s, rb_r, g2_s, g2_r,
):
    rad, lon = lax.axis_index("rad"), lax.axis_index("lon")
    right, left = lax.rem(lon + 1, NLON), lax.rem(lon + NLON - 1, NLON)
    me_yx = rad * (NYX // NRAD) + lax.div(lon, NZC)
    me_zc = lax.rem(lon, NZC)

    x_at, z_at, core_at = lax.div(lon, NZC), lax.rem(lax.div(lon, 2), 4), lax.rem(lon, 2)

    def yx_peer(k):
        y, x = lax.rem(rad + k // 4, NRAD), lax.rem(x_at + k % 4, NYX // NRAD)
        return y * (NYX // NRAD) + x, (y, x * NZC + me_zc)

    def zc_peer(k):
        core = 1 - core_at if k % 2 else core_at
        i = lax.rem(z_at + k // 2, 4) * 2 + core
        return i, (rad, x_at * NZC + i)

    def hops(n):
        return min(n, 4 - n)

    yx_order = sorted(range(1, NYX), key=lambda k: -hops(k // 4) - hops(k % 4))
    zc_order = sorted(range(1, NZC), key=lambda k: -2 * hops(k // 2) - k % 2)

    small = [
        pltpu.make_async_copy(src, dst, small_sem.at[i])
        for i, (src, dst) in enumerate((
            (matrices_in, matrices), (speeds_in, speeds), (table_in, table),
            (targets_in, targets), (tiles_in, tiles),
            (injection, inj), (courant, cou), (weight, wei),
        ))
    ]
    for copy in small:
        copy.start()

    def load(b):
        return pltpu.make_async_copy(
            state.at[:, pl.ds(b * RB, RB)], cells.at[:, pl.ds(3 + b * RB, RB)], load_sem.at[b]
        )

    for b in [0, 1, NB - 1] + list(range(2, NB - 1)):
        load(b).start()
    vol_copy = pltpu.make_async_copy(volume, vol, vol_sem)
    vol_copy.start()
    dens_copy = pltpu.make_async_copy(phase, dens, dens_sem)
    dens_copy.start()

    barrier = pltpu.get_barrier_semaphore()

    def greet(device):
        pl.semaphore_signal(barrier, inc=1, device_id=device, device_id_type=MESH)

    greet((rad, right))
    greet((rad, left))
    for k in yx_order:
        greet(yx_peer(k)[1])
    for k in zc_order:
        greet(zc_peer(k)[1])

    cells[:, 0:3] = jnp.zeros((NF, 3, CL, CZ), F32)
    cells[:, 3 + CR :] = jnp.zeros((NF, 3, CL, CZ), F32)

    for copy in small:
        copy.wait()
    lane = lax.broadcasted_iota(jnp.int32, (CL, 128), 1)
    sub = lax.broadcasted_iota(jnp.int32, (CL, 128), 0)
    block = lax.shift_right_logical(lane, 4)
    same_l = jnp.bitwise_and(lane, CL - 1) == sub
    odd, even = table[C_ODD : C_ODD + CL].astype(F32), table[C_EVEN : C_EVEN + CL].astype(F32)
    rows_l = []
    zero = jnp.zeros((CL, 128), BF16)
    for f in range(NF):
        row_r = jnp.zeros((CL, 128), F32)
        row_l = jnp.zeros((CL, 128), F32)
        for g in range(NF):
            row_r = jnp.where(block == g, matrices[0, f, g], row_r)
            row_l = jnp.where(block == g, matrices[1, f, g], row_l)
        rows_l.append(row_l)
        eye = lane == sub + f * CL
        w = (
            (SCALE * speeds[1]) * jnp.where(block == f, even, 0.0)
            - SCALE * row_l * odd
            + jnp.where(eye, 1.0 - 20.0 * SCALE * speeds[0], 0.0)
        )
        whi, wlo = split(w)
        rhi, rlo = split(jnp.where(same_l, (-45.0 * SCALE) * row_r, 0.0))
        at = {0: 0, 7: CL}.get(f, (f - 1) * CL)
        h, l, hr, lr = (H_07, L_07, HR_07, LR_07) if f in (0, 7) else (H_16, L_16, HR_16, LR_16)
        for start, high, low in ((h, whi, None), (l, wlo, zero), (hr, rhi, None), (lr, rlo, zero)):
            lhs[start + at : start + at + CL, 0:128] = high
            lhs[start + at : start + at + CL, 128:256] = high if low is None else low
    q = lax.broadcasted_iota(jnp.int32, (24, 128), 0)
    row_e = jnp.zeros((24, 128), F32)
    for pos, f in enumerate(ORDER):
        wide = jnp.concatenate([rows_l[f][0:8]] * 3, axis=0)
        row_e = jnp.where((q >= 3 * pos) & (q < 3 * pos + 3), wide, row_e)
    row_e = jnp.concatenate([row_e, row_e], axis=0)
    we = (SCALE * speeds[1]) * table[C_EEVEN : C_EEVEN + 48].astype(F32) - (
        SCALE * row_e * table[C_EODD : C_EODD + 48].astype(F32)
    )
    ehi, elo = split(we)
    lhs[H_EDGE : H_EDGE + 48, 0:128] = ehi
    lhs[H_EDGE : H_EDGE + 48, 128:256] = ehi
    lhs[L_EDGE : L_EDGE + 48, 0:128] = elo
    lhs[L_EDGE : L_EDGE + 48, 128:256] = jnp.zeros((48, 128), BF16)

    def row(i):
        return cells[:, i].reshape(NF * CL, CZ)

    def rad_edge(side):
        radial = jnp.concatenate(
            [lhs[HR_07:LR_07], lhs[HR_16:LR_16], lhs[LR_07:H_16], lhs[LR_16:M_END]], axis=0
        )
        for k in range(3):
            d = jnp.zeros((128, CZ), F32)
            e = jnp.zeros((128, CZ), F32)
            for j in range(3):
                off = j - k - 3 if side == 0 else 3 + j - k
                if off in ODD:
                    u = row(CR + j if side == 0 else 3 + j)
                    d = d + (ODD[off] / 45.0) * u
                    e = e + EVEN[off] * u
            y = jnp.dot(
                radial, jnp.concatenate(split(d), axis=0), preferred_element_type=F32
            )
            y = y[0:128] + y[128:256]
            for pos, f in enumerate(ORDER):
                rad_send[side, pos, k] = y[pos * CL : (pos + 1) * CL] + (
                    SCALE * speeds[0]
                ) * e[f * CL : (f + 1) * CL]

    rad_parts = ((0, 2), (2, 3), (5, 3))

    def rad_copy(side, part_of):
        fields = pl.ds(*rad_parts[part_of])
        return pltpu.make_async_remote_copy(
            src_ref=rad_send.at[side, fields],
            dst_ref=rad_recv.at[side, fields],
            send_sem=rad_s.at[side, part_of],
            recv_sem=rad_r.at[side, part_of],
            device_id=(rad + 1 if side == 0 else rad - 1, lon),
            device_id_type=MESH,
        )

    def send_rad(part_of):
        for side in range(2):
            @pl.when(has[side])
            def _():
                rad_copy(side, part_of).start()

    has = (rad < NRAD - 1, rad > 0)

    def lon_copy(side, part, b):
        src, dst = (send0, recv0) if part == 0 else (send1, recv1)
        ss, rs = (lon_s0, lon_r0) if part == 0 else (lon_s1, lon_r1)
        rows = pl.ds(b * (RB // 4), RB // 4)
        return pltpu.make_async_remote_copy(
            src_ref=src.at[side, rows],
            dst_ref=dst.at[side, rows],
            send_sem=ss.at[side, b],
            recv_sem=rs.at[side, b],
            device_id=(rad, right if side == 0 else left),
            device_id_type=MESH,
        )

    first_eight = lax.broadcasted_iota(jnp.int32, (8, CZ), 0)

    def pick(n, a, b):
        return jnp.where(first_eight < n, a, b)

    def lon_pass(b):
        tops = ([], [])
        for i in range(RB):
            r = b * RB + i
            t1 = jnp.concatenate(split(row(r + 3)), axis=0)
            tt1[r] = t1
            y = jnp.dot(lhs[H_07:HR_07], t1, preferred_element_type=F32)
            new = y[0:32] + y[32:64]
            out[0, r] = new[0:CL]
            out[7, r] = new[CL:]
            edge = y[64:112] + y[112:160]
            g, j = b * (RB // 4) + i // 4, i % 4
            for side in range(2):
                tops[side].append(edge[side * 24 : side * 24 + 8])
                send1[side, g, j * 16 : (j + 1) * 16] = edge[side * 24 + 8 : side * 24 + 24]
        for h in range(RB // 4):
            g = b * (RB // 4) + h
            for side in range(2):
                z0, z1, z2, z3 = tops[side][4 * h : 4 * h + 4]
                a, b1, c = (
                    pltpu.roll(z1, 6, axis=0), pltpu.roll(z2, 4, axis=0), pltpu.roll(z3, 2, axis=0)
                )
                send0[side, g, 0:8] = pick(6, z0, a)
                send0[side, g, 8:16] = pick(4, a, b1)
                send0[side, g, 16:24] = pick(2, b1, c)
                a, b1, c = (
                    pltpu.roll(z0, 2, axis=0), pltpu.roll(z1, 4, axis=0), pltpu.roll(z2, 6, axis=0)
                )
                send1[side, g, 64:72] = pick(2, a, pick(4, b1, pick(6, c, z3)))

    def rad_pass(b, _):
        for i in range(RB):
            r = b * RB + i
            m3, m2, m1, p1, p2, p3 = (row(r + n) for n in (0, 1, 2, 4, 5, 6))
            d = (p1 - m1) - 0.2 * ((p2 - m2) - (1.0 / 9.0) * (p3 - m3))
            m3, m2, m1, p1, p2, p3 = (
                jnp.concatenate([x[0:CL], x[112:128]], axis=0) for x in (m3, m2, m1, p1, p2, p3)
            )
            e = (p1 + m1) - 0.4 * ((p2 + m2) - (1.0 / 6.0) * (p3 + m3))
            t2 = jnp.concatenate(split(d), axis=0)
            tt2[r] = t2
            y = jnp.dot(lhs[HR_07:H_16], t2, preferred_element_type=F32)
            new = (y[0:32] + y[32:64]) + (15.0 * SCALE * speeds[0]) * e
            out[0, r] = out[0, r] + new[0:CL]
            out[7, r] = out[7, r] + new[CL:]
        return 0

    def second_pass(g, _):
        for i in range(4):
            r = 4 * g + i
            m3, m2, m1, p1, p2, p3 = (
                cells[1:7, r + n].reshape(96, CZ) for n in (0, 1, 2, 4, 5, 6)
            )
            e = (p1 + m1) - 0.4 * ((p2 + m2) - (1.0 / 6.0) * (p3 + m3))
            y1 = jnp.dot(lhs[H_16:HR_16], tt1[r], preferred_element_type=F32)
            y2 = jnp.dot(lhs[HR_16:M_END], tt2[r], preferred_element_type=F32)
            new = (y1[0:96] + y1[96:192] + y2[0:96] + y2[96:192]) + (
                15.0 * SCALE * speeds[0]
            ) * e
            out[1:7, r] = new.reshape(6, CL, CZ)
        return 0

    def send_early(b):
        lon_copy(0, 0, b).start()
        lon_copy(1, 0, b).start()

    def send_late(b, _):
        lon_copy(0, 1, b).start()
        lon_copy(1, 1, b).start()
        return 0

    load(0).wait()
    lon_pass(0)
    pl.semaphore_wait(barrier, 2 + NYX - 1 + NZC - 1)
    send_early(0)
    load(1).wait()
    lon_pass(1)
    send_early(1)
    load(NB - 1).wait()
    rad_edge(0)
    rad_edge(1)
    send_rad(0)
    send_rad(1)

    def rest(b, _):
        @pl.when(b < NB - 1)
        def _():
            load(b).wait()

        lon_pass(b)
        send_early(b)
        return 0

    lax.fori_loop(2, NB, rest, 0)
    lax.fori_loop(SENDS[0], SENDS[1], send_late, 0)
    tile_col = jnp.broadcast_to(tiles[...].astype(F32), (DEVICES, DEVICES)).T
    target_row = jnp.broadcast_to(targets[...].astype(F32), (DEVICES, CR))
    hit = (tile_col[:, 0:CR] == target_row).astype(BF16)
    spread = lax.shift_right_logical(
        lax.broadcasted_iota(jnp.int32, (CR, CR * 8), 1), 3
    ) == lax.broadcasted_iota(jnp.int32, (CR, CR * 8), 0)
    hit_db[...] = jnp.dot(
        hit, spread.astype(F32).astype(BF16), preferred_element_type=F32
    ).astype(BF16)
    target_col = jnp.concatenate(
        [target_row, jnp.zeros((DEVICES, DEVICES - CR), F32)], axis=1
    ).T
    hit_bd[...] = (target_col[0:CR] == tiles[...].astype(F32)).astype(F32).astype(BF16)

    seg_t[...] = (
        jnp.bitwise_and(lax.broadcasted_iota(jnp.int32, (2 * TP, CZ), 0), ZSEG - 1)
        == lax.shift_right_logical(lax.broadcasted_iota(jnp.int32, (2 * TP, CZ), 1), 5)
    ).astype(F32).astype(BF16)

    lax.fori_loop(0, NB, rad_pass, 0)

    def add_rad(part_of):
        for side in range(2):
            @pl.when(has[1 - side])
            def _():
                rad_copy(side, part_of).wait_recv()
                for pos in range(rad_parts[part_of][0], sum(rad_parts[part_of])):
                    for k in range(3):
                        r = k if side == 0 else CR - 3 + k
                        out[ORDER[pos], r] = out[ORDER[pos], r] + rad_recv[side, pos, k]

    add_rad(0)
    vol_copy.wait()
    seg = table[C_SEG : C_SEG + CZ]
    mask = table[C_MASK : C_MASK + CL].astype(F32)

    def early(b, _):
        for i in range(2):
            lon_copy(0, 0, 2 * b + i).wait_recv()
            lon_copy(1, 0, 2 * b + i).wait_recv()
        highs, lows = [], []
        for h in range(4):
            g = b * 4 + h
            got = jnp.concatenate(
                [recv0[0, g], recv0[1, g], jnp.zeros((16, CZ), F32)], axis=0
            )
            add = jnp.dot(
                table[C_FIX07 : C_FIX07 + 128],
                jnp.concatenate(split(got), axis=0),
                preferred_element_type=F32,
            )
            v = vol[pl.ds(4 * g, 4)].reshape(64, CZ)
            for c, f in enumerate((0, 7)):
                new = out[f, pl.ds(4 * g, 4)].reshape(64, CZ) + add[c * 64 : (c + 1) * 64]
                out[f, pl.ds(4 * g, 4)] = new.reshape(4, CL, CZ)
                yh, yl = split(v * new)
                highs.append(yh)
                lows.append(yl)
        t = jnp.dot(jnp.concatenate(highs + lows, axis=0), seg, preferred_element_type=F32)
        t = t[0:512] + t[512:1024]
        for h in range(4):
            for c in range(2):
                at = (h * 2 + c) * 64
                x = t[at : at + 64].reshape(4, CL, TP) * mask[None]
                pay[pl.ds(b * 128 + h * 32, 32), c * TP : (c + 1) * TP] = (
                    x[:, 0:8] + x[:, 8:16]
                ).reshape(32, TP)
        return 0

    lax.fori_loop(0, NB // 2, early, 0)

    pay_hi, pay_lo = split(pay[...])
    buf[...] = (
        jnp.dot(hit_db[...], pay_hi, preferred_element_type=F32)
        + jnp.dot(hit_db[...], pay_lo, preferred_element_type=F32)
    ).reshape(NYX, NZC, 2 * TP)

    def ra_copy(k):
        a, device = yx_peer(k)
        return pltpu.make_async_remote_copy(
            src_ref=buf.at[a], dst_ref=ra.at[k], send_sem=ra_s.at[k], recv_sem=ra_r.at[k],
            device_id=device, device_id_type=MESH,
        )

    def rb_copy(k):
        i, device = zc_peer(k)
        return pltpu.make_async_remote_copy(
            src_ref=part, dst_ref=rb.at[me_zc], send_sem=rb_s.at[k], recv_sem=rb_r.at[k],
            device_id=device, device_id_type=MESH,
        )

    def g2_copy(k):
        a, device = yx_peer(k)
        return pltpu.make_async_remote_copy(
            src_ref=g0, dst_ref=g2.at[me_yx], send_sem=g2_s.at[k], recv_sem=g2_r.at[k],
            device_id=device, device_id_type=MESH,
        )

    def late(b, _):
        lon_copy(0, 1, b).wait_recv()
        lon_copy(1, 1, b).wait_recv()

        def late_row(i, _):
            r = b * RB + i
            got = jnp.concatenate(
                [recv0[0, r], recv1[0, r], recv0[1, r], recv1[1, r], jnp.zeros((16, CZ), F32)],
                axis=0,
            )
            hi, lo = split(got)
            add = jnp.dot(
                table[C_FIX : C_FIX + 96],
                jnp.concatenate([hi, lo], axis=0),
                preferred_element_type=F32,
            )
            out[1:7, r] = out[1:7, r] + add.reshape(6, CL, CZ)
            return 0

        lax.fori_loop(0, RB, late_row, 0, unroll=8)
        return 0

    def late(b, _):
        lon_copy(0, 1, b).wait_recv()
        lon_copy(1, 1, b).wait_recv()
        for h in range(RB // 4):
            g = b * (RB // 4) + h
            tail = [recv1[0, g, 64:72], recv1[1, g, 64:72], jnp.zeros((16, CZ), F32)]
            for i in range(4):
                got = jnp.concatenate(
                    [recv1[side, g, i * 16 : (i + 1) * 16] for side in range(2)] + tail, axis=0
                )
                add = jnp.dot(
                    table[C_FIX + i * 96 : C_FIX + (i + 1) * 96],
                    jnp.concatenate(split(got), axis=0),
                    preferred_element_type=F32,
                )
                r = 4 * g + i
                out[1:7, r] = out[1:7, r] + add.reshape(6, CL, CZ)
        return 0

    for k in yx_order:
        ra_copy(k).start()
    lax.fori_loop(SENDS[1], SENDS[2], send_late, 0)
    send_rad(2)

    lax.fori_loop(0, PASS[0], second_pass, 0)
    cols[...] = jnp.zeros((8, 256), F32)
    cols[0:2, 0:CH] = inj[...]
    cols[2:3, 0:CH] = cou[...]
    cols[3:4, 0:CH] = wei[...]
    columns = cols[...].T
    channel_rate = jnp.broadcast_to(columns[0:CH, 2:3], (CH, TP))
    channel_weight = jnp.broadcast_to(columns[0:CH, 3:4], (CH, TP))

    def drift(density):
        for _ in range(DRIFT):
            density = density - channel_rate * (density - pltpu.roll(density, 1, axis=1))
        return density

    dens_copy.wait()
    bare = jnp.sum(channel_weight * drift(dens[...]), axis=0, keepdims=True)

    rate_row, weight_row = cols[2:3], cols[3:4]
    keep = 1.0 - rate_row
    powers = (
        keep * keep * keep,
        3.0 * keep * keep * rate_row,
        3.0 * keep * rate_row * rate_row,
        rate_row * rate_row * rate_row,
    )
    taps = [
        [
            jnp.sum(0.5 * weight_row * cols[i : i + 1] * power, axis=1, keepdims=True)
            for power in powers
        ]
        for i in range(2)
    ]

    total = buf[me_yx]
    for k in range(1, NYX):
        ra_copy(k).wait_recv()
        total = total + ra[k]
    part[:, 0 : 2 * TP] = total
    part[:, 2 * TP :] = jnp.broadcast_to(bare, (NZC, TP))
    for k in zc_order:
        rb_copy(k).start()
    lax.fori_loop(SENDS[2], SENDS[3], send_late, 0)
    lax.fori_loop(PASS[0], CR // 4, second_pass, 0)
    add_rad(1)
    lax.fori_loop(0, LATE[0], late, 0)
    rb[me_zc] = part[...]
    for k in range(1, NZC):
        rb_copy(k).wait_recv()
    source = rb[0, :, 0 : 2 * TP]
    for j in range(1, NZC):
        source = source + rb[j, :, 0 : 2 * TP]
    tile_row = lax.broadcasted_iota(jnp.int32, (NZC, TP), 0)
    pressure = jnp.zeros((NZC, TP), F32)
    for j in range(NZC):
        pressure = jnp.where(tile_row == j, rb[j, :, 2 * TP :], pressure)
    for i in range(2):
        s = source[:, i * TP : (i + 1) * TP]
        for n in range(4):
            pressure = pressure + taps[i][n] * (pltpu.roll(s, n, axis=1) if n else s)
    g0[...] = pressure
    for k in yx_order:
        g2_copy(k).start()
    lax.fori_loop(SENDS[3], SENDS[4], send_late, 0)
    g2[me_yx] = pressure

    own = lax.broadcasted_iota(jnp.int32, (NZC, 2 * TP), 0) == me_zc
    mine = jnp.sum(jnp.where(own, source, 0.0), axis=0, keepdims=True)
    drifted[...] = drift(
        dens[...]
        + 0.5 * (columns[0:CH, 0:1] * mine[:, 0:TP] + columns[0:CH, 1:2] * mine[:, TP:])
    )
    add_rad(2)
    lax.fori_loop(LATE[0], LATE[1], late, 0)

    for k in range(1, NYX):
        g2_copy(k).wait_recv()
    back_hi, back_lo = split(g2[...].reshape(DEVICES, TP))
    pay[0:CR, 0:TP] = jnp.dot(hit_bd[...], back_hi, preferred_element_type=F32) + jnp.dot(
        hit_bd[...], back_lo, preferred_element_type=F32
    )

    def nudge(b, _):
        got = pay[pl.ds(b * 16, 16), 0:TP]
        wide = jnp.broadcast_to(got[:, None, :], (16, CL, TP)) * mask[None]
        back = jnp.dot(
            jnp.concatenate(split(wide.reshape(16 * CL, TP)), axis=1),
            seg_t[...],
            preferred_element_type=F32,
        )
        old = out[7, pl.ds(b * 16, 16)].reshape(16 * CL, CZ)
        out[7, pl.ds(b * 16, 16)] = (old + 0.5 * (back - old)).reshape(16, CL, CZ)
        return 0

    lax.fori_loop(0, CR // 16, nudge, 0, unroll=2)
    lax.fori_loop(LATE[1], NB, late, 0)

    def sent(b, _):
        for side in range(2):
            for part in range(2):
                lon_copy(side, part, b).wait_send()
        return 0

    lax.fori_loop(0, NB, sent, 0)
    for side in range(2):
        @pl.when(has[side])
        def _():
            for part_of in range(3):
                rad_copy(side, part_of).wait_send()
    for k in range(1, NYX):
        ra_copy(k).wait_send()
        g2_copy(k).wait_send()
    for k in range(1, NZC):
        rb_copy(k).wait_send()


def finish(fields, density, fields_out, density_out, sem):
    copies = [
        pltpu.make_async_copy(fields.at[f], fields_out.at[f], sem.at[f]) for f in range(NF)
    ] + [pltpu.make_async_copy(density, density_out, sem.at[NF])]
    for copy in copies:
        copy.start()
    for copy in copies:
        copy.wait()


def per_device(
    state, flux_matrices, wave_speed, flux_volume, block_tile, tile_of_device,
    phase_density, injection, drift_courant, energy_weight,
):
    hbm = pl.BlockSpec(memory_space=pltpu.HBM)
    vmem = pl.BlockSpec(memory_space=pltpu.VMEM)
    dma = pltpu.SemaphoreType.DMA
    coupled, drifted = pl.pallas_call(
        kernel,
        out_shape=(
            pltpu.VMEM((NF, CR, CL, CZ), F32),
            pltpu.VMEM((CH, TP), F32),
        ),
        in_specs=[hbm] * 11,
        out_specs=(vmem, vmem),
        scratch_shapes=[
            pltpu.SMEM((2, NF, NF), F32),
            pltpu.SMEM((2,), F32),
            pltpu.VMEM((1, CR), jnp.int32),
            pltpu.VMEM((1, DEVICES), jnp.int32),
            pltpu.VMEM((C_END, 128), BF16),
            pltpu.VMEM((2, CH), F32),
            pltpu.VMEM((1, CH), F32),
            pltpu.VMEM((1, CH), F32),
            pltpu.VMEM((NF, CR + 6, CL, CZ), F32),
            pltpu.VMEM((CR, CL, CZ), F32),
            pltpu.VMEM((CH, TP), F32),
            pltpu.VMEM((M_END, 256), BF16),
            pltpu.VMEM((CR, 256, CZ), BF16),
            pltpu.VMEM((CR, 256, CZ), BF16),
            pltpu.VMEM((2, CR // 4, 24, CZ), F32),
            pltpu.VMEM((2, CR // 4, 72, CZ), F32),
            pltpu.VMEM((2, CR // 4, 24, CZ), F32),
            pltpu.VMEM((2, CR // 4, 72, CZ), F32),
            pltpu.VMEM((2, NF, 3, CL, CZ), F32),
            pltpu.VMEM((2, NF, 3, CL, CZ), F32),
            pltpu.VMEM((8, 256), F32),
            pltpu.VMEM((CR * 8, 2 * TP), F32),
            pltpu.VMEM((DEVICES, CR * 8), BF16),
            pltpu.VMEM((CR, DEVICES), BF16),
            pltpu.VMEM((2 * TP, CZ), BF16),
            pltpu.VMEM((NYX, NZC, 2 * TP), F32),
            pltpu.VMEM((NYX, NZC, 2 * TP), F32),
            pltpu.VMEM((NZC, 3 * TP), F32),
            pltpu.VMEM((NZC, NZC, 3 * TP), F32),
            pltpu.VMEM((NZC, TP), F32),
            pltpu.VMEM((NYX, NZC, TP), F32),
            dma((8,)), dma((NB,)), dma, dma,
            dma((2, NB)), dma((2, NB)), dma((2, NB)), dma((2, NB)),
            dma((2, 3)), dma((2, 3)), dma((NYX,)), dma((NYX,)),
            dma((NZC,)), dma((NZC,)), dma((NYX,)), dma((NYX,)),
        ],
        compiler_params=pltpu.CompilerParams(
            collective_id=0, has_side_effects=True, vmem_limit_bytes=54 << 20
        ),
    )(
        state,
        flux_volume,
        phase_density.reshape(CH, TP),
        flux_matrices,
        wave_speed,
        block_tile.reshape(1, CR),
        tile_of_device.reshape(1, DEVICES),
        injection,
        drift_courant.reshape(1, CH),
        energy_weight.reshape(1, CH),
        jnp.asarray(constants()),
    )
    coupled, drifted = pl.pallas_call(
        finish,
        out_shape=(
            jax.ShapeDtypeStruct((NF, CR, CL, CZ), F32),
            jax.ShapeDtypeStruct((CH, TP), F32),
        ),
        in_specs=[vmem, vmem],
        out_specs=(hbm, hbm),
        scratch_shapes=[dma((NF + 1,))],
        compiler_params=pltpu.CompilerParams(vmem_limit_bytes=1 << 20),
    )(coupled, drifted)
    return coupled, drifted[None]


def solution(mesh):
    in_specs = (
        P(None, "rad", "lon", None),
        P(),
        P(),
        P("rad", "lon", None),
        P("lon", "rad", None),
        P(),
        P(("rad", "lon"), None, None),
        P(),
        P(),
        P(),
    )
    out_specs = (P(None, "rad", "lon", None), P(("rad", "lon"), None, None))
    return jax.shard_map(
        per_device, mesh=mesh, in_specs=in_specs, out_specs=out_specs, check_vma=False
    )
```

```python
import numpy as np

import jax
import jax.numpy as jnp
import ml_dtypes
from jax import lax
from jax.experimental import pallas as pl
from jax.experimental.pallas import tpu as pltpu
from jax.sharding import PartitionSpec as P

F32 = jnp.float32
BF16 = jnp.bfloat16
HIGHEST = lax.Precision.HIGHEST
MESH = pl.DeviceIdType.MESH

NF, CR, CL, CZ = 8, 64, 16, 256
ZSEG = 8
DRIFT = 3
CH, TP = 200, 128
NRAD, NLON = 4, 32
NYX, NZC = 16, 8
DEVICES = NRAD * NLON

SCALE = 0.4 * 0.5 / 30.0
ORDER = (0, 7, 1, 2, 3, 4, 5, 6)
ODD = {-3: -1.0, -2: 9.0, -1: -45.0, 1: 45.0, 2: -9.0, 3: 1.0}
EVEN = {-3: 1.0, -2: -6.0, -1: 15.0, 0: -20.0, 1: 15.0, 2: -6.0, 3: 1.0}

RB = 8
NB = CR // RB
SENDS = (0, 4, 6, 6, NB)
PASS = (10,)
LATE = (4, 7)

C_FIX07, C_FIX, C_SEG, C_MASK, C_ODD, C_EVEN, C_EODD, C_EEVEN, C_END = (
    0, 128, 512, 768, 784, 800, 816, 864, 912
)
H_07, L_07, H_EDGE, L_EDGE, HR_07, LR_07, H_16, L_16, HR_16, LR_16, M_END = (
    0, 32, 64, 112, 160, 192, 224, 320, 416, 512, 608
)


def constants():
    t = np.zeros((C_END, 128), np.float32)
    half = 64
    for c in range(2):
        for r in range(4):
            for l in range(CL):
                row = C_FIX07 + (c * 4 + r) * CL + l
                for h in range(2):
                    if l < 3:
                        t[row, h * half + r * 6 + 3 * c + l] = 1
                    if l >= CL - 3:
                        t[row, h * half + 24 + r * 6 + 3 * c + l - (CL - 3)] = 1
    for r in range(4):
        for pos in range(2, NF):
            for l in range(CL):
                row = C_FIX + r * 96 + (pos - 2) * CL + l
                side = 0 if l < 3 else 1
                k = l if l < 3 else l - (CL - 3)
                if 0 <= k < 3:
                    q = 3 * pos + k
                    at = side * 16 + q - 8 if q >= 8 else 32 + side * 8 + r * 2 + q - 6
                    for h in range(2):
                        t[row, h * half + at] = 1
    for z in range(CZ):
        for p in range(TP):
            t[C_SEG + z, p] = z // (CZ // ZSEG) == p % ZSEG
    for l in range(CL):
        for p in range(TP):
            t[C_MASK + l, p] = p // ZSEG == l
    for l in range(CL):
        for f in range(NF):
            for j in range(CL):
                t[C_ODD + l, f * CL + j] = ODD.get(j - l, 0.0)
                t[C_EVEN + l, f * CL + j] = EVEN.get(j - l, 0.0)
    for side in range(2):
        for pos in range(NF):
            for k in range(3):
                row = side * 24 + 3 * pos + k
                for f in range(NF):
                    for j in range(CL):
                        off = j - CL - k if side == 0 else 3 + j - k
                        t[C_EODD + row, f * CL + j] = ODD.get(off, 0.0)
                        if f == ORDER[pos]:
                            t[C_EEVEN + row, f * CL + j] = EVEN.get(off, 0.0)
    return t.astype(ml_dtypes.bfloat16)


def split(x):
    hi = x.astype(BF16)
    return hi, (x - hi.astype(F32)).astype(BF16)


def kernel(
    state, volume, phase, matrices_in, speeds_in, targets_in, tiles_in, injection, courant, weight,
    table_in,
    out, drifted,
    matrices, speeds, targets, tiles, table, inj, cou, wei, cells, vol, dens, lhs, tt1, tt2,
    send0, send1, recv0, recv1, rad_send, rad_recv, cols, pay, hit_db, hit_bd, seg_t, buf, ra,
    part, rb, g0, g2,
    small_sem, load_sem, vol_sem, dens_sem, lon_s0, lon_r0, lon_s1, lon_r1, rad_s, rad_r,
    ra_s, ra_r, rb_s, rb_r, g2_s, g2_r,
):
    rad, lon = lax.axis_index("rad"), lax.axis_index("lon")
    right, left = lax.rem(lon + 1, NLON), lax.rem(lon + NLON - 1, NLON)
    me_yx = rad * (NYX // NRAD) + lax.div(lon, NZC)
    me_zc = lax.rem(lon, NZC)

    x_at, z_at, core_at = lax.div(lon, NZC), lax.rem(lax.div(lon, 2), 4), lax.rem(lon, 2)

    def yx_peer(k):
        y, x = lax.rem(rad + k // 4, NRAD), lax.rem(x_at + k % 4, NYX // NRAD)
        return y * (NYX // NRAD) + x, (y, x * NZC + me_zc)

    def zc_peer(k):
        core = 1 - core_at if k % 2 else core_at
        i = lax.rem(z_at + k // 2, 4) * 2 + core
        return i, (rad, x_at * NZC + i)

    def hops(n):
        return min(n, 4 - n)

    yx_order = sorted(range(1, NYX), key=lambda k: -hops(k // 4) - hops(k % 4))
    zc_order = sorted(range(1, NZC), key=lambda k: -2 * hops(k // 2) - k % 2)

    small = [
        pltpu.make_async_copy(src, dst, small_sem.at[i])
        for i, (src, dst) in enumerate((
            (matrices_in, matrices), (speeds_in, speeds), (table_in, table),
            (targets_in, targets), (tiles_in, tiles),
            (injection, inj), (courant, cou), (weight, wei),
        ))
    ]
    for copy in small:
        copy.start()

    def load(b):
        return pltpu.make_async_copy(
            state.at[:, pl.ds(b * RB, RB)], cells.at[:, pl.ds(3 + b * RB, RB)], load_sem.at[b]
        )

    for b in [0, 1, NB - 1] + list(range(2, NB - 1)):
        load(b).start()
    vol_copy = pltpu.make_async_copy(volume, vol, vol_sem)
    vol_copy.start()
    dens_copy = pltpu.make_async_copy(phase, dens, dens_sem)
    dens_copy.start()

    barrier = pltpu.get_barrier_semaphore()

    def greet(device):
        pl.semaphore_signal(barrier, inc=1, device_id=device, device_id_type=MESH)

    greet((rad, right))
    greet((rad, left))
    for k in yx_order:
        greet(yx_peer(k)[1])
    for k in zc_order:
        greet(zc_peer(k)[1])

    cells[:, 0:3] = jnp.zeros((NF, 3, CL, CZ), F32)
    cells[:, 3 + CR :] = jnp.zeros((NF, 3, CL, CZ), F32)

    for copy in small:
        copy.wait()
    lane = lax.broadcasted_iota(jnp.int32, (CL, 128), 1)
    sub = lax.broadcasted_iota(jnp.int32, (CL, 128), 0)
    block = lax.shift_right_logical(lane, 4)
    same_l = jnp.bitwise_and(lane, CL - 1) == sub
    odd, even = table[C_ODD : C_ODD + CL].astype(F32), table[C_EVEN : C_EVEN + CL].astype(F32)
    rows_l = []
    zero = jnp.zeros((CL, 128), BF16)
    for f in range(NF):
        row_r = jnp.zeros((CL, 128), F32)
        row_l = jnp.zeros((CL, 128), F32)
        for g in range(NF):
            row_r = jnp.where(block == g, matrices[0, f, g], row_r)
            row_l = jnp.where(block == g, matrices[1, f, g], row_l)
        rows_l.append(row_l)
        eye = lane == sub + f * CL
        w = (
            (SCALE * speeds[1]) * jnp.where(block == f, even, 0.0)
            - SCALE * row_l * odd
            + jnp.where(eye, 1.0 - 20.0 * SCALE * speeds[0], 0.0)
        )
        whi, wlo = split(w)
        rhi, rlo = split(jnp.where(same_l, (-45.0 * SCALE) * row_r, 0.0))
        at = {0: 0, 7: CL}.get(f, (f - 1) * CL)
        h, l, hr, lr = (H_07, L_07, HR_07, LR_07) if f in (0, 7) else (H_16, L_16, HR_16, LR_16)
        for start, high, low in ((h, whi, None), (l, wlo, zero), (hr, rhi, None), (lr, rlo, zero)):
            lhs[start + at : start + at + CL, 0:128] = high
            lhs[start + at : start + at + CL, 128:256] = high if low is None else low
    q = lax.broadcasted_iota(jnp.int32, (24, 128), 0)
    row_e = jnp.zeros((24, 128), F32)
    for pos, f in enumerate(ORDER):
        wide = jnp.concatenate([rows_l[f][0:8]] * 3, axis=0)
        row_e = jnp.where((q >= 3 * pos) & (q < 3 * pos + 3), wide, row_e)
    row_e = jnp.concatenate([row_e, row_e], axis=0)
    we = (SCALE * speeds[1]) * table[C_EEVEN : C_EEVEN + 48].astype(F32) - (
        SCALE * row_e * table[C_EODD : C_EODD + 48].astype(F32)
    )
    ehi, elo = split(we)
    lhs[H_EDGE : H_EDGE + 48, 0:128] = ehi
    lhs[H_EDGE : H_EDGE + 48, 128:256] = ehi
    lhs[L_EDGE : L_EDGE + 48, 0:128] = elo
    lhs[L_EDGE : L_EDGE + 48, 128:256] = jnp.zeros((48, 128), BF16)

    def row(i):
        return cells[:, i].reshape(NF * CL, CZ)

    def rad_edge(side):
        radial = jnp.concatenate(
            [lhs[HR_07:LR_07], lhs[HR_16:LR_16], lhs[LR_07:H_16], lhs[LR_16:M_END]], axis=0
        )
        for k in range(3):
            d = jnp.zeros((128, CZ), F32)
            e = jnp.zeros((128, CZ), F32)
            for j in range(3):
                off = j - k - 3 if side == 0 else 3 + j - k
                if off in ODD:
                    u = row(CR + j if side == 0 else 3 + j)
                    d = d + (ODD[off] / 45.0) * u
                    e = e + EVEN[off] * u
            y = jnp.dot(
                radial, jnp.concatenate(split(d), axis=0), preferred_element_type=F32
            )
            y = y[0:128] + y[128:256]
            for pos, f in enumerate(ORDER):
                rad_send[side, pos, k] = y[pos * CL : (pos + 1) * CL] + (
                    SCALE * speeds[0]
                ) * e[f * CL : (f + 1) * CL]

    rad_parts = ((0, 2), (2, 3), (5, 3))

    def rad_copy(side, part_of):
        fields = pl.ds(*rad_parts[part_of])
        return pltpu.make_async_remote_copy(
            src_ref=rad_send.at[side, fields],
            dst_ref=rad_recv.at[side, fields],
            send_sem=rad_s.at[side, part_of],
            recv_sem=rad_r.at[side, part_of],
            device_id=(rad + 1 if side == 0 else rad - 1, lon),
            device_id_type=MESH,
        )

    def send_rad(part_of):
        for side in range(2):
            @pl.when(has[side])
            def _():
                rad_copy(side, part_of).start()

    has = (rad < NRAD - 1, rad > 0)

    def lon_copy(side, part, b):
        src, dst = (send0, recv0) if part == 0 else (send1, recv1)
        ss, rs = (lon_s0, lon_r0) if part == 0 else (lon_s1, lon_r1)
        rows = pl.ds(b * (RB // 4), RB // 4)
        return pltpu.make_async_remote_copy(
            src_ref=src.at[side, rows],
            dst_ref=dst.at[side, rows],
            send_sem=ss.at[side, b],
            recv_sem=rs.at[side, b],
            device_id=(rad, right if side == 0 else left),
            device_id_type=MESH,
        )

    first_eight = lax.broadcasted_iota(jnp.int32, (8, CZ), 0)

    def pick(n, a, b):
        return jnp.where(first_eight < n, a, b)

    def lon_pass(b):
        tops = ([], [])
        for i in range(RB):
            r = b * RB + i
            t1 = jnp.concatenate(split(row(r + 3)), axis=0)
            tt1[r] = t1
            y = jnp.dot(lhs[H_07:HR_07], t1, preferred_element_type=F32)
            new = y[0:32] + y[32:64]
            out[0, r] = new[0:CL]
            out[7, r] = new[CL:]
            edge = y[64:112] + y[112:160]
            g, j = b * (RB // 4) + i // 4, i % 4
            for side in range(2):
                tops[side].append(edge[side * 24 : side * 24 + 8])
                send1[side, g, j * 16 : (j + 1) * 16] = edge[side * 24 + 8 : side * 24 + 24]
        for h in range(RB // 4):
            g = b * (RB // 4) + h
            for side in range(2):
                z0, z1, z2, z3 = tops[side][4 * h : 4 * h + 4]
                a, b1, c = (
                    pltpu.roll(z1, 6, axis=0), pltpu.roll(z2, 4, axis=0), pltpu.roll(z3, 2, axis=0)
                )
                send0[side, g, 0:8] = pick(6, z0, a)
                send0[side, g, 8:16] = pick(4, a, b1)
                send0[side, g, 16:24] = pick(2, b1, c)
                a, b1, c = (
                    pltpu.roll(z0, 2, axis=0), pltpu.roll(z1, 4, axis=0), pltpu.roll(z2, 6, axis=0)
                )
                send1[side, g, 64:72] = pick(2, a, pick(4, b1, pick(6, c, z3)))

    def rad_pass(b, _):
        for i in range(RB):
            r = b * RB + i
            m3, m2, m1, p1, p2, p3 = (row(r + n) for n in (0, 1, 2, 4, 5, 6))
            d = (p1 - m1) - 0.2 * ((p2 - m2) - (1.0 / 9.0) * (p3 - m3))
            m3, m2, m1, p1, p2, p3 = (
                jnp.concatenate([x[0:CL], x[112:128]], axis=0) for x in (m3, m2, m1, p1, p2, p3)
            )
            e = (p1 + m1) - 0.4 * ((p2 + m2) - (1.0 / 6.0) * (p3 + m3))
            t2 = jnp.concatenate(split(d), axis=0)
            tt2[r] = t2
            y = jnp.dot(lhs[HR_07:H_16], t2, preferred_element_type=F32)
            new = (y[0:32] + y[32:64]) + (15.0 * SCALE * speeds[0]) * e
            out[0, r] = out[0, r] + new[0:CL]
            out[7, r] = out[7, r] + new[CL:]
        return 0

    def second_pass(g, _):
        for i in range(4):
            r = 4 * g + i
            m3, m2, m1, p1, p2, p3 = (
                cells[1:7, r + n].reshape(96, CZ) for n in (0, 1, 2, 4, 5, 6)
            )
            e = (p1 + m1) - 0.4 * ((p2 + m2) - (1.0 / 6.0) * (p3 + m3))
            y1 = jnp.dot(lhs[H_16:HR_16], tt1[r], preferred_element_type=F32)
            y2 = jnp.dot(lhs[HR_16:M_END], tt2[r], preferred_element_type=F32)
            new = (y1[0:96] + y1[96:192] + y2[0:96] + y2[96:192]) + (
                15.0 * SCALE * speeds[0]
            ) * e
            out[1:7, r] = new.reshape(6, CL, CZ)
        return 0

    def send_early(b):
        lon_copy(0, 0, b).start()
        lon_copy(1, 0, b).start()

    def send_late(b, _):
        lon_copy(0, 1, b).start()
        lon_copy(1, 1, b).start()
        return 0

    load(0).wait()
    lon_pass(0)
    pl.semaphore_wait(barrier, 2 + NYX - 1 + NZC - 1)
    send_early(0)
    load(1).wait()
    lon_pass(1)
    send_early(1)
    load(NB - 1).wait()
    rad_edge(0)
    rad_edge(1)
    send_rad(0)
    send_rad(1)

    def rest(b, _):
        @pl.when(b < NB - 1)
        def _():
            load(b).wait()

        lon_pass(b)
        send_early(b)
        return 0

    lax.fori_loop(2, NB, rest, 0)
    lax.fori_loop(SENDS[0], SENDS[1], send_late, 0)
    tile_col = jnp.broadcast_to(tiles[...].astype(F32), (DEVICES, DEVICES)).T
    target_row = jnp.broadcast_to(targets[...].astype(F32), (DEVICES, CR))
    hit = (tile_col[:, 0:CR] == target_row).astype(BF16)
    spread = lax.shift_right_logical(
        lax.broadcasted_iota(jnp.int32, (CR, CR * 8), 1), 3
    ) == lax.broadcasted_iota(jnp.int32, (CR, CR * 8), 0)
    hit_db[...] = jnp.dot(
        hit, spread.astype(F32).astype(BF16), preferred_element_type=F32
    ).astype(BF16)
    target_col = jnp.concatenate(
        [target_row, jnp.zeros((DEVICES, DEVICES - CR), F32)], axis=1
    ).T
    hit_bd[...] = (target_col[0:CR] == tiles[...].astype(F32)).astype(F32).astype(BF16)

    seg_t[...] = (
        jnp.bitwise_and(lax.broadcasted_iota(jnp.int32, (2 * TP, CZ), 0), ZSEG - 1)
        == lax.shift_right_logical(lax.broadcasted_iota(jnp.int32, (2 * TP, CZ), 1), 5)
    ).astype(F32).astype(BF16)

    lax.fori_loop(0, NB, rad_pass, 0)

    def add_rad(part_of):
        for side in range(2):
            @pl.when(has[1 - side])
            def _():
                rad_copy(side, part_of).wait_recv()
                for pos in range(rad_parts[part_of][0], sum(rad_parts[part_of])):
                    for k in range(3):
                        r = k if side == 0 else CR - 3 + k
                        out[ORDER[pos], r] = out[ORDER[pos], r] + rad_recv[side, pos, k]

    add_rad(0)
    vol_copy.wait()
    seg = table[C_SEG : C_SEG + CZ]
    mask = table[C_MASK : C_MASK + CL].astype(F32)

    def early(b, _):
        for i in range(2):
            lon_copy(0, 0, 2 * b + i).wait_recv()
            lon_copy(1, 0, 2 * b + i).wait_recv()
        highs, lows = [], []
        for h in range(4):
            g = b * 4 + h
            got = jnp.concatenate(
                [recv0[0, g], recv0[1, g], jnp.zeros((16, CZ), F32)], axis=0
            )
            add = jnp.dot(
                table[C_FIX07 : C_FIX07 + 128],
                jnp.concatenate(split(got), axis=0),
                preferred_element_type=F32,
            )
            v = vol[pl.ds(4 * g, 4)].reshape(64, CZ)
            for c, f in enumerate((0, 7)):
                new = out[f, pl.ds(4 * g, 4)].reshape(64, CZ) + add[c * 64 : (c + 1) * 64]
                out[f, pl.ds(4 * g, 4)] = new.reshape(4, CL, CZ)
                yh, yl = split(v * new)
                highs.append(yh)
                lows.append(yl)
        t = jnp.dot(jnp.concatenate(highs + lows, axis=0), seg, preferred_element_type=F32)
        t = t[0:512] + t[512:1024]
        for h in range(4):
            for c in range(2):
                at = (h * 2 + c) * 64
                x = t[at : at + 64].reshape(4, CL, TP) * mask[None]
                pay[pl.ds(b * 128 + h * 32, 32), c * TP : (c + 1) * TP] = (
                    x[:, 0:8] + x[:, 8:16]
                ).reshape(32, TP)
        return 0

    lax.fori_loop(0, NB // 2, early, 0)

    pay_hi, pay_lo = split(pay[...])
    buf[...] = (
        jnp.dot(hit_db[...], pay_hi, preferred_element_type=F32)
        + jnp.dot(hit_db[...], pay_lo, preferred_element_type=F32)
    ).reshape(NYX, NZC, 2 * TP)

    def ra_copy(k):
        a, device = yx_peer(k)
        return pltpu.make_async_remote_copy(
            src_ref=buf.at[a], dst_ref=ra.at[k], send_sem=ra_s.at[k], recv_sem=ra_r.at[k],
            device_id=device, device_id_type=MESH,
        )

    def rb_copy(k):
        i, device = zc_peer(k)
        return pltpu.make_async_remote_copy(
            src_ref=part, dst_ref=rb.at[me_zc], send_sem=rb_s.at[k], recv_sem=rb_r.at[k],
            device_id=device, device_id_type=MESH,
        )

    def g2_copy(k):
        a, device = yx_peer(k)
        return pltpu.make_async_remote_copy(
            src_ref=g0, dst_ref=g2.at[me_yx], send_sem=g2_s.at[k], recv_sem=g2_r.at[k],
            device_id=device, device_id_type=MESH,
        )

    def late(b, _):
        lon_copy(0, 1, b).wait_recv()
        lon_copy(1, 1, b).wait_recv()

        def late_row(i, _):
            r = b * RB + i
            got = jnp.concatenate(
                [recv0[0, r], recv1[0, r], recv0[1, r], recv1[1, r], jnp.zeros((16, CZ), F32)],
                axis=0,
            )
            hi, lo = split(got)
            add = jnp.dot(
                table[C_FIX : C_FIX + 96],
                jnp.concatenate([hi, lo], axis=0),
                preferred_element_type=F32,
            )
            out[1:7, r] = out[1:7, r] + add.reshape(6, CL, CZ)
            return 0

        lax.fori_loop(0, RB, late_row, 0, unroll=8)
        return 0

    def late(b, _):
        lon_copy(0, 1, b).wait_recv()
        lon_copy(1, 1, b).wait_recv()
        for h in range(RB // 4):
            g = b * (RB // 4) + h
            tail = [recv1[0, g, 64:72], recv1[1, g, 64:72], jnp.zeros((16, CZ), F32)]
            for i in range(4):
                got = jnp.concatenate(
                    [recv1[side, g, i * 16 : (i + 1) * 16] for side in range(2)] + tail, axis=0
                )
                add = jnp.dot(
                    table[C_FIX + i * 96 : C_FIX + (i + 1) * 96],
                    jnp.concatenate(split(got), axis=0),
                    preferred_element_type=F32,
                )
                r = 4 * g + i
                out[1:7, r] = out[1:7, r] + add.reshape(6, CL, CZ)
        return 0

    for k in yx_order:
        ra_copy(k).start()
    lax.fori_loop(SENDS[1], SENDS[2], send_late, 0)
    send_rad(2)

    lax.fori_loop(0, PASS[0], second_pass, 0)
    cols[...] = jnp.zeros((8, 256), F32)
    cols[0:2, 0:CH] = inj[...]
    cols[2:3, 0:CH] = cou[...]
    cols[3:4, 0:CH] = wei[...]
    columns = cols[...].T
    channel_rate = jnp.broadcast_to(columns[0:CH, 2:3], (CH, TP))
    channel_weight = jnp.broadcast_to(columns[0:CH, 3:4], (CH, TP))

    def drift(density):
        for _ in range(DRIFT):
            density = density - channel_rate * (density - pltpu.roll(density, 1, axis=1))
        return density

    dens_copy.wait()
    bare = jnp.sum(channel_weight * drift(dens[...]), axis=0, keepdims=True)

    rate_row, weight_row = cols[2:3], cols[3:4]
    keep = 1.0 - rate_row
    powers = (
        keep * keep * keep,
        3.0 * keep * keep * rate_row,
        3.0 * keep * rate_row * rate_row,
        rate_row * rate_row * rate_row,
    )
    taps = [
        [
            jnp.sum(0.5 * weight_row * cols[i : i + 1] * power, axis=1, keepdims=True)
            for power in powers
        ]
        for i in range(2)
    ]

    total = buf[me_yx]
    for k in range(1, NYX):
        ra_copy(k).wait_recv()
        total = total + ra[k]
    part[:, 0 : 2 * TP] = total
    part[:, 2 * TP :] = jnp.broadcast_to(bare, (NZC, TP))
    for k in zc_order:
        rb_copy(k).start()
    lax.fori_loop(SENDS[2], SENDS[3], send_late, 0)
    lax.fori_loop(PASS[0], CR // 4, second_pass, 0)
    add_rad(1)
    lax.fori_loop(0, LATE[0], late, 0)
    rb[me_zc] = part[...]
    for k in range(1, NZC):
        rb_copy(k).wait_recv()
    source = rb[0, :, 0 : 2 * TP]
    for j in range(1, NZC):
        source = source + rb[j, :, 0 : 2 * TP]
    tile_row = lax.broadcasted_iota(jnp.int32, (NZC, TP), 0)
    pressure = jnp.zeros((NZC, TP), F32)
    for j in range(NZC):
        pressure = jnp.where(tile_row == j, rb[j, :, 2 * TP :], pressure)
    for i in range(2):
        s = source[:, i * TP : (i + 1) * TP]
        for n in range(4):
            pressure = pressure + taps[i][n] * (pltpu.roll(s, n, axis=1) if n else s)
    g0[...] = pressure
    for k in yx_order:
        g2_copy(k).start()
    lax.fori_loop(SENDS[3], SENDS[4], send_late, 0)
    g2[me_yx] = pressure

    own = lax.broadcasted_iota(jnp.int32, (NZC, 2 * TP), 0) == me_zc
    mine = jnp.sum(jnp.where(own, source, 0.0), axis=0, keepdims=True)
    drifted[...] = drift(
        dens[...]
        + 0.5 * (columns[0:CH, 0:1] * mine[:, 0:TP] + columns[0:CH, 1:2] * mine[:, TP:])
    )
    add_rad(2)
    lax.fori_loop(LATE[0], LATE[1], late, 0)

    for k in range(1, NYX):
        g2_copy(k).wait_recv()
    back_hi, back_lo = split(g2[...].reshape(DEVICES, TP))
    pay[0:CR, 0:TP] = jnp.dot(hit_bd[...], back_hi, preferred_element_type=F32) + jnp.dot(
        hit_bd[...], back_lo, preferred_element_type=F32
    )

    def nudge(b, _):
        got = pay[pl.ds(b * 16, 16), 0:TP]
        wide = jnp.broadcast_to(got[:, None, :], (16, CL, TP)) * mask[None]
        back = jnp.dot(
            jnp.concatenate(split(wide.reshape(16 * CL, TP)), axis=1),
            seg_t[...],
            preferred_element_type=F32,
        )
        old = out[7, pl.ds(b * 16, 16)].reshape(16 * CL, CZ)
        out[7, pl.ds(b * 16, 16)] = (old + 0.5 * (back - old)).reshape(16, CL, CZ)
        return 0

    lax.fori_loop(0, CR // 16, nudge, 0, unroll=2)
    lax.fori_loop(LATE[1], NB, late, 0)

    def sent(b, _):
        for side in range(2):
            for part in range(2):
                lon_copy(side, part, b).wait_send()
        return 0

    lax.fori_loop(0, NB, sent, 0)
    for side in range(2):
        @pl.when(has[side])
        def _():
            for part_of in range(3):
                rad_copy(side, part_of).wait_send()
    for k in range(1, NYX):
        ra_copy(k).wait_send()
        g2_copy(k).wait_send()
    for k in range(1, NZC):
        rb_copy(k).wait_send()


def finish(fields, density, fields_out, density_out, sem):
    copies = [
        pltpu.make_async_copy(fields.at[f], fields_out.at[f], sem.at[f]) for f in range(NF)
    ] + [pltpu.make_async_copy(density, density_out, sem.at[NF])]
    for copy in copies:
        copy.start()
    for copy in copies:
        copy.wait()


def per_device(
    state, flux_matrices, wave_speed, flux_volume, block_tile, tile_of_device,
    phase_density, injection, drift_courant, energy_weight,
):
    hbm = pl.BlockSpec(memory_space=pltpu.HBM)
    vmem = pl.BlockSpec(memory_space=pltpu.VMEM)
    dma = pltpu.SemaphoreType.DMA
    coupled, drifted = pl.pallas_call(
        kernel,
        out_shape=(
            pltpu.VMEM((NF, CR, CL, CZ), F32),
            pltpu.VMEM((CH, TP), F32),
        ),
        in_specs=[hbm] * 11,
        out_specs=(vmem, vmem),
        scratch_shapes=[
            pltpu.SMEM((2, NF, NF), F32),
            pltpu.SMEM((2,), F32),
            pltpu.VMEM((1, CR), jnp.int32),
            pltpu.VMEM((1, DEVICES), jnp.int32),
            pltpu.VMEM((C_END, 128), BF16),
            pltpu.VMEM((2, CH), F32),
            pltpu.VMEM((1, CH), F32),
            pltpu.VMEM((1, CH), F32),
            pltpu.VMEM((NF, CR + 6, CL, CZ), F32),
            pltpu.VMEM((CR, CL, CZ), F32),
            pltpu.VMEM((CH, TP), F32),
            pltpu.VMEM((M_END, 256), BF16),
            pltpu.VMEM((CR, 256, CZ), BF16),
            pltpu.VMEM((CR, 256, CZ), BF16),
            pltpu.VMEM((2, CR // 4, 24, CZ), F32),
            pltpu.VMEM((2, CR // 4, 72, CZ), F32),
            pltpu.VMEM((2, CR // 4, 24, CZ), F32),
            pltpu.VMEM((2, CR // 4, 72, CZ), F32),
            pltpu.VMEM((2, NF, 3, CL, CZ), F32),
            pltpu.VMEM((2, NF, 3, CL, CZ), F32),
            pltpu.VMEM((8, 256), F32),
            pltpu.VMEM((CR * 8, 2 * TP), F32),
            pltpu.VMEM((DEVICES, CR * 8), BF16),
            pltpu.VMEM((CR, DEVICES), BF16),
            pltpu.VMEM((2 * TP, CZ), BF16),
            pltpu.VMEM((NYX, NZC, 2 * TP), F32),
            pltpu.VMEM((NYX, NZC, 2 * TP), F32),
            pltpu.VMEM((NZC, 3 * TP), F32),
            pltpu.VMEM((NZC, NZC, 3 * TP), F32),
            pltpu.VMEM((NZC, TP), F32),
            pltpu.VMEM((NYX, NZC, TP), F32),
            dma((8,)), dma((NB,)), dma, dma,
            dma((2, NB)), dma((2, NB)), dma((2, NB)), dma((2, NB)),
            dma((2, 3)), dma((2, 3)), dma((NYX,)), dma((NYX,)),
            dma((NZC,)), dma((NZC,)), dma((NYX,)), dma((NYX,)),
        ],
        compiler_params=pltpu.CompilerParams(
            collective_id=0, has_side_effects=True, vmem_limit_bytes=54 << 20
        ),
    )(
        state,
        flux_volume,
        phase_density.reshape(CH, TP),
        flux_matrices,
        wave_speed,
        block_tile.reshape(1, CR),
        tile_of_device.reshape(1, DEVICES),
        injection,
        drift_courant.reshape(1, CH),
        energy_weight.reshape(1, CH),
        jnp.asarray(constants()),
    )
    coupled, drifted = pl.pallas_call(
        finish,
        out_shape=(
            jax.ShapeDtypeStruct((NF, CR, CL, CZ), F32),
            jax.ShapeDtypeStruct((CH, TP), F32),
        ),
        in_specs=[vmem, vmem],
        out_specs=(hbm, hbm),
        scratch_shapes=[dma((NF + 1,))],
        compiler_params=pltpu.CompilerParams(vmem_limit_bytes=1 << 20),
    )(coupled, drifted)
    return coupled, drifted[None]


def solution(mesh):
    in_specs = (
        P(None, "rad", "lon", None),
        P(),
        P(),
        P("rad", "lon", None),
        P("lon", "rad", None),
        P(),
        P(("rad", "lon"), None, None),
        P(),
        P(),
        P(),
    )
    out_specs = (P(None, "rad", "lon", None), P(("rad", "lon"), None, None))
    return jax.shard_map(
        per_device, mesh=mesh, in_specs=in_specs, out_specs=out_specs, check_vma=False
    )
```

```python
import numpy as np

import jax
import jax.numpy as jnp
import ml_dtypes
from jax import lax
from jax.experimental import pallas as pl
from jax.experimental.pallas import tpu as pltpu
from jax.sharding import PartitionSpec as P

F32 = jnp.float32
BF16 = jnp.bfloat16
HIGHEST = lax.Precision.HIGHEST
MESH = pl.DeviceIdType.MESH

NF, CR, CL, CZ = 8, 64, 16, 256
ZSEG = 8
DRIFT = 3
CH, TP = 200, 128
NRAD, NLON = 4, 32
NYX, NZC = 16, 8
DEVICES = NRAD * NLON

SCALE = 0.4 * 0.5 / 30.0
ORDER = (0, 7, 1, 2, 3, 4, 5, 6)
ODD = {-3: -1.0, -2: 9.0, -1: -45.0, 1: 45.0, 2: -9.0, 3: 1.0}
EVEN = {-3: 1.0, -2: -6.0, -1: 15.0, 0: -20.0, 1: 15.0, 2: -6.0, 3: 1.0}

RB = 8
NB = CR // RB
SENDS = (0, 4, 6, 7, NB)
PASS = (10,)
TWO = 0
LATE = (4, 7)

C_FIX07, C_FIX, C_SEG, C_MASK, C_ODD, C_EVEN, C_EODD, C_EEVEN, C_END = (
    0, 128, 512, 768, 784, 800, 816, 864, 912
)
H_07, L_07, H_EDGE, L_EDGE, HR_07, LR_07, H_16, L_16, HR_16, LR_16, M_END = (
    0, 32, 64, 112, 160, 192, 224, 320, 416, 512, 608
)


def constants():
    t = np.zeros((C_END, 128), np.float32)
    half = 64
    for c in range(2):
        for r in range(4):
            for l in range(CL):
                row = C_FIX07 + (c * 4 + r) * CL + l
                for h in range(2):
                    if l < 3:
                        t[row, h * half + r * 6 + 3 * c + l] = 1
                    if l >= CL - 3:
                        t[row, h * half + 24 + r * 6 + 3 * c + l - (CL - 3)] = 1
    for r in range(4):
        for pos in range(2, NF):
            for l in range(CL):
                row = C_FIX + r * 96 + (pos - 2) * CL + l
                side = 0 if l < 3 else 1
                k = l if l < 3 else l - (CL - 3)
                if 0 <= k < 3:
                    q = 3 * pos + k
                    at = side * 16 + q - 8 if q >= 8 else 32 + side * 8 + r * 2 + q - 6
                    for h in range(2):
                        t[row, h * half + at] = 1
    for z in range(CZ):
        for p in range(TP):
            t[C_SEG + z, p] = z // (CZ // ZSEG) == p % ZSEG
    for l in range(CL):
        for p in range(TP):
            t[C_MASK + l, p] = p // ZSEG == l
    for l in range(CL):
        for f in range(NF):
            for j in range(CL):
                t[C_ODD + l, f * CL + j] = ODD.get(j - l, 0.0)
                t[C_EVEN + l, f * CL + j] = EVEN.get(j - l, 0.0)
    for side in range(2):
        for pos in range(NF):
            for k in range(3):
                row = side * 24 + 3 * pos + k
                for f in range(NF):
                    for j in range(CL):
                        off = j - CL - k if side == 0 else 3 + j - k
                        t[C_EODD + row, f * CL + j] = ODD.get(off, 0.0)
                        if f == ORDER[pos]:
                            t[C_EEVEN + row, f * CL + j] = EVEN.get(off, 0.0)
    return t.astype(ml_dtypes.bfloat16)


def split(x):
    hi = x.astype(BF16)
    return hi, (x - hi.astype(F32)).astype(BF16)


def kernel(
    state, volume, phase, matrices_in, speeds_in, targets_in, tiles_in, injection, courant, weight,
    table_in,
    out, drifted,
    matrices, speeds, targets, tiles, table, inj, cou, wei, cells, vol, dens, lhs, tt1, tt2,
    send0, send1, recv0, recv1, rad_send, rad_recv, cols, pay, hit_db, hit_bd, seg_t, buf, ra,
    part, other, both, rb, g0, g2,
    small_sem, load_sem, vol_sem, dens_sem, lon_s0, lon_r0, lon_s1, lon_r1, rad_s, rad_r,
    ra_s, ra_r, swap_s, swap_r, rb_s, rb_r, g2_s, g2_r,
):
    rad, lon = lax.axis_index("rad"), lax.axis_index("lon")
    right, left = lax.rem(lon + 1, NLON), lax.rem(lon + NLON - 1, NLON)
    me_yx = rad * (NYX // NRAD) + lax.div(lon, NZC)
    me_zc = lax.rem(lon, NZC)

    x_at, z_at, core_at = lax.div(lon, NZC), lax.rem(lax.div(lon, 2), 4), lax.rem(lon, 2)

    def yx_peer(k):
        y, x = lax.rem(rad + k // 4, NRAD), lax.rem(x_at + k % 4, NYX // NRAD)
        return y * (NYX // NRAD) + x, (y, x * NZC + me_zc)

    def zc_peer(k):
        core = 1 - core_at if k % 2 else core_at
        i = lax.rem(z_at + k // 2, 4) * 2 + core
        return i, (rad, x_at * NZC + i)

    def hops(n):
        return min(n, 4 - n)

    yx_order = sorted(range(1, NYX), key=lambda k: -hops(k // 4) - hops(k % 4))
    zc_order = sorted(range(1, NZC), key=lambda k: -2 * hops(k // 2) - k % 2)

    small = [
        pltpu.make_async_copy(src, dst, small_sem.at[i])
        for i, (src, dst) in enumerate((
            (matrices_in, matrices), (speeds_in, speeds), (table_in, table),
            (targets_in, targets), (tiles_in, tiles),
            (injection, inj), (courant, cou), (weight, wei),
        ))
    ]
    for copy in small:
        copy.start()

    def load(b):
        return pltpu.make_async_copy(
            state.at[:, pl.ds(b * RB, RB)], cells.at[:, pl.ds(3 + b * RB, RB)], load_sem.at[b]
        )

    for b in [0, 1, NB - 1] + list(range(2, NB - 1)):
        load(b).start()
    vol_copy = pltpu.make_async_copy(volume, vol, vol_sem)
    vol_copy.start()
    dens_copy = pltpu.make_async_copy(phase, dens, dens_sem)
    dens_copy.start()

    barrier = pltpu.get_barrier_semaphore()

    def greet(device):
        pl.semaphore_signal(barrier, inc=1, device_id=device, device_id_type=MESH)

    greet((rad, right))
    greet((rad, left))
    for k in yx_order:
        greet(yx_peer(k)[1])
    for k in zc_order:
        greet(zc_peer(k)[1])

    cells[:, 0:3] = jnp.zeros((NF, 3, CL, CZ), F32)
    cells[:, 3 + CR :] = jnp.zeros((NF, 3, CL, CZ), F32)

    for copy in small:
        copy.wait()
    lane = lax.broadcasted_iota(jnp.int32, (CL, 128), 1)
    sub = lax.broadcasted_iota(jnp.int32, (CL, 128), 0)
    block = lax.shift_right_logical(lane, 4)
    same_l = jnp.bitwise_and(lane, CL - 1) == sub
    odd, even = table[C_ODD : C_ODD + CL].astype(F32), table[C_EVEN : C_EVEN + CL].astype(F32)
    rows_l = []
    zero = jnp.zeros((CL, 128), BF16)
    for f in range(NF):
        row_r = jnp.zeros((CL, 128), F32)
        row_l = jnp.zeros((CL, 128), F32)
        for g in range(NF):
            row_r = jnp.where(block == g, matrices[0, f, g], row_r)
            row_l = jnp.where(block == g, matrices[1, f, g], row_l)
        rows_l.append(row_l)
        eye = lane == sub + f * CL
        w = (
            (SCALE * speeds[1]) * jnp.where(block == f, even, 0.0)
            - SCALE * row_l * odd
            + jnp.where(eye, 1.0 - 20.0 * SCALE * speeds[0], 0.0)
        )
        whi, wlo = split(w)
        rhi, rlo = split(jnp.where(same_l, (-45.0 * SCALE) * row_r, 0.0))
        at = {0: 0, 7: CL}.get(f, (f - 1) * CL)
        h, l, hr, lr = (H_07, L_07, HR_07, LR_07) if f in (0, 7) else (H_16, L_16, HR_16, LR_16)
        for start, high, low in ((h, whi, None), (l, wlo, zero), (hr, rhi, None), (lr, rlo, zero)):
            lhs[start + at : start + at + CL, 0:128] = high
            lhs[start + at : start + at + CL, 128:256] = high if low is None else low
    q = lax.broadcasted_iota(jnp.int32, (24, 128), 0)
    row_e = jnp.zeros((24, 128), F32)
    for pos, f in enumerate(ORDER):
        wide = jnp.concatenate([rows_l[f][0:8]] * 3, axis=0)
        row_e = jnp.where((q >= 3 * pos) & (q < 3 * pos + 3), wide, row_e)
    row_e = jnp.concatenate([row_e, row_e], axis=0)
    we = (SCALE * speeds[1]) * table[C_EEVEN : C_EEVEN + 48].astype(F32) - (
        SCALE * row_e * table[C_EODD : C_EODD + 48].astype(F32)
    )
    ehi, elo = split(we)
    lhs[H_EDGE : H_EDGE + 48, 0:128] = ehi
    lhs[H_EDGE : H_EDGE + 48, 128:256] = ehi
    lhs[L_EDGE : L_EDGE + 48, 0:128] = elo
    lhs[L_EDGE : L_EDGE + 48, 128:256] = jnp.zeros((48, 128), BF16)

    def row(i):
        return cells[:, i].reshape(NF * CL, CZ)

    def rad_edge(side):
        radial = jnp.concatenate(
            [lhs[HR_07:LR_07], lhs[HR_16:LR_16], lhs[LR_07:H_16], lhs[LR_16:M_END]], axis=0
        )
        for k in range(3):
            d = jnp.zeros((128, CZ), F32)
            e = jnp.zeros((128, CZ), F32)
            for j in range(3):
                off = j - k - 3 if side == 0 else 3 + j - k
                if off in ODD:
                    u = row(CR + j if side == 0 else 3 + j)
                    d = d + (ODD[off] / 45.0) * u
                    e = e + EVEN[off] * u
            y = jnp.dot(
                radial, jnp.concatenate(split(d), axis=0), preferred_element_type=F32
            )
            y = y[0:128] + y[128:256]
            for pos, f in enumerate(ORDER):
                rad_send[side, pos, k] = y[pos * CL : (pos + 1) * CL] + (
                    SCALE * speeds[0]
                ) * e[f * CL : (f + 1) * CL]

    rad_parts = ((0, 2), (2, 3), (5, 3))

    def rad_copy(side, part_of):
        fields = pl.ds(*rad_parts[part_of])
        return pltpu.make_async_remote_copy(
            src_ref=rad_send.at[side, fields],
            dst_ref=rad_recv.at[side, fields],
            send_sem=rad_s.at[side, part_of],
            recv_sem=rad_r.at[side, part_of],
            device_id=(rad + 1 if side == 0 else rad - 1, lon),
            device_id_type=MESH,
        )

    def send_rad(part_of):
        for side in range(2):
            @pl.when(has[side])
            def _():
                rad_copy(side, part_of).start()

    has = (rad < NRAD - 1, rad > 0)

    def lon_copy(side, part, b):
        src, dst = (send0, recv0) if part == 0 else (send1, recv1)
        ss, rs = (lon_s0, lon_r0) if part == 0 else (lon_s1, lon_r1)
        rows = pl.ds(b * (RB // 4), RB // 4)
        return pltpu.make_async_remote_copy(
            src_ref=src.at[side, rows],
            dst_ref=dst.at[side, rows],
            send_sem=ss.at[side, b],
            recv_sem=rs.at[side, b],
            device_id=(rad, right if side == 0 else left),
            device_id_type=MESH,
        )

    first_eight = lax.broadcasted_iota(jnp.int32, (8, CZ), 0)

    def pick(n, a, b):
        return jnp.where(first_eight < n, a, b)

    def lon_pass(b):
        tops = ([], [])
        for i in range(RB):
            r = b * RB + i
            t1 = jnp.concatenate(split(row(r + 3)), axis=0)
            tt1[r] = t1
            y = jnp.dot(lhs[H_07:HR_07], t1, preferred_element_type=F32)
            new = y[0:32] + y[32:64]
            out[0, r] = new[0:CL]
            out[7, r] = new[CL:]
            edge = y[64:112] + y[112:160]
            g, j = b * (RB // 4) + i // 4, i % 4
            for side in range(2):
                tops[side].append(edge[side * 24 : side * 24 + 8])
                send1[side, g, j * 16 : (j + 1) * 16] = edge[side * 24 + 8 : side * 24 + 24]
        for h in range(RB // 4):
            g = b * (RB // 4) + h
            for side in range(2):
                z0, z1, z2, z3 = tops[side][4 * h : 4 * h + 4]
                a, b1, c = (
                    pltpu.roll(z1, 6, axis=0), pltpu.roll(z2, 4, axis=0), pltpu.roll(z3, 2, axis=0)
                )
                send0[side, g, 0:8] = pick(6, z0, a)
                send0[side, g, 8:16] = pick(4, a, b1)
                send0[side, g, 16:24] = pick(2, b1, c)
                a, b1, c = (
                    pltpu.roll(z0, 2, axis=0), pltpu.roll(z1, 4, axis=0), pltpu.roll(z2, 6, axis=0)
                )
                send1[side, g, 64:72] = pick(2, a, pick(4, b1, pick(6, c, z3)))

    def rad_pass(b, _):
        for i in range(RB):
            r = b * RB + i
            m3, m2, m1, p1, p2, p3 = (row(r + n) for n in (0, 1, 2, 4, 5, 6))
            d = (p1 - m1) - 0.2 * ((p2 - m2) - (1.0 / 9.0) * (p3 - m3))
            m3, m2, m1, p1, p2, p3 = (
                jnp.concatenate([x[0:CL], x[112:128]], axis=0) for x in (m3, m2, m1, p1, p2, p3)
            )
            e = (p1 + m1) - 0.4 * ((p2 + m2) - (1.0 / 6.0) * (p3 + m3))
            t2 = jnp.concatenate(split(d), axis=0)
            tt2[r] = t2
            y = jnp.dot(lhs[HR_07:H_16], t2, preferred_element_type=F32)
            new = (y[0:32] + y[32:64]) + (15.0 * SCALE * speeds[0]) * e
            out[0, r] = out[0, r] + new[0:CL]
            out[7, r] = out[7, r] + new[CL:]
        return 0

    def second_pass(g, _):
        for i in range(4):
            r = 4 * g + i
            m3, m2, m1, p1, p2, p3 = (
                cells[1:7, r + n].reshape(96, CZ) for n in (0, 1, 2, 4, 5, 6)
            )
            e = (p1 + m1) - 0.4 * ((p2 + m2) - (1.0 / 6.0) * (p3 + m3))
            y1 = jnp.dot(lhs[H_16:HR_16], tt1[r], preferred_element_type=F32)
            y2 = jnp.dot(lhs[HR_16:M_END], tt2[r], preferred_element_type=F32)
            new = (y1[0:96] + y1[96:192] + y2[0:96] + y2[96:192]) + (
                15.0 * SCALE * speeds[0]
            ) * e
            out[1:7, r] = new.reshape(6, CL, CZ)
        return 0

    def send_early(b):
        lon_copy(0, 0, b).start()
        lon_copy(1, 0, b).start()

    def send_late(b, _):
        lon_copy(0, 1, b).start()
        lon_copy(1, 1, b).start()
        return 0

    load(0).wait()
    lon_pass(0)
    pl.semaphore_wait(barrier, 2 + NYX - 1 + NZC - 1)
    send_early(0)
    load(1).wait()
    lon_pass(1)
    send_early(1)
    load(NB - 1).wait()
    rad_edge(0)
    rad_edge(1)
    send_rad(0)
    send_rad(1)

    def rest(b, _):
        @pl.when(b < NB - 1)
        def _():
            load(b).wait()

        lon_pass(b)
        send_early(b)
        return 0

    lax.fori_loop(2, NB, rest, 0)
    lax.fori_loop(SENDS[0], SENDS[1], send_late, 0)
    tile_col = jnp.broadcast_to(tiles[...].astype(F32), (DEVICES, DEVICES)).T
    target_row = jnp.broadcast_to(targets[...].astype(F32), (DEVICES, CR))
    hit = (tile_col[:, 0:CR] == target_row).astype(BF16)
    spread = lax.shift_right_logical(
        lax.broadcasted_iota(jnp.int32, (CR, CR * 8), 1), 3
    ) == lax.broadcasted_iota(jnp.int32, (CR, CR * 8), 0)
    hit_db[...] = jnp.dot(
        hit, spread.astype(F32).astype(BF16), preferred_element_type=F32
    ).astype(BF16)
    target_col = jnp.concatenate(
        [target_row, jnp.zeros((DEVICES, DEVICES - CR), F32)], axis=1
    ).T
    hit_bd[...] = (target_col[0:CR] == tiles[...].astype(F32)).astype(F32).astype(BF16)

    seg_t[...] = (
        jnp.bitwise_and(lax.broadcasted_iota(jnp.int32, (2 * TP, CZ), 0), ZSEG - 1)
        == lax.shift_right_logical(lax.broadcasted_iota(jnp.int32, (2 * TP, CZ), 1), 5)
    ).astype(F32).astype(BF16)

    lax.fori_loop(0, NB, rad_pass, 0)

    def add_rad(part_of):
        for side in range(2):
            @pl.when(has[1 - side])
            def _():
                rad_copy(side, part_of).wait_recv()
                for pos in range(rad_parts[part_of][0], sum(rad_parts[part_of])):
                    for k in range(3):
                        r = k if side == 0 else CR - 3 + k
                        out[ORDER[pos], r] = out[ORDER[pos], r] + rad_recv[side, pos, k]

    add_rad(0)
    vol_copy.wait()
    seg = table[C_SEG : C_SEG + CZ]
    mask = table[C_MASK : C_MASK + CL].astype(F32)

    def early(b, _):
        for i in range(2):
            lon_copy(0, 0, 2 * b + i).wait_recv()
            lon_copy(1, 0, 2 * b + i).wait_recv()
        highs, lows = [], []
        for h in range(4):
            g = b * 4 + h
            got = jnp.concatenate(
                [recv0[0, g], recv0[1, g], jnp.zeros((16, CZ), F32)], axis=0
            )
            add = jnp.dot(
                table[C_FIX07 : C_FIX07 + 128],
                jnp.concatenate(split(got), axis=0),
                preferred_element_type=F32,
            )
            v = vol[pl.ds(4 * g, 4)].reshape(64, CZ)
            for c, f in enumerate((0, 7)):
                new = out[f, pl.ds(4 * g, 4)].reshape(64, CZ) + add[c * 64 : (c + 1) * 64]
                out[f, pl.ds(4 * g, 4)] = new.reshape(4, CL, CZ)
                yh, yl = split(v * new)
                highs.append(yh)
                lows.append(yl)
        t = jnp.dot(jnp.concatenate(highs + lows, axis=0), seg, preferred_element_type=F32)
        t = t[0:512] + t[512:1024]
        for h in range(4):
            for c in range(2):
                at = (h * 2 + c) * 64
                x = t[at : at + 64].reshape(4, CL, TP) * mask[None]
                pay[pl.ds(b * 128 + h * 32, 32), c * TP : (c + 1) * TP] = (
                    x[:, 0:8] + x[:, 8:16]
                ).reshape(32, TP)
        return 0

    lax.fori_loop(0, NB // 2, early, 0)

    pay_hi, pay_lo = split(pay[...])
    buf[...] = (
        jnp.dot(hit_db[...], pay_hi, preferred_element_type=F32)
        + jnp.dot(hit_db[...], pay_lo, preferred_element_type=F32)
    ).reshape(NYX, NZC, 2 * TP)

    def ra_copy(k):
        a, device = yx_peer(k)
        return pltpu.make_async_remote_copy(
            src_ref=buf.at[a], dst_ref=ra.at[k], send_sem=ra_s.at[k], recv_sem=ra_r.at[k],
            device_id=device, device_id_type=MESH,
        )

    def swap_copy():
        return pltpu.make_async_remote_copy(
            src_ref=part, dst_ref=other, send_sem=swap_s, recv_sem=swap_r,
            device_id=(rad, lon + 1 - 2 * core_at), device_id_type=MESH,
        )

    def z_copy(n, core):
        return pltpu.make_async_remote_copy(
            src_ref=both, dst_ref=rb.at[z_at], send_sem=rb_s.at[n, core], recv_sem=rb_r.at[n],
            device_id=(rad, x_at * NZC + lax.rem(z_at + n, 4) * 2 + core), device_id_type=MESH,
        )

    def each_z(act):
        for sender in range(2):
            @pl.when(core_at == sender)
            def _():
                for n in (2, 1, 3):
                    if sender == {1: 0, 2: TWO, 3: 1}[n]:
                        for core in range(2):
                            act(z_copy(n, core))

    def g2_copy(k):
        a, device = yx_peer(k)
        return pltpu.make_async_remote_copy(
            src_ref=g0, dst_ref=g2.at[me_yx], send_sem=g2_s.at[k], recv_sem=g2_r.at[k],
            device_id=device, device_id_type=MESH,
        )

    def late(b, _):
        lon_copy(0, 1, b).wait_recv()
        lon_copy(1, 1, b).wait_recv()

        def late_row(i, _):
            r = b * RB + i
            got = jnp.concatenate(
                [recv0[0, r], recv1[0, r], recv0[1, r], recv1[1, r], jnp.zeros((16, CZ), F32)],
                axis=0,
            )
            hi, lo = split(got)
            add = jnp.dot(
                table[C_FIX : C_FIX + 96],
                jnp.concatenate([hi, lo], axis=0),
                preferred_element_type=F32,
            )
            out[1:7, r] = out[1:7, r] + add.reshape(6, CL, CZ)
            return 0

        lax.fori_loop(0, RB, late_row, 0, unroll=8)
        return 0

    def late(b, _):
        lon_copy(0, 1, b).wait_recv()
        lon_copy(1, 1, b).wait_recv()
        for h in range(RB // 4):
            g = b * (RB // 4) + h
            tail = [recv1[0, g, 64:72], recv1[1, g, 64:72], jnp.zeros((16, CZ), F32)]
            for i in range(4):
                got = jnp.concatenate(
                    [recv1[side, g, i * 16 : (i + 1) * 16] for side in range(2)] + tail, axis=0
                )
                add = jnp.dot(
                    table[C_FIX + i * 96 : C_FIX + (i + 1) * 96],
                    jnp.concatenate(split(got), axis=0),
                    preferred_element_type=F32,
                )
                r = 4 * g + i
                out[1:7, r] = out[1:7, r] + add.reshape(6, CL, CZ)
        return 0

    for k in yx_order:
        ra_copy(k).start()
    lax.fori_loop(SENDS[1], SENDS[2], send_late, 0)
    send_rad(2)

    lax.fori_loop(0, PASS[0], second_pass, 0)
    cols[...] = jnp.zeros((8, 256), F32)
    cols[0:2, 0:CH] = inj[...]
    cols[2:3, 0:CH] = cou[...]
    cols[3:4, 0:CH] = wei[...]
    columns = cols[...].T
    channel_rate = jnp.broadcast_to(columns[0:CH, 2:3], (CH, TP))
    channel_weight = jnp.broadcast_to(columns[0:CH, 3:4], (CH, TP))

    def drift(density):
        for _ in range(DRIFT):
            density = density - channel_rate * (density - pltpu.roll(density, 1, axis=1))
        return density

    dens_copy.wait()
    bare = jnp.sum(channel_weight * drift(dens[...]), axis=0, keepdims=True)

    rate_row, weight_row = cols[2:3], cols[3:4]
    keep = 1.0 - rate_row
    powers = (
        keep * keep * keep,
        3.0 * keep * keep * rate_row,
        3.0 * keep * rate_row * rate_row,
        rate_row * rate_row * rate_row,
    )
    taps = [
        [
            jnp.sum(0.5 * weight_row * cols[i : i + 1] * power, axis=1, keepdims=True)
            for power in powers
        ]
        for i in range(2)
    ]

    total = buf[me_yx]
    for k in range(1, NYX):
        ra_copy(k).wait_recv()
        total = total + ra[k]
    part[:, 0 : 2 * TP] = total
    part[:, 2 * TP :] = jnp.broadcast_to(bare, (NZC, TP))
    swap_copy().start()
    swap_copy().wait_recv()
    both[:, 0 : 2 * TP] = part[:, 0 : 2 * TP] + other[:, 0 : 2 * TP]
    first = core_at == 0
    both[:, 2 * TP : 3 * TP] = jnp.where(first, part[:, 2 * TP :], other[:, 2 * TP :])
    both[:, 3 * TP :] = jnp.where(first, other[:, 2 * TP :], part[:, 2 * TP :])
    each_z(lambda copy: copy.start())
    lax.fori_loop(SENDS[2], SENDS[3], send_late, 0)
    lax.fori_loop(PASS[0], CR // 4, second_pass, 0)
    add_rad(1)
    lax.fori_loop(0, LATE[0], late, 0)
    rb[z_at] = both[...]
    for n in (1, 2, 3):
        z_copy(n, 0).wait_recv()
    source = rb[0, :, 0 : 2 * TP]
    for j in range(1, 4):
        source = source + rb[j, :, 0 : 2 * TP]
    tile_row = lax.broadcasted_iota(jnp.int32, (NZC, TP), 0)
    pressure = jnp.zeros((NZC, TP), F32)
    for j in range(NZC):
        at = (2 + j % 2) * TP
        pressure = jnp.where(tile_row == j, rb[j // 2, :, at : at + TP], pressure)
    for i in range(2):
        s = source[:, i * TP : (i + 1) * TP]
        for n in range(4):
            pressure = pressure + taps[i][n] * (pltpu.roll(s, n, axis=1) if n else s)
    g0[...] = pressure
    for k in yx_order:
        g2_copy(k).start()
    lax.fori_loop(SENDS[3], SENDS[4], send_late, 0)
    g2[me_yx] = pressure

    own = lax.broadcasted_iota(jnp.int32, (NZC, 2 * TP), 0) == me_zc
    mine = jnp.sum(jnp.where(own, source, 0.0), axis=0, keepdims=True)
    drifted[...] = drift(
        dens[...]
        + 0.5 * (columns[0:CH, 0:1] * mine[:, 0:TP] + columns[0:CH, 1:2] * mine[:, TP:])
    )
    add_rad(2)
    lax.fori_loop(LATE[0], LATE[1], late, 0)

    for k in range(1, NYX):
        g2_copy(k).wait_recv()
    back_hi, back_lo = split(g2[...].reshape(DEVICES, TP))
    pay[0:CR, 0:TP] = jnp.dot(hit_bd[...], back_hi, preferred_element_type=F32) + jnp.dot(
        hit_bd[...], back_lo, preferred_element_type=F32
    )

    def nudge(b, _):
        got = pay[pl.ds(b * 16, 16), 0:TP]
        wide = jnp.broadcast_to(got[:, None, :], (16, CL, TP)) * mask[None]
        back = jnp.dot(
            jnp.concatenate(split(wide.reshape(16 * CL, TP)), axis=1),
            seg_t[...],
            preferred_element_type=F32,
        )
        old = out[7, pl.ds(b * 16, 16)].reshape(16 * CL, CZ)
        out[7, pl.ds(b * 16, 16)] = (old + 0.5 * (back - old)).reshape(16, CL, CZ)
        return 0

    lax.fori_loop(0, CR // 16, nudge, 0, unroll=2)
    lax.fori_loop(LATE[1], NB, late, 0)

    def sent(b, _):
        for side in range(2):
            for part in range(2):
                lon_copy(side, part, b).wait_send()
        return 0

    lax.fori_loop(0, NB, sent, 0)
    for side in range(2):
        @pl.when(has[side])
        def _():
            for part_of in range(3):
                rad_copy(side, part_of).wait_send()
    for k in range(1, NYX):
        ra_copy(k).wait_send()
        g2_copy(k).wait_send()
    swap_copy().wait_send()
    each_z(lambda copy: copy.wait_send())


def finish(fields, density, fields_out, density_out, sem):
    copies = [
        pltpu.make_async_copy(fields.at[f], fields_out.at[f], sem.at[f]) for f in range(NF)
    ] + [pltpu.make_async_copy(density, density_out, sem.at[NF])]
    for copy in copies:
        copy.start()
    for copy in copies:
        copy.wait()


def per_device(
    state, flux_matrices, wave_speed, flux_volume, block_tile, tile_of_device,
    phase_density, injection, drift_courant, energy_weight,
):
    hbm = pl.BlockSpec(memory_space=pltpu.HBM)
    vmem = pl.BlockSpec(memory_space=pltpu.VMEM)
    dma = pltpu.SemaphoreType.DMA
    coupled, drifted = pl.pallas_call(
        kernel,
        out_shape=(
            pltpu.VMEM((NF, CR, CL, CZ), F32),
            pltpu.VMEM((CH, TP), F32),
        ),
        in_specs=[hbm] * 11,
        out_specs=(vmem, vmem),
        scratch_shapes=[
            pltpu.SMEM((2, NF, NF), F32),
            pltpu.SMEM((2,), F32),
            pltpu.VMEM((1, CR), jnp.int32),
            pltpu.VMEM((1, DEVICES), jnp.int32),
            pltpu.VMEM((C_END, 128), BF16),
            pltpu.VMEM((2, CH), F32),
            pltpu.VMEM((1, CH), F32),
            pltpu.VMEM((1, CH), F32),
            pltpu.VMEM((NF, CR + 6, CL, CZ), F32),
            pltpu.VMEM((CR, CL, CZ), F32),
            pltpu.VMEM((CH, TP), F32),
            pltpu.VMEM((M_END, 256), BF16),
            pltpu.VMEM((CR, 256, CZ), BF16),
            pltpu.VMEM((CR, 256, CZ), BF16),
            pltpu.VMEM((2, CR // 4, 24, CZ), F32),
            pltpu.VMEM((2, CR // 4, 72, CZ), F32),
            pltpu.VMEM((2, CR // 4, 24, CZ), F32),
            pltpu.VMEM((2, CR // 4, 72, CZ), F32),
            pltpu.VMEM((2, NF, 3, CL, CZ), F32),
            pltpu.VMEM((2, NF, 3, CL, CZ), F32),
            pltpu.VMEM((8, 256), F32),
            pltpu.VMEM((CR * 8, 2 * TP), F32),
            pltpu.VMEM((DEVICES, CR * 8), BF16),
            pltpu.VMEM((CR, DEVICES), BF16),
            pltpu.VMEM((2 * TP, CZ), BF16),
            pltpu.VMEM((NYX, NZC, 2 * TP), F32),
            pltpu.VMEM((NYX, NZC, 2 * TP), F32),
            pltpu.VMEM((NZC, 3 * TP), F32),
            pltpu.VMEM((NZC, 3 * TP), F32),
            pltpu.VMEM((NZC, 4 * TP), F32),
            pltpu.VMEM((4, NZC, 4 * TP), F32),
            pltpu.VMEM((NZC, TP), F32),
            pltpu.VMEM((NYX, NZC, TP), F32),
            dma((8,)), dma((NB,)), dma, dma,
            dma((2, NB)), dma((2, NB)), dma((2, NB)), dma((2, NB)),
            dma((2, 3)), dma((2, 3)), dma((NYX,)), dma((NYX,)),
            dma, dma, dma((4, 2)), dma((4,)), dma((NYX,)), dma((NYX,)),
        ],
        compiler_params=pltpu.CompilerParams(
            collective_id=0, has_side_effects=True, vmem_limit_bytes=54 << 20
        ),
    )(
        state,
        flux_volume,
        phase_density.reshape(CH, TP),
        flux_matrices,
        wave_speed,
        block_tile.reshape(1, CR),
        tile_of_device.reshape(1, DEVICES),
        injection,
        drift_courant.reshape(1, CH),
        energy_weight.reshape(1, CH),
        jnp.asarray(constants()),
    )
    coupled, drifted = pl.pallas_call(
        finish,
        out_shape=(
            jax.ShapeDtypeStruct((NF, CR, CL, CZ), F32),
            jax.ShapeDtypeStruct((CH, TP), F32),
        ),
        in_specs=[vmem, vmem],
        out_specs=(hbm, hbm),
        scratch_shapes=[dma((NF + 1,))],
        compiler_params=pltpu.CompilerParams(vmem_limit_bytes=1 << 20),
    )(coupled, drifted)
    return coupled, drifted[None]


def solution(mesh):
    in_specs = (
        P(None, "rad", "lon", None),
        P(),
        P(),
        P("rad", "lon", None),
        P("lon", "rad", None),
        P(),
        P(("rad", "lon"), None, None),
        P(),
        P(),
        P(),
    )
    out_specs = (P(None, "rad", "lon", None), P(("rad", "lon"), None, None))
    return jax.shard_map(
        per_device, mesh=mesh, in_specs=in_specs, out_specs=out_specs, check_vma=False
    )
```

```python
import numpy as np

import jax
import jax.numpy as jnp
import ml_dtypes
from jax import lax
from jax.experimental import pallas as pl
from jax.experimental.pallas import tpu as pltpu
from jax.sharding import PartitionSpec as P

F32 = jnp.float32
BF16 = jnp.bfloat16
HIGHEST = lax.Precision.HIGHEST
MESH = pl.DeviceIdType.MESH

NF, CR, CL, CZ = 8, 64, 16, 256
ZSEG = 8
DRIFT = 3
CH, TP = 200, 128
NRAD, NLON = 4, 32
NYX, NZC = 16, 8
DEVICES = NRAD * NLON

SCALE = 0.4 * 0.5 / 30.0
ORDER = (0, 7, 1, 2, 3, 4, 5, 6)
ODD = {-3: -1.0, -2: 9.0, -1: -45.0, 1: 45.0, 2: -9.0, 3: 1.0}
EVEN = {-3: 1.0, -2: -6.0, -1: 15.0, 0: -20.0, 1: 15.0, 2: -6.0, 3: 1.0}

RB = 8
NB = CR // RB
SENDS = (0, 4, 7, 7, NB)
PASS = (10,)
TWO = 0
LATE = (4, NB)

C_FIX07, C_FIX, C_SEG, C_MASK, C_ODD, C_EVEN, C_EODD, C_EEVEN, C_END = (
    0, 128, 512, 768, 784, 800, 816, 864, 912
)
H_07, L_07, H_EDGE, L_EDGE, HR_07, LR_07, H_16, L_16, HR_16, LR_16, M_END = (
    0, 32, 64, 112, 160, 192, 224, 320, 416, 512, 608
)


def constants():
    t = np.zeros((C_END, 128), np.float32)
    half = 64
    for c in range(2):
        for r in range(4):
            for l in range(CL):
                row = C_FIX07 + (c * 4 + r) * CL + l
                for h in range(2):
                    if l < 3:
                        t[row, h * half + r * 6 + 3 * c + l] = 1
                    if l >= CL - 3:
                        t[row, h * half + 24 + r * 6 + 3 * c + l - (CL - 3)] = 1
    for r in range(4):
        for pos in range(2, NF):
            for l in range(CL):
                row = C_FIX + r * 96 + (pos - 2) * CL + l
                side = 0 if l < 3 else 1
                k = l if l < 3 else l - (CL - 3)
                if 0 <= k < 3:
                    q = 3 * pos + k
                    at = side * 16 + q - 8 if q >= 8 else 32 + side * 8 + r * 2 + q - 6
                    for h in range(2):
                        t[row, h * half + at] = 1
    for z in range(CZ):
        for p in range(TP):
            t[C_SEG + z, p] = z // (CZ // ZSEG) == p % ZSEG
    for l in range(CL):
        for p in range(TP):
            t[C_MASK + l, p] = p // ZSEG == l
    for l in range(CL):
        for f in range(NF):
            for j in range(CL):
                t[C_ODD + l, f * CL + j] = ODD.get(j - l, 0.0)
                t[C_EVEN + l, f * CL + j] = EVEN.get(j - l, 0.0)
    for side in range(2):
        for pos in range(NF):
            for k in range(3):
                row = side * 24 + 3 * pos + k
                for f in range(NF):
                    for j in range(CL):
                        off = j - CL - k if side == 0 else 3 + j - k
                        t[C_EODD + row, f * CL + j] = ODD.get(off, 0.0)
                        if f == ORDER[pos]:
                            t[C_EEVEN + row, f * CL + j] = EVEN.get(off, 0.0)
    return t.astype(ml_dtypes.bfloat16)


def split(x):
    hi = x.astype(BF16)
    return hi, (x - hi.astype(F32)).astype(BF16)


def kernel(
    state, volume, phase, matrices_in, speeds_in, targets_in, tiles_in, injection, courant, weight,
    table_in,
    out, drifted,
    matrices, speeds, targets, tiles, table, inj, cou, wei, cells, vol, dens, lhs, tt1, tt2,
    send0, send1, recv0, recv1, rad_send, rad_recv, cols, pay, hit_db, hit_bd, seg_t, buf, ra,
    part, other, both, rb, g0, g2,
    small_sem, load_sem, vol_sem, dens_sem, lon_s0, lon_r0, lon_s1, lon_r1, rad_s, rad_r,
    ra_s, ra_r, swap_s, swap_r, rb_s, rb_r, g2_s, g2_r,
):
    rad, lon = lax.axis_index("rad"), lax.axis_index("lon")
    right, left = lax.rem(lon + 1, NLON), lax.rem(lon + NLON - 1, NLON)
    me_yx = rad * (NYX // NRAD) + lax.div(lon, NZC)
    me_zc = lax.rem(lon, NZC)

    x_at, z_at, core_at = lax.div(lon, NZC), lax.rem(lax.div(lon, 2), 4), lax.rem(lon, 2)

    def yx_peer(k):
        y, x = lax.rem(rad + k // 4, NRAD), lax.rem(x_at + k % 4, NYX // NRAD)
        return y * (NYX // NRAD) + x, (y, x * NZC + me_zc)

    def zc_peer(k):
        core = 1 - core_at if k % 2 else core_at
        i = lax.rem(z_at + k // 2, 4) * 2 + core
        return i, (rad, x_at * NZC + i)

    def hops(n):
        return min(n, 4 - n)

    yx_order = sorted(range(1, NYX), key=lambda k: -hops(k // 4) - hops(k % 4))
    zc_order = sorted(range(1, NZC), key=lambda k: -2 * hops(k // 2) - k % 2)

    small = [
        pltpu.make_async_copy(src, dst, small_sem.at[i])
        for i, (src, dst) in enumerate((
            (matrices_in, matrices), (speeds_in, speeds), (table_in, table),
            (targets_in, targets), (tiles_in, tiles),
            (injection, inj), (courant, cou), (weight, wei),
        ))
    ]
    for copy in small:
        copy.start()

    def load(b):
        return pltpu.make_async_copy(
            state.at[:, pl.ds(b * RB, RB)], cells.at[:, pl.ds(3 + b * RB, RB)], load_sem.at[b]
        )

    for b in [0, 1, NB - 1] + list(range(2, NB - 1)):
        load(b).start()
    vol_copy = pltpu.make_async_copy(volume, vol, vol_sem)
    vol_copy.start()
    dens_copy = pltpu.make_async_copy(phase, dens, dens_sem)
    dens_copy.start()

    barrier = pltpu.get_barrier_semaphore()

    def greet(device):
        pl.semaphore_signal(barrier, inc=1, device_id=device, device_id_type=MESH)

    greet((rad, right))
    greet((rad, left))
    for k in yx_order:
        greet(yx_peer(k)[1])
    for k in zc_order:
        greet(zc_peer(k)[1])

    cells[:, 0:3] = jnp.zeros((NF, 3, CL, CZ), F32)
    cells[:, 3 + CR :] = jnp.zeros((NF, 3, CL, CZ), F32)

    for copy in small:
        copy.wait()
    lane = lax.broadcasted_iota(jnp.int32, (CL, 128), 1)
    sub = lax.broadcasted_iota(jnp.int32, (CL, 128), 0)
    block = lax.shift_right_logical(lane, 4)
    same_l = jnp.bitwise_and(lane, CL - 1) == sub
    odd, even = table[C_ODD : C_ODD + CL].astype(F32), table[C_EVEN : C_EVEN + CL].astype(F32)
    rows_l = []
    zero = jnp.zeros((CL, 128), BF16)
    for f in range(NF):
        row_r = jnp.zeros((CL, 128), F32)
        row_l = jnp.zeros((CL, 128), F32)
        for g in range(NF):
            row_r = jnp.where(block == g, matrices[0, f, g], row_r)
            row_l = jnp.where(block == g, matrices[1, f, g], row_l)
        rows_l.append(row_l)
        eye = lane == sub + f * CL
        w = (
            (SCALE * speeds[1]) * jnp.where(block == f, even, 0.0)
            - SCALE * row_l * odd
            + jnp.where(eye, 1.0 - 20.0 * SCALE * speeds[0], 0.0)
        )
        whi, wlo = split(w)
        rhi, rlo = split(jnp.where(same_l, (-45.0 * SCALE) * row_r, 0.0))
        at = {0: 0, 7: CL}.get(f, (f - 1) * CL)
        h, l, hr, lr = (H_07, L_07, HR_07, LR_07) if f in (0, 7) else (H_16, L_16, HR_16, LR_16)
        for start, high, low in ((h, whi, None), (l, wlo, zero), (hr, rhi, None), (lr, rlo, zero)):
            lhs[start + at : start + at + CL, 0:128] = high
            lhs[start + at : start + at + CL, 128:256] = high if low is None else low
    q = lax.broadcasted_iota(jnp.int32, (24, 128), 0)
    row_e = jnp.zeros((24, 128), F32)
    for pos, f in enumerate(ORDER):
        wide = jnp.concatenate([rows_l[f][0:8]] * 3, axis=0)
        row_e = jnp.where((q >= 3 * pos) & (q < 3 * pos + 3), wide, row_e)
    row_e = jnp.concatenate([row_e, row_e], axis=0)
    we = (SCALE * speeds[1]) * table[C_EEVEN : C_EEVEN + 48].astype(F32) - (
        SCALE * row_e * table[C_EODD : C_EODD + 48].astype(F32)
    )
    ehi, elo = split(we)
    lhs[H_EDGE : H_EDGE + 48, 0:128] = ehi
    lhs[H_EDGE : H_EDGE + 48, 128:256] = ehi
    lhs[L_EDGE : L_EDGE + 48, 0:128] = elo
    lhs[L_EDGE : L_EDGE + 48, 128:256] = jnp.zeros((48, 128), BF16)

    def row(i):
        return cells[:, i].reshape(NF * CL, CZ)

    def rad_edge(side):
        radial = jnp.concatenate(
            [lhs[HR_07:LR_07], lhs[HR_16:LR_16], lhs[LR_07:H_16], lhs[LR_16:M_END]], axis=0
        )
        for k in range(3):
            d = jnp.zeros((128, CZ), F32)
            e = jnp.zeros((128, CZ), F32)
            for j in range(3):
                off = j - k - 3 if side == 0 else 3 + j - k
                if off in ODD:
                    u = row(CR + j if side == 0 else 3 + j)
                    d = d + (ODD[off] / 45.0) * u
                    e = e + EVEN[off] * u
            y = jnp.dot(
                radial, jnp.concatenate(split(d), axis=0), preferred_element_type=F32
            )
            y = y[0:128] + y[128:256]
            for pos, f in enumerate(ORDER):
                rad_send[side, pos, k] = y[pos * CL : (pos + 1) * CL] + (
                    SCALE * speeds[0]
                ) * e[f * CL : (f + 1) * CL]

    rad_parts = ((0, 2), (2, 3), (5, 3))

    def rad_copy(side, part_of):
        fields = pl.ds(*rad_parts[part_of])
        return pltpu.make_async_remote_copy(
            src_ref=rad_send.at[side, fields],
            dst_ref=rad_recv.at[side, fields],
            send_sem=rad_s.at[side, part_of],
            recv_sem=rad_r.at[side, part_of],
            device_id=(rad + 1 if side == 0 else rad - 1, lon),
            device_id_type=MESH,
        )

    def send_rad(part_of):
        for side in range(2):
            @pl.when(has[side])
            def _():
                rad_copy(side, part_of).start()

    has = (rad < NRAD - 1, rad > 0)

    def lon_copy(side, part, b):
        src, dst = (send0, recv0) if part == 0 else (send1, recv1)
        ss, rs = (lon_s0, lon_r0) if part == 0 else (lon_s1, lon_r1)
        rows = pl.ds(b * (RB // 4), RB // 4)
        return pltpu.make_async_remote_copy(
            src_ref=src.at[side, rows],
            dst_ref=dst.at[side, rows],
            send_sem=ss.at[side, b],
            recv_sem=rs.at[side, b],
            device_id=(rad, right if side == 0 else left),
            device_id_type=MESH,
        )

    first_eight = lax.broadcasted_iota(jnp.int32, (8, CZ), 0)

    def pick(n, a, b):
        return jnp.where(first_eight < n, a, b)

    def lon_pass(b):
        tops = ([], [])
        for i in range(RB):
            r = b * RB + i
            t1 = jnp.concatenate(split(row(r + 3)), axis=0)
            tt1[r] = t1
            y = jnp.dot(lhs[H_07:HR_07], t1, preferred_element_type=F32)
            new = y[0:32] + y[32:64]
            out[0, r] = new[0:CL]
            out[7, r] = new[CL:]
            edge = y[64:112] + y[112:160]
            g, j = b * (RB // 4) + i // 4, i % 4
            for side in range(2):
                tops[side].append(edge[side * 24 : side * 24 + 8])
                send1[side, g, j * 16 : (j + 1) * 16] = edge[side * 24 + 8 : side * 24 + 24]
        for h in range(RB // 4):
            g = b * (RB // 4) + h
            for side in range(2):
                z0, z1, z2, z3 = tops[side][4 * h : 4 * h + 4]
                a, b1, c = (
                    pltpu.roll(z1, 6, axis=0), pltpu.roll(z2, 4, axis=0), pltpu.roll(z3, 2, axis=0)
                )
                send0[side, g, 0:8] = pick(6, z0, a)
                send0[side, g, 8:16] = pick(4, a, b1)
                send0[side, g, 16:24] = pick(2, b1, c)
                a, b1, c = (
                    pltpu.roll(z0, 2, axis=0), pltpu.roll(z1, 4, axis=0), pltpu.roll(z2, 6, axis=0)
                )
                send1[side, g, 64:72] = pick(2, a, pick(4, b1, pick(6, c, z3)))

    def rad_pass(b, _):
        for i in range(RB):
            r = b * RB + i
            m3, m2, m1, p1, p2, p3 = (row(r + n) for n in (0, 1, 2, 4, 5, 6))
            d = (p1 - m1) - 0.2 * ((p2 - m2) - (1.0 / 9.0) * (p3 - m3))
            m3, m2, m1, p1, p2, p3 = (
                jnp.concatenate([x[0:CL], x[112:128]], axis=0) for x in (m3, m2, m1, p1, p2, p3)
            )
            e = (p1 + m1) - 0.4 * ((p2 + m2) - (1.0 / 6.0) * (p3 + m3))
            t2 = jnp.concatenate(split(d), axis=0)
            tt2[r] = t2
            y = jnp.dot(lhs[HR_07:H_16], t2, preferred_element_type=F32)
            new = (y[0:32] + y[32:64]) + (15.0 * SCALE * speeds[0]) * e
            out[0, r] = out[0, r] + new[0:CL]
            out[7, r] = out[7, r] + new[CL:]
        return 0

    def second_pass(g, _):
        for i in range(4):
            r = 4 * g + i
            m3, m2, m1, p1, p2, p3 = (
                cells[1:7, r + n].reshape(96, CZ) for n in (0, 1, 2, 4, 5, 6)
            )
            e = (p1 + m1) - 0.4 * ((p2 + m2) - (1.0 / 6.0) * (p3 + m3))
            y1 = jnp.dot(lhs[H_16:HR_16], tt1[r], preferred_element_type=F32)
            y2 = jnp.dot(lhs[HR_16:M_END], tt2[r], preferred_element_type=F32)
            new = (y1[0:96] + y1[96:192] + y2[0:96] + y2[96:192]) + (
                15.0 * SCALE * speeds[0]
            ) * e
            out[1:7, r] = new.reshape(6, CL, CZ)
        return 0

    def send_early(b):
        lon_copy(0, 0, b).start()
        lon_copy(1, 0, b).start()

    def send_late(b, _):
        lon_copy(0, 1, b).start()
        lon_copy(1, 1, b).start()
        return 0

    load(0).wait()
    lon_pass(0)
    pl.semaphore_wait(barrier, 2 + NYX - 1 + NZC - 1)
    send_early(0)
    load(1).wait()
    lon_pass(1)
    send_early(1)
    load(NB - 1).wait()
    rad_edge(0)
    rad_edge(1)
    send_rad(0)
    send_rad(1)

    def rest(b, _):
        @pl.when(b < NB - 1)
        def _():
            load(b).wait()

        lon_pass(b)
        send_early(b)
        return 0

    lax.fori_loop(2, NB, rest, 0)
    lax.fori_loop(SENDS[0], SENDS[1], send_late, 0)
    tile_col = jnp.broadcast_to(tiles[...].astype(F32), (DEVICES, DEVICES)).T
    target_row = jnp.broadcast_to(targets[...].astype(F32), (DEVICES, CR))
    hit = (tile_col[:, 0:CR] == target_row).astype(BF16)
    spread = lax.shift_right_logical(
        lax.broadcasted_iota(jnp.int32, (CR, CR * 8), 1), 3
    ) == lax.broadcasted_iota(jnp.int32, (CR, CR * 8), 0)
    hit_db[...] = jnp.dot(
        hit, spread.astype(F32).astype(BF16), preferred_element_type=F32
    ).astype(BF16)
    target_col = jnp.concatenate(
        [target_row, jnp.zeros((DEVICES, DEVICES - CR), F32)], axis=1
    ).T
    hit_bd[...] = (target_col[0:CR] == tiles[...].astype(F32)).astype(F32).astype(BF16)

    seg_t[...] = (
        jnp.bitwise_and(lax.broadcasted_iota(jnp.int32, (2 * TP, CZ), 0), ZSEG - 1)
        == lax.shift_right_logical(lax.broadcasted_iota(jnp.int32, (2 * TP, CZ), 1), 5)
    ).astype(F32).astype(BF16)

    lax.fori_loop(0, NB, rad_pass, 0)

    def add_rad(part_of):
        for side in range(2):
            @pl.when(has[1 - side])
            def _():
                rad_copy(side, part_of).wait_recv()
                for pos in range(rad_parts[part_of][0], sum(rad_parts[part_of])):
                    for k in range(3):
                        r = k if side == 0 else CR - 3 + k
                        out[ORDER[pos], r] = out[ORDER[pos], r] + rad_recv[side, pos, k]

    add_rad(0)
    vol_copy.wait()
    seg = table[C_SEG : C_SEG + CZ]
    mask = table[C_MASK : C_MASK + CL].astype(F32)

    def early(b, _):
        for i in range(2):
            lon_copy(0, 0, 2 * b + i).wait_recv()
            lon_copy(1, 0, 2 * b + i).wait_recv()
        highs, lows = [], []
        for h in range(4):
            g = b * 4 + h
            got = jnp.concatenate(
                [recv0[0, g], recv0[1, g], jnp.zeros((16, CZ), F32)], axis=0
            )
            add = jnp.dot(
                table[C_FIX07 : C_FIX07 + 128],
                jnp.concatenate(split(got), axis=0),
                preferred_element_type=F32,
            )
            v = vol[pl.ds(4 * g, 4)].reshape(64, CZ)
            for c, f in enumerate((0, 7)):
                new = out[f, pl.ds(4 * g, 4)].reshape(64, CZ) + add[c * 64 : (c + 1) * 64]
                out[f, pl.ds(4 * g, 4)] = new.reshape(4, CL, CZ)
                yh, yl = split(v * new)
                highs.append(yh)
                lows.append(yl)
        t = jnp.dot(jnp.concatenate(highs + lows, axis=0), seg, preferred_element_type=F32)
        t = t[0:512] + t[512:1024]
        for h in range(4):
            for c in range(2):
                at = (h * 2 + c) * 64
                x = t[at : at + 64].reshape(4, CL, TP) * mask[None]
                pay[pl.ds(b * 128 + h * 32, 32), c * TP : (c + 1) * TP] = (
                    x[:, 0:8] + x[:, 8:16]
                ).reshape(32, TP)
        return 0

    lax.fori_loop(0, NB // 2, early, 0)

    pay_hi, pay_lo = split(pay[...])
    buf[...] = (
        jnp.dot(hit_db[...], pay_hi, preferred_element_type=F32)
        + jnp.dot(hit_db[...], pay_lo, preferred_element_type=F32)
    ).reshape(NYX, NZC, 2 * TP)

    def ra_copy(k):
        a, device = yx_peer(k)
        return pltpu.make_async_remote_copy(
            src_ref=buf.at[a], dst_ref=ra.at[k], send_sem=ra_s.at[k], recv_sem=ra_r.at[k],
            device_id=device, device_id_type=MESH,
        )

    def swap_copy():
        return pltpu.make_async_remote_copy(
            src_ref=part, dst_ref=other, send_sem=swap_s, recv_sem=swap_r,
            device_id=(rad, lon + 1 - 2 * core_at), device_id_type=MESH,
        )

    def z_copy(n, core):
        return pltpu.make_async_remote_copy(
            src_ref=both, dst_ref=rb.at[z_at], send_sem=rb_s.at[n, core], recv_sem=rb_r.at[n],
            device_id=(rad, x_at * NZC + lax.rem(z_at + n, 4) * 2 + core), device_id_type=MESH,
        )

    def each_z(act):
        for sender in range(2):
            @pl.when(core_at == sender)
            def _():
                for n in (2, 1, 3):
                    if sender == {1: 0, 2: TWO, 3: 1}[n]:
                        for core in range(2):
                            act(z_copy(n, core))

    def g2_copy(k):
        a, device = yx_peer(k)
        return pltpu.make_async_remote_copy(
            src_ref=g0, dst_ref=g2.at[me_yx], send_sem=g2_s.at[k], recv_sem=g2_r.at[k],
            device_id=device, device_id_type=MESH,
        )

    def late(b, _):
        lon_copy(0, 1, b).wait_recv()
        lon_copy(1, 1, b).wait_recv()

        def late_row(i, _):
            r = b * RB + i
            got = jnp.concatenate(
                [recv0[0, r], recv1[0, r], recv0[1, r], recv1[1, r], jnp.zeros((16, CZ), F32)],
                axis=0,
            )
            hi, lo = split(got)
            add = jnp.dot(
                table[C_FIX : C_FIX + 96],
                jnp.concatenate([hi, lo], axis=0),
                preferred_element_type=F32,
            )
            out[1:7, r] = out[1:7, r] + add.reshape(6, CL, CZ)
            return 0

        lax.fori_loop(0, RB, late_row, 0, unroll=8)
        return 0

    def late(b, _):
        lon_copy(0, 1, b).wait_recv()
        lon_copy(1, 1, b).wait_recv()
        for h in range(RB // 4):
            g = b * (RB // 4) + h
            tail = [recv1[0, g, 64:72], recv1[1, g, 64:72], jnp.zeros((16, CZ), F32)]
            for i in range(4):
                got = jnp.concatenate(
                    [recv1[side, g, i * 16 : (i + 1) * 16] for side in range(2)] + tail, axis=0
                )
                add = jnp.dot(
                    table[C_FIX + i * 96 : C_FIX + (i + 1) * 96],
                    jnp.concatenate(split(got), axis=0),
                    preferred_element_type=F32,
                )
                r = 4 * g + i
                out[1:7, r] = out[1:7, r] + add.reshape(6, CL, CZ)
        return 0

    for k in yx_order:
        ra_copy(k).start()
    lax.fori_loop(SENDS[1], SENDS[2], send_late, 0)
    send_rad(2)

    lax.fori_loop(0, PASS[0], second_pass, 0)
    cols[...] = jnp.zeros((8, 256), F32)
    cols[0:2, 0:CH] = inj[...]
    cols[2:3, 0:CH] = cou[...]
    cols[3:4, 0:CH] = wei[...]
    columns = cols[...].T
    channel_rate = jnp.broadcast_to(columns[0:CH, 2:3], (CH, TP))
    channel_weight = jnp.broadcast_to(columns[0:CH, 3:4], (CH, TP))

    def drift(density):
        for _ in range(DRIFT):
            density = density - channel_rate * (density - pltpu.roll(density, 1, axis=1))
        return density

    dens_copy.wait()
    bare = jnp.sum(channel_weight * drift(dens[...]), axis=0, keepdims=True)

    rate_row, weight_row = cols[2:3], cols[3:4]
    keep = 1.0 - rate_row
    powers = (
        keep * keep * keep,
        3.0 * keep * keep * rate_row,
        3.0 * keep * rate_row * rate_row,
        rate_row * rate_row * rate_row,
    )
    taps = [
        [
            jnp.sum(0.5 * weight_row * cols[i : i + 1] * power, axis=1, keepdims=True)
            for power in powers
        ]
        for i in range(2)
    ]

    total = buf[me_yx]
    for k in range(1, NYX):
        ra_copy(k).wait_recv()
        total = total + ra[k]
    part[:, 0 : 2 * TP] = total
    part[:, 2 * TP :] = jnp.broadcast_to(bare, (NZC, TP))
    swap_copy().start()
    swap_copy().wait_recv()
    both[:, 0 : 2 * TP] = part[:, 0 : 2 * TP] + other[:, 0 : 2 * TP]
    first = core_at == 0
    both[:, 2 * TP : 3 * TP] = jnp.where(first, part[:, 2 * TP :], other[:, 2 * TP :])
    both[:, 3 * TP :] = jnp.where(first, other[:, 2 * TP :], part[:, 2 * TP :])
    each_z(lambda copy: copy.start())
    lax.fori_loop(SENDS[2], SENDS[3], send_late, 0)
    lax.fori_loop(PASS[0], CR // 4, second_pass, 0)
    add_rad(1)
    lax.fori_loop(0, LATE[0], late, 0)
    rb[z_at] = both[...]
    for n in (1, 2, 3):
        z_copy(n, 0).wait_recv()
    source = rb[0, :, 0 : 2 * TP]
    for j in range(1, 4):
        source = source + rb[j, :, 0 : 2 * TP]
    tile_row = lax.broadcasted_iota(jnp.int32, (NZC, TP), 0)
    pressure = jnp.zeros((NZC, TP), F32)
    for j in range(NZC):
        at = (2 + j % 2) * TP
        pressure = jnp.where(tile_row == j, rb[j // 2, :, at : at + TP], pressure)
    for i in range(2):
        s = source[:, i * TP : (i + 1) * TP]
        for n in range(4):
            pressure = pressure + taps[i][n] * (pltpu.roll(s, n, axis=1) if n else s)
    g0[...] = pressure
    for k in yx_order:
        g2_copy(k).start()
    lax.fori_loop(SENDS[3], SENDS[4], send_late, 0)
    g2[me_yx] = pressure

    own = lax.broadcasted_iota(jnp.int32, (NZC, 2 * TP), 0) == me_zc
    mine = jnp.sum(jnp.where(own, source, 0.0), axis=0, keepdims=True)
    drifted[...] = drift(
        dens[...]
        + 0.5 * (columns[0:CH, 0:1] * mine[:, 0:TP] + columns[0:CH, 1:2] * mine[:, TP:])
    )
    add_rad(2)
    lax.fori_loop(LATE[0], LATE[1], late, 0)

    def sent(b, _):
        for side in range(2):
            for part in range(2):
                lon_copy(side, part, b).wait_send()
        return 0

    lax.fori_loop(0, NB, sent, 0)
    for side in range(2):
        @pl.when(has[side])
        def _():
            for part_of in range(3):
                rad_copy(side, part_of).wait_send()
    for k in range(1, NYX):
        ra_copy(k).wait_send()
    swap_copy().wait_send()
    each_z(lambda copy: copy.wait_send())

    for k in range(1, NYX):
        g2_copy(k).wait_recv()
    back_hi, back_lo = split(g2[...].reshape(DEVICES, TP))
    pay[0:CR, 0:TP] = jnp.dot(hit_bd[...], back_hi, preferred_element_type=F32) + jnp.dot(
        hit_bd[...], back_lo, preferred_element_type=F32
    )

    def nudge(b, _):
        got = pay[pl.ds(b * 16, 16), 0:TP]
        wide = jnp.broadcast_to(got[:, None, :], (16, CL, TP)) * mask[None]
        back = jnp.dot(
            jnp.concatenate(split(wide.reshape(16 * CL, TP)), axis=1),
            seg_t[...],
            preferred_element_type=F32,
        )
        old = out[7, pl.ds(b * 16, 16)].reshape(16 * CL, CZ)
        out[7, pl.ds(b * 16, 16)] = (old + 0.5 * (back - old)).reshape(16, CL, CZ)
        return 0

    lax.fori_loop(0, CR // 16, nudge, 0, unroll=4)

    for k in range(1, NYX):
        g2_copy(k).wait_send()


def finish(fields, density, fields_out, density_out, sem):
    copies = [
        pltpu.make_async_copy(fields.at[f], fields_out.at[f], sem.at[f]) for f in range(NF)
    ] + [pltpu.make_async_copy(density, density_out, sem.at[NF])]
    for copy in copies:
        copy.start()
    for copy in copies:
        copy.wait()


def per_device(
    state, flux_matrices, wave_speed, flux_volume, block_tile, tile_of_device,
    phase_density, injection, drift_courant, energy_weight,
):
    hbm = pl.BlockSpec(memory_space=pltpu.HBM)
    vmem = pl.BlockSpec(memory_space=pltpu.VMEM)
    dma = pltpu.SemaphoreType.DMA
    coupled, drifted = pl.pallas_call(
        kernel,
        out_shape=(
            pltpu.VMEM((NF, CR, CL, CZ), F32),
            pltpu.VMEM((CH, TP), F32),
        ),
        in_specs=[hbm] * 11,
        out_specs=(vmem, vmem),
        scratch_shapes=[
            pltpu.SMEM((2, NF, NF), F32),
            pltpu.SMEM((2,), F32),
            pltpu.VMEM((1, CR), jnp.int32),
            pltpu.VMEM((1, DEVICES), jnp.int32),
            pltpu.VMEM((C_END, 128), BF16),
            pltpu.VMEM((2, CH), F32),
            pltpu.VMEM((1, CH), F32),
            pltpu.VMEM((1, CH), F32),
            pltpu.VMEM((NF, CR + 6, CL, CZ), F32),
            pltpu.VMEM((CR, CL, CZ), F32),
            pltpu.VMEM((CH, TP), F32),
            pltpu.VMEM((M_END, 256), BF16),
            pltpu.VMEM((CR, 256, CZ), BF16),
            pltpu.VMEM((CR, 256, CZ), BF16),
            pltpu.VMEM((2, CR // 4, 24, CZ), F32),
            pltpu.VMEM((2, CR // 4, 72, CZ), F32),
            pltpu.VMEM((2, CR // 4, 24, CZ), F32),
            pltpu.VMEM((2, CR // 4, 72, CZ), F32),
            pltpu.VMEM((2, NF, 3, CL, CZ), F32),
            pltpu.VMEM((2, NF, 3, CL, CZ), F32),
            pltpu.VMEM((8, 256), F32),
            pltpu.VMEM((CR * 8, 2 * TP), F32),
            pltpu.VMEM((DEVICES, CR * 8), BF16),
            pltpu.VMEM((CR, DEVICES), BF16),
            pltpu.VMEM((2 * TP, CZ), BF16),
            pltpu.VMEM((NYX, NZC, 2 * TP), F32),
            pltpu.VMEM((NYX, NZC, 2 * TP), F32),
            pltpu.VMEM((NZC, 3 * TP), F32),
            pltpu.VMEM((NZC, 3 * TP), F32),
            pltpu.VMEM((NZC, 4 * TP), F32),
            pltpu.VMEM((4, NZC, 4 * TP), F32),
            pltpu.VMEM((NZC, TP), F32),
            pltpu.VMEM((NYX, NZC, TP), F32),
            dma((8,)), dma((NB,)), dma, dma,
            dma((2, NB)), dma((2, NB)), dma((2, NB)), dma((2, NB)),
            dma((2, 3)), dma((2, 3)), dma((NYX,)), dma((NYX,)),
            dma, dma, dma((4, 2)), dma((4,)), dma((NYX,)), dma((NYX,)),
        ],
        compiler_params=pltpu.CompilerParams(
            collective_id=0, has_side_effects=True, vmem_limit_bytes=54 << 20
        ),
    )(
        state,
        flux_volume,
        phase_density.reshape(CH, TP),
        flux_matrices,
        wave_speed,
        block_tile.reshape(1, CR),
        tile_of_device.reshape(1, DEVICES),
        injection,
        drift_courant.reshape(1, CH),
        energy_weight.reshape(1, CH),
        jnp.asarray(constants()),
    )
    coupled, drifted = pl.pallas_call(
        finish,
        out_shape=(
            jax.ShapeDtypeStruct((NF, CR, CL, CZ), F32),
            jax.ShapeDtypeStruct((CH, TP), F32),
        ),
        in_specs=[vmem, vmem],
        out_specs=(hbm, hbm),
        scratch_shapes=[dma((NF + 1,))],
        compiler_params=pltpu.CompilerParams(vmem_limit_bytes=1 << 20),
    )(coupled, drifted)
    return coupled, drifted[None]


def solution(mesh):
    in_specs = (
        P(None, "rad", "lon", None),
        P(),
        P(),
        P("rad", "lon", None),
        P("lon", "rad", None),
        P(),
        P(("rad", "lon"), None, None),
        P(),
        P(),
        P(),
    )
    out_specs = (P(None, "rad", "lon", None), P(("rad", "lon"), None, None))
    return jax.shard_map(
        per_device, mesh=mesh, in_specs=in_specs, out_specs=out_specs, check_vma=False
    )
```

```python
import numpy as np

import jax
import jax.numpy as jnp
import ml_dtypes
from jax import lax
from jax.experimental import pallas as pl
from jax.experimental.pallas import tpu as pltpu
from jax.sharding import PartitionSpec as P

F32 = jnp.float32
BF16 = jnp.bfloat16
HIGHEST = lax.Precision.HIGHEST
MESH = pl.DeviceIdType.MESH

NF, CR, CL, CZ = 8, 64, 16, 256
ZSEG = 8
DRIFT = 3
CH, TP = 200, 128
NRAD, NLON = 4, 32
NYX, NZC = 16, 8
DEVICES = NRAD * NLON

SCALE = 0.4 * 0.5 / 30.0
ORDER = (0, 7, 1, 2, 3, 4, 5, 6)
ODD = {-3: -1.0, -2: 9.0, -1: -45.0, 1: 45.0, 2: -9.0, 3: 1.0}
EVEN = {-3: 1.0, -2: -6.0, -1: 15.0, 0: -20.0, 1: 15.0, 2: -6.0, 3: 1.0}

RB = 8
NB = CR // RB
SENDS = (0, 4, 7, 7, NB)
PASS = (10,)
TWO = 0
LATE = (4, NB)

C_FIX07, C_FIX, C_SEG, C_MASK, C_ODD, C_EVEN, C_EODD, C_EEVEN, C_END = (
    0, 128, 512, 768, 784, 800, 816, 864, 912
)
H_07, L_07, H_EDGE, L_EDGE, HR_07, LR_07, H_16, L_16, HR_16, LR_16, M_END = (
    0, 32, 64, 112, 160, 192, 224, 320, 416, 512, 608
)


def constants():
    t = np.zeros((C_END, 128), np.float32)
    half = 64
    for c in range(2):
        for r in range(4):
            for l in range(CL):
                row = C_FIX07 + (c * 4 + r) * CL + l
                for h in range(2):
                    if l < 3:
                        t[row, h * half + r * 6 + 3 * c + l] = 1
                    if l >= CL - 3:
                        t[row, h * half + 24 + r * 6 + 3 * c + l - (CL - 3)] = 1
    for r in range(4):
        for pos in range(2, NF):
            for l in range(CL):
                row = C_FIX + r * 96 + (pos - 2) * CL + l
                side = 0 if l < 3 else 1
                k = l if l < 3 else l - (CL - 3)
                if 0 <= k < 3:
                    q = 3 * pos + k
                    at = side * 16 + q - 8 if q >= 8 else 32 + side * 8 + r * 2 + q - 6
                    for h in range(2):
                        t[row, h * half + at] = 1
    for z in range(CZ):
        for p in range(TP):
            t[C_SEG + z, p] = z // (CZ // ZSEG) == p % ZSEG
    for l in range(CL):
        for p in range(TP):
            t[C_MASK + l, p] = p // ZSEG == l
    for l in range(CL):
        for f in range(NF):
            for j in range(CL):
                t[C_ODD + l, f * CL + j] = ODD.get(j - l, 0.0)
                t[C_EVEN + l, f * CL + j] = EVEN.get(j - l, 0.0)
    for side in range(2):
        for pos in range(NF):
            for k in range(3):
                row = side * 24 + 3 * pos + k
                for f in range(NF):
                    for j in range(CL):
                        off = j - CL - k if side == 0 else 3 + j - k
                        t[C_EODD + row, f * CL + j] = ODD.get(off, 0.0)
                        if f == ORDER[pos]:
                            t[C_EEVEN + row, f * CL + j] = EVEN.get(off, 0.0)
    return t.astype(ml_dtypes.bfloat16)


def split(x):
    hi = x.astype(BF16)
    return hi, (x - hi.astype(F32)).astype(BF16)


def kernel(
    state, volume, phase, matrices_in, speeds_in, targets_in, tiles_in, injection, courant, weight,
    table_in,
    out, drifted,
    matrices, speeds, targets, tiles, table, inj, cou, wei, cells, vol, dens, lhs, tt1, tt2,
    send0, send1, recv0, recv1, rad_send, rad_recv, cols, pay, hit_db, hit_bd, seg_t, buf, ra,
    part, other, both, rb, g0, g2,
    lines, small_sem, load_sem, vol_sem, dens_sem, lon_s0, lon_r0, lon_s1, lon_r1, rad_s, rad_r,
    ra_s, ra_r, swap_s, swap_r, rb_s, rb_r, g2_s, g2_r,
):
    rad, lon = lax.axis_index("rad"), lax.axis_index("lon")
    right, left = lax.rem(lon + 1, NLON), lax.rem(lon + NLON - 1, NLON)
    me_yx = rad * (NYX // NRAD) + lax.div(lon, NZC)
    me_zc = lax.rem(lon, NZC)

    x_at, z_at, core_at = lax.div(lon, NZC), lax.rem(lax.div(lon, 2), 4), lax.rem(lon, 2)

    def yx_peer(k):
        y, x = lax.rem(rad + k // 4, NRAD), lax.rem(x_at + k % 4, NYX // NRAD)
        return y * (NYX // NRAD) + x, (y, x * NZC + me_zc)

    def zc_peer(k):
        core = 1 - core_at if k % 2 else core_at
        i = lax.rem(z_at + k // 2, 4) * 2 + core
        return i, (rad, x_at * NZC + i)

    def hops(n):
        return min(n, 4 - n)

    yx_order = sorted(range(1, NYX), key=lambda k: -hops(k // 4) - hops(k % 4))
    zc_order = sorted(range(1, NZC), key=lambda k: -2 * hops(k // 2) - k % 2)

    small = [
        pltpu.make_async_copy(src, dst, small_sem.at[i])
        for i, (src, dst) in enumerate((
            (matrices_in, matrices), (speeds_in, speeds), (table_in, table),
            (targets_in, targets), (tiles_in, tiles),
            (injection, inj), (courant, cou), (weight, wei),
        ))
    ]
    for copy in small:
        copy.start()

    def load(b):
        return pltpu.make_async_copy(
            state.at[:, pl.ds(b * RB, RB)], cells.at[:, pl.ds(3 + b * RB, RB)], load_sem.at[b]
        )

    for b in [0, 1, NB - 1] + list(range(2, NB - 1)):
        load(b).start()
    vol_copy = pltpu.make_async_copy(volume, vol, vol_sem)
    vol_copy.start()
    dens_copy = pltpu.make_async_copy(phase, dens, dens_sem)
    dens_copy.start()

    barrier = pltpu.get_barrier_semaphore()

    def greet(device):
        pl.semaphore_signal(barrier, inc=1, device_id=device, device_id_type=MESH)

    greet((rad, right))
    greet((rad, left))
    for k in (2, 1, 3):
        greet(yx_peer(4 * k)[1])
        greet(yx_peer(k)[1])
        greet(zc_peer(2 * k)[1])
    greet(zc_peer(1)[1])

    def pass_on(device):
        pl.semaphore_signal(lines, inc=1, device_id=device, device_id_type=MESH)

    cells[:, 0:3] = jnp.zeros((NF, 3, CL, CZ), F32)
    cells[:, 3 + CR :] = jnp.zeros((NF, 3, CL, CZ), F32)

    for copy in small:
        copy.wait()
    lane = lax.broadcasted_iota(jnp.int32, (CL, 128), 1)
    sub = lax.broadcasted_iota(jnp.int32, (CL, 128), 0)
    block = lax.shift_right_logical(lane, 4)
    same_l = jnp.bitwise_and(lane, CL - 1) == sub
    odd, even = table[C_ODD : C_ODD + CL].astype(F32), table[C_EVEN : C_EVEN + CL].astype(F32)
    rows_l = []
    zero = jnp.zeros((CL, 128), BF16)
    for f in range(NF):
        row_r = jnp.zeros((CL, 128), F32)
        row_l = jnp.zeros((CL, 128), F32)
        for g in range(NF):
            row_r = jnp.where(block == g, matrices[0, f, g], row_r)
            row_l = jnp.where(block == g, matrices[1, f, g], row_l)
        rows_l.append(row_l)
        eye = lane == sub + f * CL
        w = (
            (SCALE * speeds[1]) * jnp.where(block == f, even, 0.0)
            - SCALE * row_l * odd
            + jnp.where(eye, 1.0 - 20.0 * SCALE * speeds[0], 0.0)
        )
        whi, wlo = split(w)
        rhi, rlo = split(jnp.where(same_l, (-45.0 * SCALE) * row_r, 0.0))
        at = {0: 0, 7: CL}.get(f, (f - 1) * CL)
        h, l, hr, lr = (H_07, L_07, HR_07, LR_07) if f in (0, 7) else (H_16, L_16, HR_16, LR_16)
        for start, high, low in ((h, whi, None), (l, wlo, zero), (hr, rhi, None), (lr, rlo, zero)):
            lhs[start + at : start + at + CL, 0:128] = high
            lhs[start + at : start + at + CL, 128:256] = high if low is None else low
    q = lax.broadcasted_iota(jnp.int32, (24, 128), 0)
    row_e = jnp.zeros((24, 128), F32)
    for pos, f in enumerate(ORDER):
        wide = jnp.concatenate([rows_l[f][0:8]] * 3, axis=0)
        row_e = jnp.where((q >= 3 * pos) & (q < 3 * pos + 3), wide, row_e)
    row_e = jnp.concatenate([row_e, row_e], axis=0)
    we = (SCALE * speeds[1]) * table[C_EEVEN : C_EEVEN + 48].astype(F32) - (
        SCALE * row_e * table[C_EODD : C_EODD + 48].astype(F32)
    )
    ehi, elo = split(we)
    lhs[H_EDGE : H_EDGE + 48, 0:128] = ehi
    lhs[H_EDGE : H_EDGE + 48, 128:256] = ehi
    lhs[L_EDGE : L_EDGE + 48, 0:128] = elo
    lhs[L_EDGE : L_EDGE + 48, 128:256] = jnp.zeros((48, 128), BF16)

    def row(i):
        return cells[:, i].reshape(NF * CL, CZ)

    def rad_edge(side):
        radial = jnp.concatenate(
            [lhs[HR_07:LR_07], lhs[HR_16:LR_16], lhs[LR_07:H_16], lhs[LR_16:M_END]], axis=0
        )
        for k in range(3):
            d = jnp.zeros((128, CZ), F32)
            e = jnp.zeros((128, CZ), F32)
            for j in range(3):
                off = j - k - 3 if side == 0 else 3 + j - k
                if off in ODD:
                    u = row(CR + j if side == 0 else 3 + j)
                    d = d + (ODD[off] / 45.0) * u
                    e = e + EVEN[off] * u
            y = jnp.dot(
                radial, jnp.concatenate(split(d), axis=0), preferred_element_type=F32
            )
            y = y[0:128] + y[128:256]
            for pos, f in enumerate(ORDER):
                rad_send[side, pos, k] = y[pos * CL : (pos + 1) * CL] + (
                    SCALE * speeds[0]
                ) * e[f * CL : (f + 1) * CL]

    rad_parts = ((0, 2), (2, 3), (5, 3))

    def rad_copy(side, part_of):
        fields = pl.ds(*rad_parts[part_of])
        return pltpu.make_async_remote_copy(
            src_ref=rad_send.at[side, fields],
            dst_ref=rad_recv.at[side, fields],
            send_sem=rad_s.at[side, part_of],
            recv_sem=rad_r.at[side, part_of],
            device_id=(rad + 1 if side == 0 else rad - 1, lon),
            device_id_type=MESH,
        )

    def send_rad(part_of):
        for side in range(2):
            @pl.when(has[side])
            def _():
                rad_copy(side, part_of).start()

    has = (rad < NRAD - 1, rad > 0)

    def lon_copy(side, part, b):
        src, dst = (send0, recv0) if part == 0 else (send1, recv1)
        ss, rs = (lon_s0, lon_r0) if part == 0 else (lon_s1, lon_r1)
        rows = pl.ds(b * (RB // 4), RB // 4)
        return pltpu.make_async_remote_copy(
            src_ref=src.at[side, rows],
            dst_ref=dst.at[side, rows],
            send_sem=ss.at[side, b],
            recv_sem=rs.at[side, b],
            device_id=(rad, right if side == 0 else left),
            device_id_type=MESH,
        )

    first_eight = lax.broadcasted_iota(jnp.int32, (8, CZ), 0)

    def pick(n, a, b):
        return jnp.where(first_eight < n, a, b)

    def lon_pass(b):
        tops = ([], [])
        for i in range(RB):
            r = b * RB + i
            t1 = jnp.concatenate(split(row(r + 3)), axis=0)
            tt1[r] = t1
            y = jnp.dot(lhs[H_07:HR_07], t1, preferred_element_type=F32)
            new = y[0:32] + y[32:64]
            out[0, r] = new[0:CL]
            out[7, r] = new[CL:]
            edge = y[64:112] + y[112:160]
            g, j = b * (RB // 4) + i // 4, i % 4
            for side in range(2):
                tops[side].append(edge[side * 24 : side * 24 + 8])
                send1[side, g, j * 16 : (j + 1) * 16] = edge[side * 24 + 8 : side * 24 + 24]
        for h in range(RB // 4):
            g = b * (RB // 4) + h
            for side in range(2):
                z0, z1, z2, z3 = tops[side][4 * h : 4 * h + 4]
                a, b1, c = (
                    pltpu.roll(z1, 6, axis=0), pltpu.roll(z2, 4, axis=0), pltpu.roll(z3, 2, axis=0)
                )
                send0[side, g, 0:8] = pick(6, z0, a)
                send0[side, g, 8:16] = pick(4, a, b1)
                send0[side, g, 16:24] = pick(2, b1, c)
                a, b1, c = (
                    pltpu.roll(z0, 2, axis=0), pltpu.roll(z1, 4, axis=0), pltpu.roll(z2, 6, axis=0)
                )
                send1[side, g, 64:72] = pick(2, a, pick(4, b1, pick(6, c, z3)))

    def rad_pass(b, _):
        for i in range(RB):
            r = b * RB + i
            m3, m2, m1, p1, p2, p3 = (row(r + n) for n in (0, 1, 2, 4, 5, 6))
            d = (p1 - m1) - 0.2 * ((p2 - m2) - (1.0 / 9.0) * (p3 - m3))
            m3, m2, m1, p1, p2, p3 = (
                jnp.concatenate([x[0:CL], x[112:128]], axis=0) for x in (m3, m2, m1, p1, p2, p3)
            )
            e = (p1 + m1) - 0.4 * ((p2 + m2) - (1.0 / 6.0) * (p3 + m3))
            t2 = jnp.concatenate(split(d), axis=0)
            tt2[r] = t2
            y = jnp.dot(lhs[HR_07:H_16], t2, preferred_element_type=F32)
            new = (y[0:32] + y[32:64]) + (15.0 * SCALE * speeds[0]) * e
            out[0, r] = out[0, r] + new[0:CL]
            out[7, r] = out[7, r] + new[CL:]
        return 0

    def second_pass(g, _):
        for i in range(4):
            r = 4 * g + i
            m3, m2, m1, p1, p2, p3 = (
                cells[1:7, r + n].reshape(96, CZ) for n in (0, 1, 2, 4, 5, 6)
            )
            e = (p1 + m1) - 0.4 * ((p2 + m2) - (1.0 / 6.0) * (p3 + m3))
            y1 = jnp.dot(lhs[H_16:HR_16], tt1[r], preferred_element_type=F32)
            y2 = jnp.dot(lhs[HR_16:M_END], tt2[r], preferred_element_type=F32)
            new = (y1[0:96] + y1[96:192] + y2[0:96] + y2[96:192]) + (
                15.0 * SCALE * speeds[0]
            ) * e
            out[1:7, r] = new.reshape(6, CL, CZ)
        return 0

    def send_early(b):
        lon_copy(0, 0, b).start()
        lon_copy(1, 0, b).start()

    def send_late(b, _):
        lon_copy(0, 1, b).start()
        lon_copy(1, 1, b).start()
        return 0

    load(0).wait()
    lon_pass(0)
    pl.semaphore_wait(barrier, 12)
    send_early(0)
    for k in (1, 2, 3):
        pass_on(yx_peer(k)[1])
    pass_on(zc_peer(1)[1])
    load(1).wait()
    lon_pass(1)
    send_early(1)
    load(NB - 1).wait()
    rad_edge(0)
    rad_edge(1)
    send_rad(0)
    send_rad(1)

    def rest(b, _):
        @pl.when(b < NB - 1)
        def _():
            load(b).wait()

        lon_pass(b)
        send_early(b)
        return 0

    lax.fori_loop(2, NB, rest, 0)
    lax.fori_loop(SENDS[0], SENDS[1], send_late, 0)
    tile_col = jnp.broadcast_to(tiles[...].astype(F32), (DEVICES, DEVICES)).T
    target_row = jnp.broadcast_to(targets[...].astype(F32), (DEVICES, CR))
    hit = (tile_col[:, 0:CR] == target_row).astype(BF16)
    spread = lax.shift_right_logical(
        lax.broadcasted_iota(jnp.int32, (CR, CR * 8), 1), 3
    ) == lax.broadcasted_iota(jnp.int32, (CR, CR * 8), 0)
    hit_db[...] = jnp.dot(
        hit, spread.astype(F32).astype(BF16), preferred_element_type=F32
    ).astype(BF16)
    target_col = jnp.concatenate(
        [target_row, jnp.zeros((DEVICES, DEVICES - CR), F32)], axis=1
    ).T
    hit_bd[...] = (target_col[0:CR] == tiles[...].astype(F32)).astype(F32).astype(BF16)

    seg_t[...] = (
        jnp.bitwise_and(lax.broadcasted_iota(jnp.int32, (2 * TP, CZ), 0), ZSEG - 1)
        == lax.shift_right_logical(lax.broadcasted_iota(jnp.int32, (2 * TP, CZ), 1), 5)
    ).astype(F32).astype(BF16)

    lax.fori_loop(0, NB, rad_pass, 0)

    def add_rad(part_of):
        for side in range(2):
            @pl.when(has[1 - side])
            def _():
                rad_copy(side, part_of).wait_recv()
                for pos in range(rad_parts[part_of][0], sum(rad_parts[part_of])):
                    for k in range(3):
                        r = k if side == 0 else CR - 3 + k
                        out[ORDER[pos], r] = out[ORDER[pos], r] + rad_recv[side, pos, k]

    add_rad(0)
    vol_copy.wait()
    seg = table[C_SEG : C_SEG + CZ]
    mask = table[C_MASK : C_MASK + CL].astype(F32)

    def early(b, _):
        for i in range(2):
            lon_copy(0, 0, 2 * b + i).wait_recv()
            lon_copy(1, 0, 2 * b + i).wait_recv()
        highs, lows = [], []
        for h in range(4):
            g = b * 4 + h
            got = jnp.concatenate(
                [recv0[0, g], recv0[1, g], jnp.zeros((16, CZ), F32)], axis=0
            )
            add = jnp.dot(
                table[C_FIX07 : C_FIX07 + 128],
                jnp.concatenate(split(got), axis=0),
                preferred_element_type=F32,
            )
            v = vol[pl.ds(4 * g, 4)].reshape(64, CZ)
            for c, f in enumerate((0, 7)):
                new = out[f, pl.ds(4 * g, 4)].reshape(64, CZ) + add[c * 64 : (c + 1) * 64]
                out[f, pl.ds(4 * g, 4)] = new.reshape(4, CL, CZ)
                yh, yl = split(v * new)
                highs.append(yh)
                lows.append(yl)
        t = jnp.dot(jnp.concatenate(highs + lows, axis=0), seg, preferred_element_type=F32)
        t = t[0:512] + t[512:1024]
        for h in range(4):
            for c in range(2):
                at = (h * 2 + c) * 64
                x = t[at : at + 64].reshape(4, CL, TP) * mask[None]
                pay[pl.ds(b * 128 + h * 32, 32), c * TP : (c + 1) * TP] = (
                    x[:, 0:8] + x[:, 8:16]
                ).reshape(32, TP)
        return 0

    lax.fori_loop(0, NB // 2, early, 0)

    pay_hi, pay_lo = split(pay[...])
    buf[...] = (
        jnp.dot(hit_db[...], pay_hi, preferred_element_type=F32)
        + jnp.dot(hit_db[...], pay_lo, preferred_element_type=F32)
    ).reshape(NYX, NZC, 2 * TP)

    def ra_copy(k):
        a, device = yx_peer(k)
        return pltpu.make_async_remote_copy(
            src_ref=buf.at[a], dst_ref=ra.at[k], send_sem=ra_s.at[k], recv_sem=ra_r.at[k],
            device_id=device, device_id_type=MESH,
        )

    def swap_copy():
        return pltpu.make_async_remote_copy(
            src_ref=part, dst_ref=other, send_sem=swap_s, recv_sem=swap_r,
            device_id=(rad, lon + 1 - 2 * core_at), device_id_type=MESH,
        )

    def z_copy(n, core):
        return pltpu.make_async_remote_copy(
            src_ref=both, dst_ref=rb.at[z_at], send_sem=rb_s.at[n, core], recv_sem=rb_r.at[n],
            device_id=(rad, x_at * NZC + lax.rem(z_at + n, 4) * 2 + core), device_id_type=MESH,
        )

    def each_z(act):
        for sender in range(2):
            @pl.when(core_at == sender)
            def _():
                for n in (2, 1, 3):
                    if sender == {1: 0, 2: TWO, 3: 1}[n]:
                        for core in range(2):
                            act(z_copy(n, core))

    def g2_copy(k):
        a, device = yx_peer(k)
        return pltpu.make_async_remote_copy(
            src_ref=g0, dst_ref=g2.at[me_yx], send_sem=g2_s.at[k], recv_sem=g2_r.at[k],
            device_id=device, device_id_type=MESH,
        )

    def late(b, _):
        lon_copy(0, 1, b).wait_recv()
        lon_copy(1, 1, b).wait_recv()

        def late_row(i, _):
            r = b * RB + i
            got = jnp.concatenate(
                [recv0[0, r], recv1[0, r], recv0[1, r], recv1[1, r], jnp.zeros((16, CZ), F32)],
                axis=0,
            )
            hi, lo = split(got)
            add = jnp.dot(
                table[C_FIX : C_FIX + 96],
                jnp.concatenate([hi, lo], axis=0),
                preferred_element_type=F32,
            )
            out[1:7, r] = out[1:7, r] + add.reshape(6, CL, CZ)
            return 0

        lax.fori_loop(0, RB, late_row, 0, unroll=8)
        return 0

    def late(b, _):
        lon_copy(0, 1, b).wait_recv()
        lon_copy(1, 1, b).wait_recv()
        for h in range(RB // 4):
            g = b * (RB // 4) + h
            tail = [recv1[0, g, 64:72], recv1[1, g, 64:72], jnp.zeros((16, CZ), F32)]
            for i in range(4):
                got = jnp.concatenate(
                    [recv1[side, g, i * 16 : (i + 1) * 16] for side in range(2)] + tail, axis=0
                )
                add = jnp.dot(
                    table[C_FIX + i * 96 : C_FIX + (i + 1) * 96],
                    jnp.concatenate(split(got), axis=0),
                    preferred_element_type=F32,
                )
                r = 4 * g + i
                out[1:7, r] = out[1:7, r] + add.reshape(6, CL, CZ)
        return 0

    pl.semaphore_wait(lines, 4)
    for k in yx_order:
        ra_copy(k).start()
    lax.fori_loop(SENDS[1], SENDS[2], send_late, 0)
    send_rad(2)

    lax.fori_loop(0, PASS[0], second_pass, 0)
    cols[...] = jnp.zeros((8, 256), F32)
    cols[0:2, 0:CH] = inj[...]
    cols[2:3, 0:CH] = cou[...]
    cols[3:4, 0:CH] = wei[...]
    columns = cols[...].T
    channel_rate = jnp.broadcast_to(columns[0:CH, 2:3], (CH, TP))
    channel_weight = jnp.broadcast_to(columns[0:CH, 3:4], (CH, TP))

    def drift(density):
        for _ in range(DRIFT):
            density = density - channel_rate * (density - pltpu.roll(density, 1, axis=1))
        return density

    dens_copy.wait()
    bare = jnp.sum(channel_weight * drift(dens[...]), axis=0, keepdims=True)

    rate_row, weight_row = cols[2:3], cols[3:4]
    keep = 1.0 - rate_row
    powers = (
        keep * keep * keep,
        3.0 * keep * keep * rate_row,
        3.0 * keep * rate_row * rate_row,
        rate_row * rate_row * rate_row,
    )
    taps = [
        [
            jnp.sum(0.5 * weight_row * cols[i : i + 1] * power, axis=1, keepdims=True)
            for power in powers
        ]
        for i in range(2)
    ]

    total = buf[me_yx]
    for k in range(1, NYX):
        ra_copy(k).wait_recv()
        total = total + ra[k]
    part[:, 0 : 2 * TP] = total
    part[:, 2 * TP :] = jnp.broadcast_to(bare, (NZC, TP))
    swap_copy().start()
    swap_copy().wait_recv()
    both[:, 0 : 2 * TP] = part[:, 0 : 2 * TP] + other[:, 0 : 2 * TP]
    first = core_at == 0
    both[:, 2 * TP : 3 * TP] = jnp.where(first, part[:, 2 * TP :], other[:, 2 * TP :])
    both[:, 3 * TP :] = jnp.where(first, other[:, 2 * TP :], part[:, 2 * TP :])
    each_z(lambda copy: copy.start())
    lax.fori_loop(SENDS[2], SENDS[3], send_late, 0)
    lax.fori_loop(PASS[0], CR // 4, second_pass, 0)
    add_rad(1)
    lax.fori_loop(0, LATE[0], late, 0)
    rb[z_at] = both[...]
    for n in (1, 2, 3):
        z_copy(n, 0).wait_recv()
    source = rb[0, :, 0 : 2 * TP]
    for j in range(1, 4):
        source = source + rb[j, :, 0 : 2 * TP]
    tile_row = lax.broadcasted_iota(jnp.int32, (NZC, TP), 0)
    pressure = jnp.zeros((NZC, TP), F32)
    for j in range(NZC):
        at = (2 + j % 2) * TP
        pressure = jnp.where(tile_row == j, rb[j // 2, :, at : at + TP], pressure)
    for i in range(2):
        s = source[:, i * TP : (i + 1) * TP]
        for n in range(4):
            pressure = pressure + taps[i][n] * (pltpu.roll(s, n, axis=1) if n else s)
    g0[...] = pressure
    for k in yx_order:
        g2_copy(k).start()
    lax.fori_loop(SENDS[3], SENDS[4], send_late, 0)
    g2[me_yx] = pressure

    own = lax.broadcasted_iota(jnp.int32, (NZC, 2 * TP), 0) == me_zc
    mine = jnp.sum(jnp.where(own, source, 0.0), axis=0, keepdims=True)
    drifted[...] = drift(
        dens[...]
        + 0.5 * (columns[0:CH, 0:1] * mine[:, 0:TP] + columns[0:CH, 1:2] * mine[:, TP:])
    )
    add_rad(2)
    lax.fori_loop(LATE[0], LATE[1], late, 0)

    def sent(b, _):
        for side in range(2):
            for part in range(2):
                lon_copy(side, part, b).wait_send()
        return 0

    lax.fori_loop(0, NB, sent, 0)
    for side in range(2):
        @pl.when(has[side])
        def _():
            for part_of in range(3):
                rad_copy(side, part_of).wait_send()
    for k in range(1, NYX):
        ra_copy(k).wait_send()
    swap_copy().wait_send()
    each_z(lambda copy: copy.wait_send())

    for k in range(1, NYX):
        g2_copy(k).wait_recv()
    back_hi, back_lo = split(g2[...].reshape(DEVICES, TP))
    pay[0:CR, 0:TP] = jnp.dot(hit_bd[...], back_hi, preferred_element_type=F32) + jnp.dot(
        hit_bd[...], back_lo, preferred_element_type=F32
    )

    def nudge(b, _):
        got = pay[pl.ds(b * 16, 16), 0:TP]
        wide = jnp.broadcast_to(got[:, None, :], (16, CL, TP)) * mask[None]
        back = jnp.dot(
            jnp.concatenate(split(wide.reshape(16 * CL, TP)), axis=1),
            seg_t[...],
            preferred_element_type=F32,
        )
        old = out[7, pl.ds(b * 16, 16)].reshape(16 * CL, CZ)
        out[7, pl.ds(b * 16, 16)] = (old + 0.5 * (back - old)).reshape(16, CL, CZ)
        return 0

    lax.fori_loop(0, CR // 16, nudge, 0, unroll=4)

    for k in range(1, NYX):
        g2_copy(k).wait_send()


def finish(fields, density, fields_out, density_out, sem):
    copies = [
        pltpu.make_async_copy(fields.at[f], fields_out.at[f], sem.at[f]) for f in range(NF)
    ] + [pltpu.make_async_copy(density, density_out, sem.at[NF])]
    for copy in copies:
        copy.start()
    for copy in copies:
        copy.wait()


def per_device(
    state, flux_matrices, wave_speed, flux_volume, block_tile, tile_of_device,
    phase_density, injection, drift_courant, energy_weight,
):
    hbm = pl.BlockSpec(memory_space=pltpu.HBM)
    vmem = pl.BlockSpec(memory_space=pltpu.VMEM)
    dma = pltpu.SemaphoreType.DMA
    coupled, drifted = pl.pallas_call(
        kernel,
        out_shape=(
            pltpu.VMEM((NF, CR, CL, CZ), F32),
            pltpu.VMEM((CH, TP), F32),
        ),
        in_specs=[hbm] * 11,
        out_specs=(vmem, vmem),
        scratch_shapes=[
            pltpu.SMEM((2, NF, NF), F32),
            pltpu.SMEM((2,), F32),
            pltpu.VMEM((1, CR), jnp.int32),
            pltpu.VMEM((1, DEVICES), jnp.int32),
            pltpu.VMEM((C_END, 128), BF16),
            pltpu.VMEM((2, CH), F32),
            pltpu.VMEM((1, CH), F32),
            pltpu.VMEM((1, CH), F32),
            pltpu.VMEM((NF, CR + 6, CL, CZ), F32),
            pltpu.VMEM((CR, CL, CZ), F32),
            pltpu.VMEM((CH, TP), F32),
            pltpu.VMEM((M_END, 256), BF16),
            pltpu.VMEM((CR, 256, CZ), BF16),
            pltpu.VMEM((CR, 256, CZ), BF16),
            pltpu.VMEM((2, CR // 4, 24, CZ), F32),
            pltpu.VMEM((2, CR // 4, 72, CZ), F32),
            pltpu.VMEM((2, CR // 4, 24, CZ), F32),
            pltpu.VMEM((2, CR // 4, 72, CZ), F32),
            pltpu.VMEM((2, NF, 3, CL, CZ), F32),
            pltpu.VMEM((2, NF, 3, CL, CZ), F32),
            pltpu.VMEM((8, 256), F32),
            pltpu.VMEM((CR * 8, 2 * TP), F32),
            pltpu.VMEM((DEVICES, CR * 8), BF16),
            pltpu.VMEM((CR, DEVICES), BF16),
            pltpu.VMEM((2 * TP, CZ), BF16),
            pltpu.VMEM((NYX, NZC, 2 * TP), F32),
            pltpu.VMEM((NYX, NZC, 2 * TP), F32),
            pltpu.VMEM((NZC, 3 * TP), F32),
            pltpu.VMEM((NZC, 3 * TP), F32),
            pltpu.VMEM((NZC, 4 * TP), F32),
            pltpu.VMEM((4, NZC, 4 * TP), F32),
            pltpu.VMEM((NZC, TP), F32),
            pltpu.VMEM((NYX, NZC, TP), F32),
            pltpu.SemaphoreType.REGULAR, dma((8,)), dma((NB,)), dma, dma,
            dma((2, NB)), dma((2, NB)), dma((2, NB)), dma((2, NB)),
            dma((2, 3)), dma((2, 3)), dma((NYX,)), dma((NYX,)),
            dma, dma, dma((4, 2)), dma((4,)), dma((NYX,)), dma((NYX,)),
        ],
        compiler_params=pltpu.CompilerParams(
            collective_id=0, has_side_effects=True, vmem_limit_bytes=54 << 20
        ),
    )(
        state,
        flux_volume,
        phase_density.reshape(CH, TP),
        flux_matrices,
        wave_speed,
        block_tile.reshape(1, CR),
        tile_of_device.reshape(1, DEVICES),
        injection,
        drift_courant.reshape(1, CH),
        energy_weight.reshape(1, CH),
        jnp.asarray(constants()),
    )
    coupled, drifted = pl.pallas_call(
        finish,
        out_shape=(
            jax.ShapeDtypeStruct((NF, CR, CL, CZ), F32),
            jax.ShapeDtypeStruct((CH, TP), F32),
        ),
        in_specs=[vmem, vmem],
        out_specs=(hbm, hbm),
        scratch_shapes=[dma((NF + 1,))],
        compiler_params=pltpu.CompilerParams(vmem_limit_bytes=1 << 20),
    )(coupled, drifted)
    return coupled, drifted[None]


def solution(mesh):
    in_specs = (
        P(None, "rad", "lon", None),
        P(),
        P(),
        P("rad", "lon", None),
        P("lon", "rad", None),
        P(),
        P(("rad", "lon"), None, None),
        P(),
        P(),
        P(),
    )
    out_specs = (P(None, "rad", "lon", None), P(("rad", "lon"), None, None))
    return jax.shard_map(
        per_device, mesh=mesh, in_specs=in_specs, out_specs=out_specs, check_vma=False
    )
```
